32 devices in a mesh: context: 8 (over y, x, core), expert: 4 (over z).
Axes of the slice: x: 2, y: 2, z: 4, core: 2. Of those that a mesh axis runs over, the one named last changes fastest.
Arguments:
- tokens: bfloat16 [4, 1024, 2048], P('expert', 'context'), may hold values from -6 to 6
- norm1_gain: bfloat16 [2048], P(('context', 'expert')), may hold values from 0.5 to 1.5
- w_query: bfloat16 [2048, 3072], P(('context', 'expert')), may hold values from -0.125 to 0.125
- w_down_kv: bfloat16 [2048, 576], P(('context', 'expert')), may hold values from -0.125 to 0.125
- kv_gain: bfloat16 [512], P(('context', 'expert')), may hold values from 0.5 to 1.5
- w_up_kv: bfloat16 [512, 4096], P(None, ('context', 'expert')), may hold values from -0.25 to 0.25
- w_attn_out: bfloat16 [2048, 2048], P(None, ('context', 'expert')), may hold values from -1.5 to 1.5
- norm2_gain: bfloat16 [2048], P(('context', 'expert')), may hold values from 0.5 to 1.5
- w_router: bfloat16 [2048, 16], P(('context', 'expert')), may hold values from -0.0625 to 0.0625
- w_shared_in: bfloat16 [2048, 5632], P(('context', 'expert')), may hold values from -0.125 to 0.125
- w_shared_out: bfloat16 [2816, 2048], P(None, ('context', 'expert')), may hold values from -0.109375 to 0.109375
- w_expert_in: bfloat16 [32, 2048, 1408], P(('context', 'expert')), may hold values from -0.125 to 0.125
- w_expert_out: bfloat16 [32, 704, 2048], P(('context', 'expert')), may hold values from -0.3125 to 0.3125
- routes: int32 [4, 1024, 6], P('expert', 'context'), may hold values from 0 to 15, as said below
- slots: int32 [4, 1024, 6], P('expert', 'context'), may hold values from 0 to 63, as said below
- blocks: int32 [4, 1024], P('expert', 'context'), may hold values from 0 to 7, never falling along the last dimension, each value on 1 to 256 neighbouring positions
- cotangent: bfloat16 [4, 1024, 2048], P('expert', 'context'), may hold values from -6 to 6
Outputs:
- output: bfloat16 [4, 1024, 2048], P('expert', 'context')
- grad_tokens: float32 [4, 1024, 2048], P('expert', 'context')
- grad_norm1_gain: float32 [2048], P(('context', 'expert'))
- grad_w_query: float32 [2048, 3072], P(('context', 'expert'))
- grad_w_down_kv: float32 [2048, 576], P(('context', 'expert'))
- grad_kv_gain: float32 [512], P(('context', 'expert'))
- grad_w_up_kv: float32 [512, 4096], P(None, ('context', 'expert'))
- grad_w_attn_out: float32 [2048, 2048], P(None, ('context', 'expert'))
- grad_norm2_gain: float32 [2048], P(('context', 'expert'))
- grad_w_router: float32 [2048, 16], P(('context', 'expert'))
- grad_w_shared_in: float32 [2048, 5632], P(('context', 'expert'))
- grad_w_shared_out: float32 [2816, 2048], P(None, ('context', 'expert'))
- grad_w_expert_in: float32 [32, 2048, 1408], P(('context', 'expert'))
- grad_w_expert_out: float32 [32, 704, 2048], P(('context', 'expert'))
The draws below stay inside these ranges and needn't reach their ends.
Inputs may be any that keep to these rules, and one draw needn't show every extreme that they name: `routes`: each token names 6 different experts. Among the tokens of one device (aligned blocks of 128 tokens) no expert is named by more than 64 of them, and some expert by exactly 64. Within one device, the rows that name the same expert have distinct slots. `blocks`: along a sequence the block ids never fall; a block holds 1 to 256 consecutive tokens, and some block exactly 256.
All inputs are finite; a program needn't handle non-finite values.
Results may differ from the reference program's by a relative error of at most 0.019.
Values may be sent and summed in bfloat16 or wider, within the bound.
A program may use at most 512 MiB of HBM per device.

```python
import math
import jax
import jax.numpy as jnp
import numpy as np
from jax import lax

D = 2048
HEADS = 16
QKD = 128
RD = 64
VD = 128
LAT = 512
FFE = 1408
TOP = 6
TOK_DEV = 128
BLOCK = 256
SHARED = 2816
HALF = 704
LENGTH = 1024
NSEQ = 4
EXPERTS = 16
CAP = 64


def plan_routes(key):
    blocks_count = NSEQ * LENGTH // TOK_DEV
    mean_load = TOK_DEV * TOP // EXPERTS
    pair_count = EXPERTS // 2
    favored_key, block_key = jax.random.split(key)
    favored = jax.random.randint(favored_key, (), 0, EXPERTS).astype(jnp.int32)
    positions = jnp.arange(TOK_DEV * TOP, dtype=jnp.int32).reshape(TOP, TOK_DEV).T

    def one_block(block_seed):
        ranking_key, surplus_key = jax.random.split(block_seed)
        ranking = jax.random.permutation(ranking_key, EXPERTS).astype(jnp.int32)
        favored_place = jnp.argmax((ranking == favored).astype(jnp.int32))
        ranking = ranking.at[favored_place].set(ranking[0]).at[0].set(favored)
        surplus = jax.random.randint(surplus_key, (pair_count,), 0, CAP - mean_load + 1).astype(jnp.int32)
        surplus = surplus.at[0].set(CAP - mean_load)
        counts = jnp.concatenate([mean_load + surplus, mean_load - surplus])
        run_ends = jnp.cumsum(counts).astype(jnp.int32)
        run_starts = run_ends - counts
        run_index = jnp.sum((positions[:, :, None] >= run_ends[None, None, :]).astype(jnp.int32), axis=-1)
        return (ranking[run_index], positions - run_starts[run_index])
    experts_drawn, slots_drawn = jax.vmap(one_block)(jax.random.split(block_key, blocks_count))
    return (experts_drawn.reshape(NSEQ, LENGTH, TOP).astype(jnp.int32), slots_drawn.reshape(NSEQ, LENGTH, TOP).astype(jnp.int32))


def draw_routes(key, part):
    return plan_routes(jax.random.fold_in(key, 5))[0]


def draw_slots(key, part):
    return plan_routes(jax.random.fold_in(key, 5))[1]


def shard_levels(own_key, shape, shards, low, largest):
    def one(axis_at, shards_of):
        heights = jax.random.uniform(jax.random.fold_in(jax.random.fold_in(own_key, 6), axis_at), (shards_of,), jnp.float32, low / len(shards), largest / len(shards))
        return jnp.repeat(jnp.exp(heights), shape[axis_at] // shards_of).reshape((-1,) + (1,) * (len(shape) - axis_at - 1))

    gain = one(*shards[0])
    for cut in shards[1:]:
        gain = gain * one(*cut)
    return gain


def profile(count, total, limit, slope):
    weights = [(1 << 20) // math.isqrt(rank ** slope) + 1 for rank in range(2, count + 1)]
    spare, given = total - limit - (count - 1), [1] * (count - 1)
    while spare > 0:
        movable = [i for i in range(count - 1) if given[i] < limit]
        pool, budget = sum([weights[i] for i in movable]), spare
        for i in movable:
            extra = min(limit - given[i], max(1, budget * weights[i] // pool), spare)
            given[i] = given[i] + extra
            spare = spare - extra
    return np.array([limit] + given)


def ragged_sizes(own_key, number_of, total, most, lean):
    if number_of == 2:
        one = jax.random.randint(own_key, (), max(1, total - most), min(most, total - 1) + 1)
        return jnp.stack([one, total - one])
    tallies = jnp.asarray(profile(number_of, total, most, lean), jnp.int32)
    pairs = (number_of - 1) // 2
    donor, sink = tallies[1:1 + 2 * pairs:2], tallies[2:2 + 2 * pairs:2]
    slack = jnp.minimum(donor - 1, most - sink)
    shifted = jax.random.randint(jax.random.fold_in(own_key, 1), (pairs,), 0, 1 << 20) % (slack + 1)
    tallies = tallies.at[1:1 + 2 * pairs:2].set(donor - shifted).at[2:2 + 2 * pairs:2].set(sink + shifted)
    return tallies[jax.random.permutation(jax.random.fold_in(own_key, 2), number_of)]


def noise(key, shape, deviation, limit, pieces=(), held_as=jnp.bfloat16):
    array = jax.random.normal(key, shape, jnp.float32) * deviation
    if len(pieces) > 0:
        array = shard_levels(key, shape, pieces, -0.22, 0.18) * array
    return jnp.clip(array, min=-limit, max=limit).astype(held_as)


def setup_inputs(seed: int = 0) -> dict:
    seeds = jax.random.split(jax.random.key(seed), 18)
    tokens = noise(seeds[0], (NSEQ, LENGTH, D), 1.0, 6.0, ((0, 4), (1, 8)))
    norm1_gain = jnp.clip(1.0 + 0.1 * jax.random.normal(seeds[1], (D,), jnp.float32), 0.5, 1.5).astype(jnp.bfloat16)
    w_query = noise(seeds[2], (D, HEADS * (QKD + RD)), D ** -0.5, 0.125, ((0, 32),))
    w_down_kv = noise(seeds[3], (D, LAT + RD), D ** -0.5, 0.125, ((0, 32),))
    kv_gain = jnp.clip(1.0 + 0.1 * jax.random.normal(seeds[4], (LAT,), jnp.float32), 0.5, 1.5).astype(jnp.bfloat16)
    w_up_kv = noise(seeds[5], (LAT, HEADS * (QKD + VD)), LAT ** -0.5, 0.25, ((1, 32),))
    w_attn_out = noise(seeds[6], (HEADS * VD, D), (max(1, HEADS * VD * 8 // LENGTH)) ** -0.5, 1.5, ((1, 32),))
    norm2_gain = jnp.clip(1.0 + 0.1 * jax.random.normal(seeds[7], (D,), jnp.float32), 0.5, 1.5).astype(jnp.bfloat16)
    w_router = noise(seeds[8], (D, EXPERTS), (4 * D) ** -0.5, 0.0625, ((0, 32),))
    w_shared_in = noise(seeds[9], (D, 2 * SHARED), D ** -0.5, 0.125, ((0, 32),))
    w_shared_out = noise(seeds[10], (SHARED, D), SHARED ** -0.5, 0.109375, ((1, 32),))
    w_expert_in = noise(seeds[11], (2 * EXPERTS, D, FFE), D ** -0.5, 0.125, ((0, 32),))
    w_expert_out = noise(seeds[12], (2 * EXPERTS, HALF, D), (FFE // 4) ** -0.5, 0.3125, ((0, 32),))
    routes = draw_routes(jax.random.fold_in(seeds[17], 71), 0)
    slots = draw_slots(jax.random.fold_in(seeds[17], 71), 0)
    blocks = jax.vmap(lambda own: jnp.searchsorted(jnp.cumsum(ragged_sizes(own, 2 * LENGTH // BLOCK, LENGTH, BLOCK, 1)), jnp.arange(LENGTH), side="right"))(jax.random.split(seeds[15], NSEQ)).reshape((NSEQ, LENGTH)).astype(jnp.int32)
    cotangent = noise(seeds[16], (NSEQ, LENGTH, D), 1.0, 6.0, ((0, 4), (1, 8)))
    return dict(tokens=tokens, norm1_gain=norm1_gain, w_query=w_query, w_down_kv=w_down_kv, kv_gain=kv_gain, w_up_kv=w_up_kv, w_attn_out=w_attn_out, norm2_gain=norm2_gain, w_router=w_router, w_shared_in=w_shared_in, w_shared_out=w_shared_out, w_expert_in=w_expert_in, w_expert_out=w_expert_out, routes=routes, slots=slots, blocks=blocks, cotangent=cotangent)


@jax.custom_vjp
def low(v):
    return lax.optimization_barrier(v.astype(jnp.bfloat16)).astype(jnp.float32)

@jax.custom_vjp
def low_back(v):
    return v

def low_keep(v):
    return (low(v), None)

def low_pass(kept, grad):
    return (grad,)

def back_keep(v):
    return (v, None)

def back_low(kept, grad):
    return (low(grad),)
low.defvjp(low_keep, low_pass)
low_back.defvjp(back_keep, back_low)
highest = lax.Precision.HIGHEST
epsilon = 1e-06

def product(left, right):
    return jnp.dot(left, right, precision=highest, preferred_element_type=jnp.float32)

def normalize(values):
    return values * lax.rsqrt(lax.optimization_barrier(jnp.mean(values * values, axis=-1, keepdims=True)) + epsilon)

def rotary(values, cosine, sine_table):
    middle = values.shape[-1] // 2
    first_half = values[..., :middle]
    second_half = values[..., middle:]
    return jnp.concatenate([first_half * cosine - second_half * sine_table, second_half * cosine + first_half * sine_table], axis=-1)

def rotation_table(positions):
    exponent = jnp.arange(RD // 2, dtype=jnp.float32) * (2.0 / RD)
    angle_table = positions[:, None] * (10000.0 ** (-exponent))[None, :]
    return (jnp.cos(angle_table), jnp.sin(angle_table))

def forward(tokens, norm1_gain, w_query, w_down_kv, kv_gain, w_up_kv, w_attn_out, norm2_gain, w_router, w_shared_in, w_shared_out, w_expert_in, w_expert_out, routes, slots, blocks):
    score_scale = (QKD + RD) ** (-0.5)
    cosine, sine_table = rotation_table(jnp.arange(LENGTH, dtype=jnp.float32))

    def attend(state_in, inputs):
        sequence, seq_blocks = inputs
        hidden_first = low(normalize(sequence) * norm1_gain)
        query_pre = low_back(product(hidden_first, w_query)).reshape(LENGTH, HEADS, QKD + RD)
        query_rot = low(jnp.concatenate([query_pre[..., :QKD], rotary(query_pre[..., QKD:], cosine[:, None, :], sine_table[:, None, :])], axis=-1))
        compressed = low_back(product(hidden_first, w_down_kv))
        latent = low(normalize(compressed[:, :LAT]) * kv_gain)
        rope_key = low(rotary(compressed[:, LAT:], cosine, sine_table))
        key_value = low(product(latent, w_up_kv)).reshape(LENGTH, HEADS, QKD + VD)
        raw_scores = jnp.einsum('qhd,khd->hqk', query_rot[..., :QKD], key_value[..., :QKD], precision=highest) + jnp.einsum('qhr,kr->hqk', query_rot[..., QKD:], rope_key, precision=highest)
        scores = low_back(raw_scores) * score_scale
        shift_table = jnp.floor(jnp.diagonal(scores, axis1=1, axis2=2))
        allowed = (seq_blocks[None, :] <= seq_blocks[:, None])[None]
        weights = jnp.where(allowed, jnp.exp(jnp.where(allowed, scores - shift_table[:, :, None], 0.0)), 0.0)
        denominator = lax.optimization_barrier(jnp.sum(weights, axis=-1))
        summed = low_back(jnp.einsum('hqk,khv->qhv', low(weights), key_value[..., QKD:], precision=highest))
        mixed_low = low((summed / jnp.transpose(denominator)[:, :, None]).reshape(LENGTH, HEADS * VD))
        return (state_in, sequence + low_back(product(mixed_low, w_attn_out)))
    unused_state, resid = lax.scan(jax.checkpoint(attend), jnp.zeros((), jnp.float32), (tokens, blocks))
    token_count = NSEQ * LENGTH
    flat_resid = resid.reshape(token_count, D)
    hidden_second = low(normalize(flat_resid) * norm2_gain)
    logits = low_back(product(hidden_second, w_router))
    route_flat = routes.reshape(token_count, TOP)
    chosen = jnp.take_along_axis(logits, route_flat, axis=1)
    gate_weights = jax.nn.softmax(chosen, axis=-1)
    shared_pre = low_back(product(hidden_second, w_shared_in))
    shared_act = low(jax.nn.silu(shared_pre[:, :SHARED]) * shared_pre[:, SHARED:])
    shared_result = low_back(product(shared_act, w_shared_out))
    block_count = token_count // TOK_DEV
    rows_expert = block_count * CAP
    owner_block = jnp.arange(token_count, dtype=jnp.int32) // TOK_DEV
    target = route_flat * rows_expert + owner_block[:, None] * CAP + slots.reshape(token_count, TOP)
    token_index = jnp.repeat(jnp.arange(token_count, dtype=jnp.int32), TOP)
    source_table = jnp.full((EXPERTS * rows_expert,), -1, jnp.int32).at[target.reshape(-1)].set(token_index)

    def expert_rows(inputs):
        sources, weights_in, weights_out = inputs
        row_block = jnp.where((sources >= 0)[:, None], hidden_second[jnp.maximum(sources, 0)], 0.0)
        combined = jnp.zeros((rows_expert, D), jnp.float32)
        for half_index in range(2):
            pre_act = low_back(product(row_block, weights_in[half_index]))
            activation = low(jax.nn.silu(pre_act[:, :HALF]) * pre_act[:, HALF:])
            combined = combined + low(low_back(product(activation, weights_out[half_index])))
        return combined
    expert_table = lax.map(jax.checkpoint(expert_rows), (source_table.reshape(EXPERTS, rows_expert), w_expert_in.reshape(EXPERTS, 2, D, FFE), w_expert_out.reshape(EXPERTS, 2, HALF, D)))
    picked = expert_table.reshape(EXPERTS * rows_expert, D)[target]
    routed = lax.optimization_barrier(jnp.sum(gate_weights[:, :, None] * picked, axis=1))
    output = flat_resid + shared_result + routed
    return output.reshape(NSEQ, LENGTH, D)

def reference(tokens, norm1_gain, w_query, w_down_kv, kv_gain, w_up_kv, w_attn_out, norm2_gain, w_router, w_shared_in, w_shared_out, w_expert_in, w_expert_out, routes, slots, blocks, cotangent):
    primals = tuple((argument_array.astype(jnp.float32) for argument_array in (tokens, norm1_gain, w_query, w_down_kv, kv_gain, w_up_kv, w_attn_out, norm2_gain, w_router, w_shared_in, w_shared_out, w_expert_in, w_expert_out)))

    def forward_floats(*values_all):
        return forward(*values_all, routes, slots, blocks)
    result, pullback = jax.vjp(forward_floats, *primals)
    gradients = pullback(cotangent.astype(jnp.float32))
    return (result.astype(jnp.bfloat16), gradients[0], gradients[1], gradients[2], gradients[3], gradients[4], gradients[5], gradients[6], gradients[7], gradients[8], gradients[9], gradients[10], gradients[11], gradients[12])
```

```python
import functools
import math

import jax
import jax.numpy as jnp
from jax import lax
from jax.sharding import PartitionSpec as P

HEADS = 16
QKD = 128
RD = 64
VD = 128
LAT = 512
TOP = 6
SHARED = 2816
HALF = 704


epsilon = 1e-06
highest = lax.Precision.HIGHEST


def normalize(values):
    scaling = lax.rsqrt(jnp.mean(values * values, axis=-1, keepdims=True) + epsilon)
    return (values * scaling, scaling)


def norm_back(grad_normed, normed, scaling, gain):
    grad_gain = jnp.sum(grad_normed * normed, axis=0)
    grad_unit = grad_normed * gain
    grad_values = scaling * (
        grad_unit - normed * jnp.mean(grad_unit * normed, axis=-1, keepdims=True)
    )
    return (grad_values, grad_gain)


def rotary(values, cosine, sine_table):
    middle = values.shape[-1] // 2
    first_half = values[..., :middle]
    second_half = values[..., middle:]
    return jnp.concatenate(
        [
            first_half * cosine - second_half * sine_table,
            second_half * cosine + first_half * sine_table,
        ],
        axis=-1,
    )


def rotary_back(grads_in, cosine, sine_table):
    middle = grads_in.shape[-1] // 2
    first_half = grads_in[..., :middle]
    second_half = grads_in[..., middle:]
    return jnp.concatenate(
        [
            first_half * cosine + second_half * sine_table,
            second_half * cosine - first_half * sine_table,
        ],
        axis=-1,
    )


def rotation_table(positions):
    exponent = jnp.arange(RD // 2, dtype=jnp.float32) * (2.0 / RD)
    angle_table = positions[:, None] * (10000.0 ** (-exponent))[None, :]
    return (jnp.cos(angle_table), jnp.sin(angle_table))


def silu_back(value, grads_in):
    sigma_value = jax.nn.sigmoid(value)
    return grads_in * sigma_value * (1.0 + value * (1.0 - sigma_value))


def head_scores(query_low, key_low, rope_low):
    nope_part = jnp.einsum(
        "thd,nhd->htn", query_low[..., :QKD], key_low, preferred_element_type=jnp.float32
    )
    rope_part = jnp.einsum(
        "thr,nr->htn", query_low[..., QKD:], rope_low, preferred_element_type=jnp.float32
    )
    return nope_part + rope_part


def both_halves(buffer_rows, experts_total, capacity):
    width = buffer_rows.shape[-1]
    shaped = buffer_rows.reshape(experts_total, 1, capacity, width)
    return jnp.broadcast_to(shaped, (experts_total, 2, capacity, width)).reshape(
        2 * experts_total, capacity, width
    )


def halves_sum(received, experts_total, capacity):
    width = received.shape[-1]
    return (
        received.astype(jnp.float32)
        .reshape(experts_total, 2, capacity, width)
        .sum(axis=1)
        .reshape(experts_total * capacity, width)
    )


def body(
    tokens,
    norm1_gain,
    w_query,
    w_down_kv,
    kv_gain,
    w_up_kv,
    w_attn_out,
    norm2_gain,
    w_router,
    w_shared_in,
    w_shared_out,
    w_expert_in,
    w_expert_out,
    routes,
    slots,
    blocks,
    cotangent,
):
    (
        gain_first,
        query_weight,
        down_weight,
        latent_gain,
        up_weight,
        out_weight,
        gain_second,
        router_weight,
        shared_in_weight,
        shared_out_weight,
    ) = (
        lax.all_gather(norm1_gain, ("context", "expert"), axis=0, tiled=True),
        lax.all_gather(w_query, ("context", "expert"), axis=0, tiled=True),
        lax.all_gather(w_down_kv, ("context", "expert"), axis=0, tiled=True),
        lax.all_gather(kv_gain, ("context", "expert"), axis=0, tiled=True),
        lax.all_gather(w_up_kv, ("context", "expert"), axis=1, tiled=True),
        lax.all_gather(w_attn_out, ("context", "expert"), axis=1, tiled=True),
        lax.all_gather(norm2_gain, ("context", "expert"), axis=0, tiled=True),
        lax.all_gather(w_router, ("context", "expert"), axis=0, tiled=True),
        lax.all_gather(w_shared_in, ("context", "expert"), axis=0, tiled=True),
        lax.all_gather(w_shared_out, ("context", "expert"), axis=1, tiled=True),
    )
    tok_count = tokens.shape[1]
    length_all = tok_count * lax.axis_size("context")
    experts_total = router_weight.shape[1]
    capacity = tok_count * TOP // experts_total * 4 // 3
    score_scale = (QKD + RD) ** (-0.5)
    residual_in = tokens[0].astype(jnp.float32)
    own_blocks = blocks[0]
    route_ids = routes[0]
    slot_ids = slots[0]
    positions = (lax.axis_index("context") * tok_count + jnp.arange(tok_count)).astype(jnp.float32)
    cosine, sine_table = rotation_table(positions)
    head_cos = cosine[:, None, :]
    head_sin = sine_table[:, None, :]
    gain_one = gain_first.astype(jnp.float32)
    gain_two = gain_second.astype(jnp.float32)
    gain_latent = latent_gain.astype(jnp.float32)
    normed_first, scaling_first = normalize(residual_in)
    hidden_first = (normed_first * gain_one).astype(jnp.bfloat16)
    query_pre = jnp.dot(hidden_first, query_weight, preferred_element_type=jnp.float32).reshape(
        tok_count, HEADS, QKD + RD
    )
    query_low = jnp.concatenate(
        [query_pre[..., :QKD], rotary(query_pre[..., QKD:], head_cos, head_sin)], axis=-1
    ).astype(jnp.bfloat16)
    compressed = jnp.dot(hidden_first, down_weight, preferred_element_type=jnp.float32)
    normed_latent, scaling_latent = normalize(compressed[:, :LAT])
    latent_low = (normed_latent * gain_latent).astype(jnp.bfloat16)
    rope_low = rotary(compressed[:, LAT:], cosine, sine_table).astype(jnp.bfloat16)
    key_value = jnp.dot(latent_low, up_weight, preferred_element_type=jnp.float32).astype(
        jnp.bfloat16
    )
    own_heads = key_value.reshape(tok_count, HEADS, QKD + VD)
    self_raw = jnp.einsum(
        "thd,thd->ht",
        query_low[..., :QKD],
        own_heads[..., :QKD],
        preferred_element_type=jnp.float32,
    ) + jnp.einsum("thr,tr->ht", query_low[..., QKD:], rope_low, preferred_element_type=jnp.float32)
    shift_table = jnp.floor(self_raw * score_scale)
    last_block = jnp.max(own_blocks)

    def block_weights(kv_piece, rope_piece, blocks_piece):
        kv_heads = kv_piece.reshape(kv_piece.shape[0], HEADS, QKD + VD)
        raw_scores = head_scores(query_low, kv_heads[..., :QKD], rope_piece)
        allowed = (blocks_piece[None, :] <= own_blocks[:, None])[None]
        shifted = jnp.where(allowed, raw_scores * score_scale - shift_table[:, :, None], 0.0)
        return (kv_heads, jnp.where(allowed, jnp.exp(shifted), 0.0))

    empty_state = (
        jnp.zeros((tok_count, HEADS, VD), jnp.float32),
        jnp.zeros((HEADS, tok_count), jnp.float32),
    )
    kv_piece = lax.all_gather(key_value, "context", axis=0, tiled=True)
    rope_piece = lax.all_gather(rope_low, "context", axis=0, tiled=True)
    blocks_piece = lax.all_gather(own_blocks, "context", axis=0, tiled=True)
    make_kv = lambda: kv_piece

    def attend_compute(state_now):
        kv_heads, weights = block_weights(make_kv(), rope_piece, blocks_piece)
        running = jnp.einsum(
            "htn,nhv->thv",
            weights.astype(jnp.bfloat16),
            kv_heads[..., QKD:],
            preferred_element_type=jnp.float32,
        )
        return (running, jnp.sum(weights, axis=-1))

    running, denominator = lax.cond(
        jnp.min(blocks_piece) > last_block, lambda state_now: state_now, attend_compute, empty_state
    )
    denom_rows = jnp.transpose(denominator)
    attended = running / denom_rows[:, :, None]
    mixed_low = attended.reshape(tok_count, HEADS * VD).astype(jnp.bfloat16)
    residual_mid = residual_in + jnp.dot(mixed_low, out_weight, preferred_element_type=jnp.float32)
    normed_second, scaling_second = normalize(residual_mid)
    hidden_second = (normed_second * gain_two).astype(jnp.bfloat16)
    logits = jnp.dot(hidden_second, router_weight, preferred_element_type=jnp.float32)
    route_onehot = (route_ids[:, :, None] == jnp.arange(experts_total)[None, None, :]).astype(
        jnp.float32
    )
    chosen = jnp.sum(route_onehot * logits[:, None, :], axis=-1)
    gate_weights = jax.nn.softmax(chosen, axis=-1)
    shared_pre = jnp.dot(hidden_second, shared_in_weight, preferred_element_type=jnp.float32)
    shared_act = (jax.nn.silu(shared_pre[:, :SHARED]) * shared_pre[:, SHARED:]).astype(jnp.bfloat16)
    shared_result = jnp.dot(shared_act, shared_out_weight, preferred_element_type=jnp.float32)
    slot_index = (route_ids * capacity + slot_ids).reshape(-1)
    model_width = hidden_second.shape[1]
    repeated = jnp.broadcast_to(hidden_second[:, None, :], (tok_count, TOP, model_width)).reshape(
        tok_count * TOP, model_width
    )
    send_rows = (
        jnp.zeros((experts_total * capacity, model_width), jnp.bfloat16)
        .at[slot_index]
        .set(repeated)
    )
    weight_in_local = w_expert_in[0]
    weight_out_local = w_expert_out[0]
    received = lax.all_to_all(
        both_halves(send_rows, experts_total, capacity),
        ("context", "expert"),
        split_axis=0,
        concat_axis=0,
        tiled=True,
    )
    pre_expert = jnp.einsum(
        "scd,df->scf", received, weight_in_local, preferred_element_type=jnp.float32
    )
    activation = (jax.nn.silu(pre_expert[..., :HALF]) * pre_expert[..., HALF:]).astype(jnp.bfloat16)
    part_rows = jnp.einsum(
        "scf,fd->scd", activation, weight_out_local, preferred_element_type=jnp.float32
    ).astype(jnp.bfloat16)
    returned = lax.all_to_all(
        part_rows, ("context", "expert"), split_axis=0, concat_axis=0, tiled=True
    )
    returned, received_rows, pre_expert = (returned, received, pre_expert)
    expert_table = halves_sum(returned, experts_total, capacity)
    picked = expert_table[slot_index].reshape(tok_count, TOP, model_width)
    routed = jnp.sum(gate_weights[:, :, None] * picked, axis=1)
    output_low = (residual_mid + shared_result + routed).astype(jnp.bfloat16)
    grad_low = cotangent[0]
    grad_out = grad_low.astype(jnp.float32)
    grad_shared_out = jnp.dot(shared_act.T, grad_low, preferred_element_type=jnp.float32)
    grad_shared_act = jnp.dot(grad_low, shared_out_weight.T, preferred_element_type=jnp.float32)
    shared_gate = shared_pre[:, :SHARED]
    shared_up = shared_pre[:, SHARED:]
    grad_shared_pre = jnp.concatenate(
        [
            silu_back(shared_gate, grad_shared_act * shared_up),
            grad_shared_act * jax.nn.silu(shared_gate),
        ],
        axis=-1,
    ).astype(jnp.bfloat16)
    grad_shared_in = jnp.dot(hidden_second.T, grad_shared_pre, preferred_element_type=jnp.float32)
    grad_hidden = jnp.dot(grad_shared_pre, shared_in_weight.T, preferred_element_type=jnp.float32)
    grad_gates = jnp.sum(grad_out[:, None, :] * picked, axis=-1)
    grad_chosen = gate_weights * (
        grad_gates - jnp.sum(gate_weights * grad_gates, axis=-1, keepdims=True)
    )
    grad_logits = jnp.sum(route_onehot * grad_chosen[:, :, None], axis=1).astype(jnp.bfloat16)
    grad_router = jnp.dot(hidden_second.T, grad_logits, preferred_element_type=jnp.float32)
    grad_hidden = grad_hidden + jnp.dot(
        grad_logits, router_weight.T, preferred_element_type=jnp.float32
    )
    grad_parts = (
        (gate_weights[:, :, None] * grad_out[:, None, :])
        .astype(jnp.bfloat16)
        .reshape(tok_count * TOP, model_width)
    )
    grad_send = (
        jnp.zeros((experts_total * capacity, model_width), jnp.bfloat16)
        .at[slot_index]
        .set(grad_parts)
    )
    grad_received = lax.all_to_all(
        both_halves(grad_send, experts_total, capacity),
        ("context", "expert"),
        split_axis=0,
        concat_axis=0,
        tiled=True,
    )
    expert_gate = pre_expert[..., :HALF]
    expert_up = pre_expert[..., HALF:]
    expert_silu = jax.nn.silu(expert_gate)
    expert_act = (expert_silu * expert_up).astype(jnp.bfloat16)
    grad_expert_out = jnp.einsum(
        "scf,scd->fd", expert_act, grad_received, preferred_element_type=jnp.float32
    )
    grad_expert_act = jnp.einsum(
        "scd,fd->scf", grad_received, weight_out_local, preferred_element_type=jnp.float32
    )
    grad_expert_pre = jnp.concatenate(
        [silu_back(expert_gate, grad_expert_act * expert_up), grad_expert_act * expert_silu],
        axis=-1,
    ).astype(jnp.bfloat16)
    grad_expert_in = jnp.einsum(
        "scd,scf->df", received_rows, grad_expert_pre, preferred_element_type=jnp.float32
    )
    grad_rows = jnp.einsum(
        "scf,df->scd", grad_expert_pre, weight_in_local, preferred_element_type=jnp.float32
    )
    grad_back = lax.all_to_all(
        grad_rows.astype(jnp.bfloat16),
        ("context", "expert"),
        split_axis=0,
        concat_axis=0,
        tiled=True,
    ).astype(grad_rows.dtype)
    grad_table = halves_sum(grad_back, experts_total, capacity)
    grad_hidden = grad_hidden + jnp.sum(
        grad_table[slot_index].reshape(tok_count, TOP, model_width), axis=1
    )
    grad_mid_norm, grad_gain_second = norm_back(
        grad_hidden, normed_second, scaling_second, gain_two
    )
    grad_resid = grad_out + grad_mid_norm
    grad_resid_low = grad_resid.astype(jnp.bfloat16)
    grad_attn_out = jnp.dot(mixed_low.T, grad_resid_low, preferred_element_type=jnp.float32)
    grad_mixed = jnp.dot(grad_resid_low, out_weight.T, preferred_element_type=jnp.float32).reshape(
        tok_count, HEADS, VD
    )
    scaled_low = (grad_mixed / denom_rows[:, :, None]).astype(jnp.bfloat16)
    correction = jnp.transpose(jnp.sum(grad_mixed * attended, axis=-1) / denom_rows)
    full_kv, full_rope, full_blocks, full_latent = (
        lax.all_gather(key_value, "context", axis=0, tiled=True),
        lax.all_gather(rope_low, "context", axis=0, tiled=True),
        lax.all_gather(own_blocks, "context", axis=0, tiled=True),
        lax.all_gather(latent_low, "context", axis=0, tiled=True),
    )
    key_block = math.gcd(length_all, 512)
    block_count = length_all // key_block
    kv_width = HEADS * (QKD + VD)

    def key_step(grad_query, block_index):
        begin_row = block_index * key_block
        kv_piece = lax.dynamic_slice_in_dim(full_kv, begin_row, key_block, 0)
        rope_piece = lax.dynamic_slice_in_dim(full_rope, begin_row, key_block, 0)
        blocks_piece = lax.dynamic_slice_in_dim(full_blocks, begin_row, key_block, 0)

        def key_compute(grad_acc):
            kv_heads, weights = block_weights(kv_piece, rope_piece, blocks_piece)
            grad_weights = jnp.einsum(
                "thv,nhv->htn", scaled_low, kv_heads[..., QKD:], preferred_element_type=jnp.float32
            )
            grad_raw = (weights * (grad_weights - correction[:, :, None]) * score_scale).astype(
                jnp.bfloat16
            )
            grad_nope = jnp.einsum(
                "htn,nhd->thd", grad_raw, kv_heads[..., :QKD], preferred_element_type=jnp.float32
            )
            grad_rot = jnp.einsum(
                "htn,nr->thr", grad_raw, rope_piece, preferred_element_type=jnp.float32
            )
            grad_key = jnp.einsum(
                "htn,thd->nhd", grad_raw, query_low[..., :QKD], preferred_element_type=jnp.float32
            )
            grad_value = jnp.einsum(
                "htn,thv->nhv",
                weights.astype(jnp.bfloat16),
                scaled_low,
                preferred_element_type=jnp.float32,
            )
            grad_rope = jnp.einsum(
                "htn,thr->nr", grad_raw, query_low[..., QKD:], preferred_element_type=jnp.float32
            )
            grad_kv = jnp.concatenate([grad_key, grad_value], axis=-1).reshape(key_block, kv_width)
            return (grad_acc + jnp.concatenate([grad_nope, grad_rot], axis=-1), grad_kv, grad_rope)

        def skipped(grad_acc):
            return (
                grad_acc,
                jnp.zeros((key_block, kv_width), jnp.float32),
                jnp.zeros((key_block, RD), jnp.float32),
            )

        grad_query, grad_kv, grad_rope = lax.cond(
            jnp.min(blocks_piece) > last_block, skipped, key_compute, grad_query
        )
        return (grad_query, (grad_kv, grad_rope))

    grad_query_rot, (grad_kv_blocks, grad_rope_blocks) = lax.scan(
        key_step, jnp.zeros((tok_count, HEADS, QKD + RD), jnp.float32), jnp.arange(block_count)
    )
    partial_kv = grad_kv_blocks.reshape(length_all, kv_width)
    partial_rope = grad_rope_blocks.reshape(length_all, RD)
    up_float = up_weight.astype(jnp.float32)
    kv_sum, rope_sum = (
        lax.psum_scatter(
            partial_kv.astype(jnp.bfloat16), "context", scatter_dimension=0, tiled=True
        ).astype(jnp.float32),
        lax.psum_scatter(
            partial_rope.astype(jnp.bfloat16), "context", scatter_dimension=0, tiled=True
        ).astype(jnp.float32),
    )
    grad_up_kv = jnp.dot(
        latent_low.astype(jnp.float32).T,
        kv_sum,
        precision=highest,
        preferred_element_type=jnp.float32,
    )
    grad_latent = jnp.dot(kv_sum, up_float.T, precision=highest, preferred_element_type=jnp.float32)
    grad_latent_pre, grad_gain_latent = norm_back(
        grad_latent, normed_latent, scaling_latent, gain_latent
    )
    grad_compressed = jnp.concatenate(
        [grad_latent_pre, rotary_back(rope_sum, cosine, sine_table)], axis=-1
    ).astype(jnp.bfloat16)
    grad_down_kv = jnp.dot(hidden_first.T, grad_compressed, preferred_element_type=jnp.float32)
    grad_query_low = (
        jnp.concatenate(
            [grad_query_rot[..., :QKD], rotary_back(grad_query_rot[..., QKD:], head_cos, head_sin)],
            axis=-1,
        )
        .astype(jnp.bfloat16)
        .reshape(tok_count, HEADS * (QKD + RD))
    )
    grad_query_weight = jnp.dot(hidden_first.T, grad_query_low, preferred_element_type=jnp.float32)
    grad_hidden_first = jnp.dot(
        grad_query_low, query_weight.T, preferred_element_type=jnp.float32
    ) + jnp.dot(grad_compressed, down_weight.T, preferred_element_type=jnp.float32)
    grad_first_norm, grad_gain_first = norm_back(
        grad_hidden_first, normed_first, scaling_first, gain_one
    )
    grad_input = grad_resid + grad_first_norm
    (
        grad_norm_one,
        grad_wq,
        grad_wdkv,
        grad_gkv,
        grad_wukv,
        grad_wo,
        grad_norm_two,
        grad_wr,
        grad_wsi,
        grad_wso,
    ) = (
        lax.psum_scatter(grad_gain_first, ("context", "expert"), scatter_dimension=0, tiled=True),
        lax.psum_scatter(grad_query_weight, ("context", "expert"), scatter_dimension=0, tiled=True),
        lax.psum_scatter(grad_down_kv, ("context", "expert"), scatter_dimension=0, tiled=True),
        lax.psum_scatter(grad_gain_latent, ("context", "expert"), scatter_dimension=0, tiled=True),
        lax.psum_scatter(grad_up_kv, ("context", "expert"), scatter_dimension=1, tiled=True),
        lax.psum_scatter(grad_attn_out, ("context", "expert"), scatter_dimension=1, tiled=True),
        lax.psum_scatter(grad_gain_second, ("context", "expert"), scatter_dimension=0, tiled=True),
        lax.psum_scatter(grad_router, ("context", "expert"), scatter_dimension=0, tiled=True),
        lax.psum_scatter(grad_shared_in, ("context", "expert"), scatter_dimension=0, tiled=True),
        lax.psum_scatter(grad_shared_out, ("context", "expert"), scatter_dimension=1, tiled=True),
    )
    return (
        output_low[None],
        grad_input[None],
        grad_norm_one,
        grad_wq,
        grad_wdkv,
        grad_gkv,
        grad_wukv,
        grad_wo,
        grad_norm_two,
        grad_wr,
        grad_wsi,
        grad_wso,
        grad_expert_in[None],
        grad_expert_out[None],
    )


def fast_body(nc, nz):
    nd = nc * nz
    hc = HEADS // nc
    qw = hc * (QKD + RD)
    ow = hc * VD
    units = SHARED // nd
    pad = -(-units // 128) * 128
    both = ("context", "expert")
    dot = functools.partial(jnp.dot, preferred_element_type=jnp.float32)
    ein = functools.partial(jnp.einsum, preferred_element_type=jnp.float32)
    low = lambda v: v.astype(jnp.bfloat16)
    wide = lambda v: v.astype(jnp.float32)

    def body(
        tokens, norm1_gain, w_query, w_down_kv, kv_gain, w_up_kv, w_attn_out, norm2_gain, w_router,
        w_shared_in, w_shared_out, w_expert_in, w_expert_out, routes, slots, blocks, cotangent,
    ):
        device = lax.axis_index("context") * nz + lax.axis_index("expert")
        my_expert = device // 2
        tok = tokens.shape[1]
        width = tokens.shape[2]
        rows = width // nd
        length = tok * nc
        total = tok * nd
        experts = w_router.shape[1]
        cap = tok * TOP // experts * 4 // 3
        scale = (QKD + RD) ** (-0.5)

        small = jnp.concatenate([norm1_gain, norm2_gain, w_router.reshape(-1), kv_gain])[None]
        small = lax.all_gather(small, both, axis=0, tiled=True)
        gain_one = wide(small[:, :rows].reshape(-1))
        gain_two = wide(small[:, rows : 2 * rows].reshape(-1))
        router = small[:, 2 * rows : 2 * rows + rows * experts].reshape(width, experts)
        gain_latent = wide(small[:, 2 * rows + rows * experts :].reshape(-1))
        tok_seq = lax.all_gather(tokens[0], "context", axis=0, tiled=True)
        down = lax.all_gather(w_down_kv, both, axis=0, tiled=True)
        wq = w_query.reshape(rows, nc, hc, QKD + RD)
        wq = jnp.concatenate(
            [
                wq[..., :QKD].reshape(rows, nc, hc * QKD),
                wq[..., QKD:].reshape(rows, nc, hc * RD),
                w_attn_out.T.reshape(rows, nc, ow),
            ],
            axis=-1,
        ).transpose(1, 0, 2)
        wq = lax.all_to_all(wq, "context", split_axis=0, concat_axis=0, tiled=True)
        wq = lax.all_gather(wq, "expert", axis=1, tiled=False).reshape(width, qw + ow)
        out_t = wq[:, qw:]
        wq = wq[:, :qw]
        up = lax.all_gather(w_up_kv, "expert", axis=1, tiled=True)
        shared = jnp.stack(
            [
                w_shared_in[:, :SHARED].reshape(rows, nd, units),
                w_shared_in[:, SHARED:].reshape(rows, nd, units),
                w_shared_out.T.reshape(rows, nd, units),
            ],
            axis=2,
        )
        shared = jnp.pad(shared, ((0, 0), (0, 0), (0, 0), (0, pad - units)))
        shared = shared.transpose(1, 0, 2, 3).reshape(nd, rows, 3 * pad)
        shared = lax.all_to_all(shared, both, split_axis=0, concat_axis=0, tiled=True)
        shared = shared.reshape(width, 3 * pad)
        shared_in = shared[:, : 2 * pad]
        shared_out_t = shared[:, 2 * pad :]
        plan = jnp.concatenate([routes[0], slots[0]], axis=1)
        plan = lax.all_gather(plan, both, axis=0, tiled=True).reshape(nd, tok, 2 * TOP)
        block_seq = lax.all_gather(blocks[0], "context", axis=0, tiled=True)
        cot_all = lax.all_gather(cotangent[0], both, axis=0, tiled=True)

        cosine, sine = rotation_table(jnp.arange(length, dtype=jnp.float32))
        head_cos, head_sin = cosine[:, None, :], sine[:, None, :]
        normed_seq, _ = normalize(wide(tok_seq))
        hidden_seq = low(normed_seq * gain_one)
        query = dot(hidden_seq, wq)
        q_nope = low(query[:, : hc * QKD]).reshape(length, hc, QKD)
        q_rope = low(rotary(query[:, hc * QKD :].reshape(length, hc, RD), head_cos, head_sin))
        compressed = dot(hidden_seq, down)
        normed_latent, scaling_latent = normalize(compressed[:, :LAT])
        latent = low(normed_latent * gain_latent)
        rope_key = low(rotary(compressed[:, LAT:], cosine, sine))
        key_value = low(dot(latent, up)).reshape(length, hc, QKD + VD)
        key, value = key_value[..., :QKD], key_value[..., QKD:]
        raw = ein("thd,nhd->htn", q_nope, key) + ein("thr,nr->htn", q_rope, rope_key)
        self_raw = jnp.sum(wide(q_nope) * wide(key), axis=-1) + jnp.sum(
            wide(q_rope) * wide(rope_key)[:, None, :], axis=-1
        )
        shift = jnp.floor(self_raw * scale).T
        allowed = (block_seq[None, :] <= block_seq[:, None])[None]
        weights = jnp.where(
            allowed, jnp.exp(jnp.where(allowed, raw * scale - shift[:, :, None], 0.0)), 0.0
        )
        weights_low = low(weights)
        denominator = jnp.sum(weights, axis=-1)
        denom_rows = denominator.T[:, :, None]
        attended = ein("htn,nhv->thv", weights_low, value) / denom_rows
        mixed = low(attended.reshape(length, ow))
        resid_part = low(lax.dot_general(mixed, out_t, (((1,), (1,)), ((), ())),
                                         preferred_element_type=jnp.float32))
        resid = wide(tokens[0]) + wide(
            lax.psum_scatter(resid_part, "context", scatter_dimension=0, tiled=True)
        )

        normed_second, scaling_second = normalize(resid)
        hidden = low(normed_second * gain_two)
        logits = dot(hidden, router)
        onehot = wide(routes[0][:, :, None] == jnp.arange(experts)[None, None, :])
        gates = jax.nn.softmax(jnp.sum(onehot * logits[:, None, :], axis=-1), axis=-1)
        gates_dense = jnp.sum(onehot * gates[:, :, None], axis=1)
        gates_all = lax.all_gather(gates_dense, both, axis=0, tiled=True)
        hidden_all = lax.all_gather(hidden, both, axis=0, tiled=True)

        named = plan[:, :, :TOP] == my_expert
        slot_of = jnp.max(jnp.where(named, plan[:, :, TOP:], -1), axis=-1)
        pick = slot_of[:, None, :] == jnp.arange(cap)[None, :, None]
        pick_low = low(pick)
        gate_col = jnp.sum(
            jnp.where(jnp.arange(experts)[None, :] == my_expert, gates_all, 0.0), axis=1
        ).reshape(nd, 1, tok)
        gate_rows = jnp.sum(jnp.where(pick, gate_col, 0.0), axis=-1).reshape(nd * cap, 1)
        take = lambda table: low(ein("bst,btd->bsd", pick_low, table.reshape(nd, tok, width))).reshape(
            nd * cap, width
        )
        give = lambda table: ein("bst,bsd->btd", pick_low, table.reshape(nd, cap, width)).reshape(
            total, width
        )
        expert_in, expert_out = w_expert_in[0], w_expert_out[0]
        picked = take(hidden_all)
        pre = dot(picked, expert_in)
        expert_gate, expert_up = pre[:, :HALF], pre[:, HALF:]
        expert_silu = jax.nn.silu(expert_gate)
        act = low(expert_silu * expert_up)
        part = wide(low(dot(act, expert_out)))
        shared_pre = dot(hidden_all, shared_in)
        shared_gate, shared_up = shared_pre[:, :pad], shared_pre[:, pad:]
        shared_silu = jax.nn.silu(shared_gate)
        shared_act = low(shared_silu * shared_up)
        result = give(low(part * gate_rows)) + lax.dot_general(
            shared_act, shared_out_t, (((1,), (1,)), ((), ())), preferred_element_type=jnp.float32
        )
        output = low(
            resid
            + wide(lax.psum_scatter(low(result), both, scatter_dimension=0, tiled=True))
        )

        cot_rows = wide(take(cot_all))
        dots = jnp.sum(cot_rows * part, axis=-1).reshape(nd, cap, 1)
        dots = jnp.sum(jnp.where(pick, dots, 0.0), axis=1)
        dots = lax.all_to_all(dots, both, split_axis=0, concat_axis=0, tiled=True)
        grad_gates = dots.reshape(experts, nd // experts, tok).sum(axis=1).T
        grad_logits = low(
            gates_dense
            * (grad_gates - jnp.sum(gates_dense * grad_gates, axis=-1, keepdims=True))
        )
        grad_part = low(cot_rows * gate_rows)
        grad_act = lax.dot_general(
            grad_part, expert_out, (((1,), (1,)), ((), ())), preferred_element_type=jnp.float32
        )
        grad_pre = low(
            jnp.concatenate(
                [silu_back(expert_gate, grad_act * expert_up), grad_act * expert_silu], axis=-1
            )
        )
        grad_expert_out = dot(act.T, grad_part)
        grad_expert_in = dot(picked.T, grad_pre)
        grad_rows = low(
            lax.dot_general(
                grad_pre, expert_in, (((1,), (1,)), ((), ())), preferred_element_type=jnp.float32
            )
        )
        grad_shared_act = dot(cot_all, shared_out_t)
        grad_shared_pre = low(
            jnp.concatenate(
                [silu_back(shared_gate, grad_shared_act * shared_up), grad_shared_act * shared_silu],
                axis=-1,
            )
        )
        grad_shared = jnp.concatenate(
            [dot(hidden_all.T, grad_shared_pre), dot(cot_all.T, shared_act)], axis=-1
        )
        grad_hidden_part = give(grad_rows) + lax.dot_general(
            grad_shared_pre, shared_in, (((1,), (1,)), ((), ())), preferred_element_type=jnp.float32
        )
        grad_hidden = wide(
            lax.psum_scatter(low(grad_hidden_part), both, scatter_dimension=0, tiled=True)
        ) + dot(grad_logits, router.T)
        grad_mid, grad_gain_two = norm_back(grad_hidden, normed_second, scaling_second, gain_two)
        grad_resid = wide(cotangent[0]) + grad_mid
        grad_router = dot(hidden.T, grad_logits)

        grad_resid_seq = lax.all_gather(low(grad_resid), "context", axis=0, tiled=True)
        grad_mixed = dot(grad_resid_seq, out_t).reshape(length, hc, VD)
        grad_out_t = dot(grad_resid_seq.T, mixed)
        scaled = low(grad_mixed / denom_rows)
        correction = (jnp.sum(grad_mixed * attended, axis=-1) / denominator.T).T
        grad_weights = ein("thv,nhv->htn", scaled, value)
        grad_raw = low(weights * (grad_weights - correction[:, :, None]) * scale)
        grad_nope = ein("htn,nhd->thd", grad_raw, key)
        grad_rot = ein("htn,nr->thr", grad_raw, rope_key)
        grad_key = ein("htn,thd->nhd", grad_raw, q_nope)
        grad_value = ein("htn,thv->nhv", weights_low, scaled)
        grad_rope = ein("htn,thr->nr", grad_raw, q_rope)
        grad_kv = low(jnp.concatenate([grad_key, grad_value], axis=-1).reshape(length, hc * (QKD + VD)))
        grad_up = dot(latent.T, grad_kv)
        grad_latent = lax.dot_general(
            grad_kv, up, (((1,), (1,)), ((), ())), preferred_element_type=jnp.float32
        )
        grad_latent_pre, grad_gain_latent = norm_back(
            grad_latent, normed_latent, scaling_latent, gain_latent
        )
        grad_compressed = low(
            jnp.concatenate([grad_latent_pre, rotary_back(grad_rope, cosine, sine)], axis=-1)
        )
        grad_query = low(
            jnp.concatenate(
                [
                    grad_nope.reshape(length, hc * QKD),
                    rotary_back(grad_rot, head_cos, head_sin).reshape(length, hc * RD),
                ],
                axis=-1,
            )
        )
        grad_attn = jnp.concatenate([dot(hidden_seq.T, grad_query), grad_out_t], axis=-1)
        grad_down = dot(hidden_seq.T, grad_compressed)
        grad_first_part = low(
            lax.dot_general(
                grad_query, wq, (((1,), (1,)), ((), ())), preferred_element_type=jnp.float32
            )
            + lax.dot_general(
                grad_compressed, down, (((1,), (1,)), ((), ())), preferred_element_type=jnp.float32
            )
        )
        grad_first = wide(
            lax.psum_scatter(grad_first_part, "context", scatter_dimension=0, tiled=True)
        )
        normed_first, scaling_first = normalize(wide(tokens[0]))
        grad_input, grad_gain_one = norm_back(grad_first, normed_first, scaling_first, gain_one)
        grad_input = grad_input + grad_resid

        exchange = lambda table: lax.all_to_all(
            low(table).reshape(nd, rows, table.shape[-1]), both, split_axis=0, concat_axis=0, tiled=True
        )
        shared_back = exchange(grad_shared).reshape(nd, rows, 3, pad)[..., :units]
        grad_wsi = wide(shared_back[:, :, :2].transpose(1, 2, 0, 3)).reshape(rows, 2 * SHARED)
        grad_wso = wide(shared_back[:, :, 2].transpose(0, 2, 1)).reshape(SHARED, rows)
        attn_back = wide(exchange(grad_attn)).reshape(nc, nz, rows, qw + ow).sum(axis=1)
        grad_wq = jnp.concatenate(
            [
                attn_back[:, :, : hc * QKD].reshape(nc, rows, hc, QKD),
                attn_back[:, :, hc * QKD : qw].reshape(nc, rows, hc, RD),
            ],
            axis=-1,
        ).transpose(1, 0, 2, 3).reshape(rows, HEADS * (QKD + RD))
        grad_wo = attn_back[:, :, qw:].transpose(0, 2, 1).reshape(HEADS * VD, rows)
        grad_wdkv = wide(exchange(grad_down)).sum(axis=0)
        grad_wukv = wide(
            lax.psum_scatter(low(grad_up), "expert", scatter_dimension=1, tiled=True)
        )
        tiny = jnp.concatenate(
            [
                grad_gain_one.reshape(nd, rows),
                grad_gain_two.reshape(nd, rows),
                grad_router.reshape(nd, rows * experts),
                grad_gain_latent.reshape(nd, LAT // nd),
            ],
            axis=1,
        )
        tiny = lax.all_to_all(tiny, both, split_axis=0, concat_axis=0, tiled=True).sum(axis=0)
        return (
            output[None],
            grad_input[None],
            tiny[:rows],
            grad_wq,
            grad_wdkv,
            tiny[2 * rows + rows * experts :],
            grad_wukv,
            grad_wo,
            tiny[rows : 2 * rows],
            tiny[2 * rows : 2 * rows + rows * experts].reshape(rows, experts),
            grad_wsi,
            grad_wso,
            grad_expert_in[None],
            grad_expert_out[None],
        )

    return body


def solution(mesh):
    placed = (
        P("expert", "context", None),
        P(("context", "expert")),
        P(("context", "expert"), None),
        P(("context", "expert"), None),
        P(("context", "expert")),
        P(None, ("context", "expert")),
        P(None, ("context", "expert")),
        P(("context", "expert")),
        P(("context", "expert"), None),
        P(("context", "expert"), None),
        P(None, ("context", "expert")),
        P(("context", "expert"), None, None),
        P(("context", "expert"), None, None),
        P("expert", "context", None),
        P("expert", "context", None),
        P("expert", "context"),
        P("expert", "context", None),
    )
    nc, nz = mesh.shape["context"], mesh.shape["expert"]
    split = HEADS % nc == 0 and SHARED % (nc * nz) == 0
    return jax.shard_map(
        fast_body(nc, nz) if split else body,
        mesh=mesh,
        in_specs=placed,
        out_specs=(
            P("expert", "context", None),
            P("expert", "context", None),
            P(("context", "expert")),
            P(("context", "expert"), None),
            P(("context", "expert"), None),
            P(("context", "expert")),
            P(None, ("context", "expert")),
            P(None, ("context", "expert")),
            P(("context", "expert")),
            P(("context", "expert"), None),
            P(("context", "expert"), None),
            P(None, ("context", "expert")),
            P(("context", "expert"), None, None),
            P(("context", "expert"), None, None),
        ),
        check_vma=False,
    )
```

```python
import functools
import math

import jax
import jax.numpy as jnp
from jax import lax
from jax.sharding import PartitionSpec as P

HEADS = 16
QKD = 128
RD = 64
VD = 128
LAT = 512
TOP = 6
SHARED = 2816
HALF = 704
CTX = "context"
EXP = "expert"
BOTH = (CTX, EXP)


epsilon = 1e-06
highest = lax.Precision.HIGHEST


def normalize(values):
    scaling = lax.rsqrt(jnp.mean(values * values, axis=-1, keepdims=True) + epsilon)
    return (values * scaling, scaling)


def norm_back(grad_normed, normed, scaling, gain):
    grad_gain = jnp.sum(grad_normed * normed, axis=0)
    grad_unit = grad_normed * gain
    grad_values = scaling * (
        grad_unit - normed * jnp.mean(grad_unit * normed, axis=-1, keepdims=True)
    )
    return (grad_values, grad_gain)


def rotary(values, cosine, sine_table):
    middle = values.shape[-1] // 2
    first_half = values[..., :middle]
    second_half = values[..., middle:]
    return jnp.concatenate(
        [
            first_half * cosine - second_half * sine_table,
            second_half * cosine + first_half * sine_table,
        ],
        axis=-1,
    )


def rotary_back(grads_in, cosine, sine_table):
    middle = grads_in.shape[-1] // 2
    first_half = grads_in[..., :middle]
    second_half = grads_in[..., middle:]
    return jnp.concatenate(
        [
            first_half * cosine + second_half * sine_table,
            second_half * cosine - first_half * sine_table,
        ],
        axis=-1,
    )


def rotation_table(positions):
    exponent = jnp.arange(RD // 2, dtype=jnp.float32) * (2.0 / RD)
    angle_table = positions[:, None] * (10000.0 ** (-exponent))[None, :]
    return (jnp.cos(angle_table), jnp.sin(angle_table))


def silu_back(value, grads_in):
    sigma_value = jax.nn.sigmoid(value)
    return grads_in * sigma_value * (1.0 + value * (1.0 - sigma_value))


def head_scores(query_low, key_low, rope_low):
    nope_part = jnp.einsum(
        "thd,nhd->htn", query_low[..., :QKD], key_low, preferred_element_type=jnp.float32
    )
    rope_part = jnp.einsum(
        "thr,nr->htn", query_low[..., QKD:], rope_low, preferred_element_type=jnp.float32
    )
    return nope_part + rope_part


def both_halves(buffer_rows, experts_total, capacity):
    width = buffer_rows.shape[-1]
    shaped = buffer_rows.reshape(experts_total, 1, capacity, width)
    return jnp.broadcast_to(shaped, (experts_total, 2, capacity, width)).reshape(
        2 * experts_total, capacity, width
    )


def halves_sum(received, experts_total, capacity):
    width = received.shape[-1]
    return (
        received.astype(jnp.float32)
        .reshape(experts_total, 2, capacity, width)
        .sum(axis=1)
        .reshape(experts_total * capacity, width)
    )


def body(
    tokens,
    norm1_gain,
    w_query,
    w_down_kv,
    kv_gain,
    w_up_kv,
    w_attn_out,
    norm2_gain,
    w_router,
    w_shared_in,
    w_shared_out,
    w_expert_in,
    w_expert_out,
    routes,
    slots,
    blocks,
    cotangent,
):
    (
        gain_first,
        query_weight,
        down_weight,
        latent_gain,
        up_weight,
        out_weight,
        gain_second,
        router_weight,
        shared_in_weight,
        shared_out_weight,
    ) = (
        lax.all_gather(norm1_gain, BOTH, axis=0, tiled=True),
        lax.all_gather(w_query, BOTH, axis=0, tiled=True),
        lax.all_gather(w_down_kv, BOTH, axis=0, tiled=True),
        lax.all_gather(kv_gain, BOTH, axis=0, tiled=True),
        lax.all_gather(w_up_kv, BOTH, axis=1, tiled=True),
        lax.all_gather(w_attn_out, BOTH, axis=1, tiled=True),
        lax.all_gather(norm2_gain, BOTH, axis=0, tiled=True),
        lax.all_gather(w_router, BOTH, axis=0, tiled=True),
        lax.all_gather(w_shared_in, BOTH, axis=0, tiled=True),
        lax.all_gather(w_shared_out, BOTH, axis=1, tiled=True),
    )
    tok_count = tokens.shape[1]
    length_all = tok_count * lax.axis_size(CTX)
    experts_total = router_weight.shape[1]
    capacity = tok_count * TOP // experts_total * 4 // 3
    score_scale = (QKD + RD) ** (-0.5)
    residual_in = tokens[0].astype(jnp.float32)
    own_blocks = blocks[0]
    route_ids = routes[0]
    slot_ids = slots[0]
    positions = (lax.axis_index(CTX) * tok_count + jnp.arange(tok_count)).astype(jnp.float32)
    cosine, sine_table = rotation_table(positions)
    head_cos = cosine[:, None, :]
    head_sin = sine_table[:, None, :]
    gain_one = gain_first.astype(jnp.float32)
    gain_two = gain_second.astype(jnp.float32)
    gain_latent = latent_gain.astype(jnp.float32)
    normed_first, scaling_first = normalize(residual_in)
    hidden_first = (normed_first * gain_one).astype(jnp.bfloat16)
    query_pre = jnp.dot(hidden_first, query_weight, preferred_element_type=jnp.float32).reshape(
        tok_count, HEADS, QKD + RD
    )
    query_low = jnp.concatenate(
        [query_pre[..., :QKD], rotary(query_pre[..., QKD:], head_cos, head_sin)], axis=-1
    ).astype(jnp.bfloat16)
    compressed = jnp.dot(hidden_first, down_weight, preferred_element_type=jnp.float32)
    normed_latent, scaling_latent = normalize(compressed[:, :LAT])
    latent_low = (normed_latent * gain_latent).astype(jnp.bfloat16)
    rope_low = rotary(compressed[:, LAT:], cosine, sine_table).astype(jnp.bfloat16)
    key_value = jnp.dot(latent_low, up_weight, preferred_element_type=jnp.float32).astype(
        jnp.bfloat16
    )
    own_heads = key_value.reshape(tok_count, HEADS, QKD + VD)
    self_raw = jnp.einsum(
        "thd,thd->ht",
        query_low[..., :QKD],
        own_heads[..., :QKD],
        preferred_element_type=jnp.float32,
    ) + jnp.einsum("thr,tr->ht", query_low[..., QKD:], rope_low, preferred_element_type=jnp.float32)
    shift_table = jnp.floor(self_raw * score_scale)
    last_block = jnp.max(own_blocks)

    def block_weights(kv_piece, rope_piece, blocks_piece):
        kv_heads = kv_piece.reshape(kv_piece.shape[0], HEADS, QKD + VD)
        raw_scores = head_scores(query_low, kv_heads[..., :QKD], rope_piece)
        allowed = (blocks_piece[None, :] <= own_blocks[:, None])[None]
        shifted = jnp.where(allowed, raw_scores * score_scale - shift_table[:, :, None], 0.0)
        return (kv_heads, jnp.where(allowed, jnp.exp(shifted), 0.0))

    empty_state = (
        jnp.zeros((tok_count, HEADS, VD), jnp.float32),
        jnp.zeros((HEADS, tok_count), jnp.float32),
    )
    kv_piece = lax.all_gather(key_value, CTX, axis=0, tiled=True)
    rope_piece = lax.all_gather(rope_low, CTX, axis=0, tiled=True)
    blocks_piece = lax.all_gather(own_blocks, CTX, axis=0, tiled=True)
    make_kv = lambda: kv_piece

    def attend_compute(state_now):
        kv_heads, weights = block_weights(make_kv(), rope_piece, blocks_piece)
        running = jnp.einsum(
            "htn,nhv->thv",
            weights.astype(jnp.bfloat16),
            kv_heads[..., QKD:],
            preferred_element_type=jnp.float32,
        )
        return (running, jnp.sum(weights, axis=-1))

    running, denominator = lax.cond(
        jnp.min(blocks_piece) > last_block, lambda state_now: state_now, attend_compute, empty_state
    )
    denom_rows = jnp.transpose(denominator)
    attended = running / denom_rows[:, :, None]
    mixed_low = attended.reshape(tok_count, HEADS * VD).astype(jnp.bfloat16)
    residual_mid = residual_in + jnp.dot(mixed_low, out_weight, preferred_element_type=jnp.float32)
    normed_second, scaling_second = normalize(residual_mid)
    hidden_second = (normed_second * gain_two).astype(jnp.bfloat16)
    logits = jnp.dot(hidden_second, router_weight, preferred_element_type=jnp.float32)
    route_onehot = (route_ids[:, :, None] == jnp.arange(experts_total)[None, None, :]).astype(
        jnp.float32
    )
    chosen = jnp.sum(route_onehot * logits[:, None, :], axis=-1)
    gate_weights = jax.nn.softmax(chosen, axis=-1)
    shared_pre = jnp.dot(hidden_second, shared_in_weight, preferred_element_type=jnp.float32)
    shared_act = (jax.nn.silu(shared_pre[:, :SHARED]) * shared_pre[:, SHARED:]).astype(jnp.bfloat16)
    shared_result = jnp.dot(shared_act, shared_out_weight, preferred_element_type=jnp.float32)
    slot_index = (route_ids * capacity + slot_ids).reshape(-1)
    model_width = hidden_second.shape[1]
    repeated = jnp.broadcast_to(hidden_second[:, None, :], (tok_count, TOP, model_width)).reshape(
        tok_count * TOP, model_width
    )
    send_rows = (
        jnp.zeros((experts_total * capacity, model_width), jnp.bfloat16)
        .at[slot_index]
        .set(repeated)
    )
    weight_in_local = w_expert_in[0]
    weight_out_local = w_expert_out[0]
    received = lax.all_to_all(
        both_halves(send_rows, experts_total, capacity),
        BOTH,
        split_axis=0,
        concat_axis=0,
        tiled=True,
    )
    pre_expert = jnp.einsum(
        "scd,df->scf", received, weight_in_local, preferred_element_type=jnp.float32
    )
    activation = (jax.nn.silu(pre_expert[..., :HALF]) * pre_expert[..., HALF:]).astype(jnp.bfloat16)
    part_rows = jnp.einsum(
        "scf,fd->scd", activation, weight_out_local, preferred_element_type=jnp.float32
    ).astype(jnp.bfloat16)
    returned = lax.all_to_all(
        part_rows, BOTH, split_axis=0, concat_axis=0, tiled=True
    )
    returned, received_rows, pre_expert = (returned, received, pre_expert)
    expert_table = halves_sum(returned, experts_total, capacity)
    picked = expert_table[slot_index].reshape(tok_count, TOP, model_width)
    routed = jnp.sum(gate_weights[:, :, None] * picked, axis=1)
    output_low = (residual_mid + shared_result + routed).astype(jnp.bfloat16)
    grad_low = cotangent[0]
    grad_out = grad_low.astype(jnp.float32)
    grad_shared_out = jnp.dot(shared_act.T, grad_low, preferred_element_type=jnp.float32)
    grad_shared_act = jnp.dot(grad_low, shared_out_weight.T, preferred_element_type=jnp.float32)
    shared_gate = shared_pre[:, :SHARED]
    shared_up = shared_pre[:, SHARED:]
    grad_shared_pre = jnp.concatenate(
        [
            silu_back(shared_gate, grad_shared_act * shared_up),
            grad_shared_act * jax.nn.silu(shared_gate),
        ],
        axis=-1,
    ).astype(jnp.bfloat16)
    grad_shared_in = jnp.dot(hidden_second.T, grad_shared_pre, preferred_element_type=jnp.float32)
    grad_hidden = jnp.dot(grad_shared_pre, shared_in_weight.T, preferred_element_type=jnp.float32)
    grad_gates = jnp.sum(grad_out[:, None, :] * picked, axis=-1)
    grad_chosen = gate_weights * (
        grad_gates - jnp.sum(gate_weights * grad_gates, axis=-1, keepdims=True)
    )
    grad_logits = jnp.sum(route_onehot * grad_chosen[:, :, None], axis=1).astype(jnp.bfloat16)
    grad_router = jnp.dot(hidden_second.T, grad_logits, preferred_element_type=jnp.float32)
    grad_hidden = grad_hidden + jnp.dot(
        grad_logits, router_weight.T, preferred_element_type=jnp.float32
    )
    grad_parts = (
        (gate_weights[:, :, None] * grad_out[:, None, :])
        .astype(jnp.bfloat16)
        .reshape(tok_count * TOP, model_width)
    )
    grad_send = (
        jnp.zeros((experts_total * capacity, model_width), jnp.bfloat16)
        .at[slot_index]
        .set(grad_parts)
    )
    grad_received = lax.all_to_all(
        both_halves(grad_send, experts_total, capacity),
        BOTH,
        split_axis=0,
        concat_axis=0,
        tiled=True,
    )
    expert_gate = pre_expert[..., :HALF]
    expert_up = pre_expert[..., HALF:]
    expert_silu = jax.nn.silu(expert_gate)
    expert_act = (expert_silu * expert_up).astype(jnp.bfloat16)
    grad_expert_out = jnp.einsum(
        "scf,scd->fd", expert_act, grad_received, preferred_element_type=jnp.float32
    )
    grad_expert_act = jnp.einsum(
        "scd,fd->scf", grad_received, weight_out_local, preferred_element_type=jnp.float32
    )
    grad_expert_pre = jnp.concatenate(
        [silu_back(expert_gate, grad_expert_act * expert_up), grad_expert_act * expert_silu],
        axis=-1,
    ).astype(jnp.bfloat16)
    grad_expert_in = jnp.einsum(
        "scd,scf->df", received_rows, grad_expert_pre, preferred_element_type=jnp.float32
    )
    grad_rows = jnp.einsum(
        "scf,df->scd", grad_expert_pre, weight_in_local, preferred_element_type=jnp.float32
    )
    grad_back = lax.all_to_all(
        grad_rows.astype(jnp.bfloat16),
        BOTH,
        split_axis=0,
        concat_axis=0,
        tiled=True,
    ).astype(grad_rows.dtype)
    grad_table = halves_sum(grad_back, experts_total, capacity)
    grad_hidden = grad_hidden + jnp.sum(
        grad_table[slot_index].reshape(tok_count, TOP, model_width), axis=1
    )
    grad_mid_norm, grad_gain_second = norm_back(
        grad_hidden, normed_second, scaling_second, gain_two
    )
    grad_resid = grad_out + grad_mid_norm
    grad_resid_low = grad_resid.astype(jnp.bfloat16)
    grad_attn_out = jnp.dot(mixed_low.T, grad_resid_low, preferred_element_type=jnp.float32)
    grad_mixed = jnp.dot(grad_resid_low, out_weight.T, preferred_element_type=jnp.float32).reshape(
        tok_count, HEADS, VD
    )
    scaled_low = (grad_mixed / denom_rows[:, :, None]).astype(jnp.bfloat16)
    correction = jnp.transpose(jnp.sum(grad_mixed * attended, axis=-1) / denom_rows)
    full_kv, full_rope, full_blocks, full_latent = (
        lax.all_gather(key_value, CTX, axis=0, tiled=True),
        lax.all_gather(rope_low, CTX, axis=0, tiled=True),
        lax.all_gather(own_blocks, CTX, axis=0, tiled=True),
        lax.all_gather(latent_low, CTX, axis=0, tiled=True),
    )
    key_block = math.gcd(length_all, 512)
    block_count = length_all // key_block
    kv_width = HEADS * (QKD + VD)

    def key_step(grad_query, block_index):
        begin_row = block_index * key_block
        kv_piece = lax.dynamic_slice_in_dim(full_kv, begin_row, key_block, 0)
        rope_piece = lax.dynamic_slice_in_dim(full_rope, begin_row, key_block, 0)
        blocks_piece = lax.dynamic_slice_in_dim(full_blocks, begin_row, key_block, 0)

        def key_compute(grad_acc):
            kv_heads, weights = block_weights(kv_piece, rope_piece, blocks_piece)
            grad_weights = jnp.einsum(
                "thv,nhv->htn", scaled_low, kv_heads[..., QKD:], preferred_element_type=jnp.float32
            )
            grad_raw = (weights * (grad_weights - correction[:, :, None]) * score_scale).astype(
                jnp.bfloat16
            )
            grad_nope = jnp.einsum(
                "htn,nhd->thd", grad_raw, kv_heads[..., :QKD], preferred_element_type=jnp.float32
            )
            grad_rot = jnp.einsum(
                "htn,nr->thr", grad_raw, rope_piece, preferred_element_type=jnp.float32
            )
            grad_key = jnp.einsum(
                "htn,thd->nhd", grad_raw, query_low[..., :QKD], preferred_element_type=jnp.float32
            )
            grad_value = jnp.einsum(
                "htn,thv->nhv",
                weights.astype(jnp.bfloat16),
                scaled_low,
                preferred_element_type=jnp.float32,
            )
            grad_rope = jnp.einsum(
                "htn,thr->nr", grad_raw, query_low[..., QKD:], preferred_element_type=jnp.float32
            )
            grad_kv = jnp.concatenate([grad_key, grad_value], axis=-1).reshape(key_block, kv_width)
            return (grad_acc + jnp.concatenate([grad_nope, grad_rot], axis=-1), grad_kv, grad_rope)

        def skipped(grad_acc):
            return (
                grad_acc,
                jnp.zeros((key_block, kv_width), jnp.float32),
                jnp.zeros((key_block, RD), jnp.float32),
            )

        grad_query, grad_kv, grad_rope = lax.cond(
            jnp.min(blocks_piece) > last_block, skipped, key_compute, grad_query
        )
        return (grad_query, (grad_kv, grad_rope))

    grad_query_rot, (grad_kv_blocks, grad_rope_blocks) = lax.scan(
        key_step, jnp.zeros((tok_count, HEADS, QKD + RD), jnp.float32), jnp.arange(block_count)
    )
    partial_kv = grad_kv_blocks.reshape(length_all, kv_width)
    partial_rope = grad_rope_blocks.reshape(length_all, RD)
    up_float = up_weight.astype(jnp.float32)
    kv_sum, rope_sum = (
        lax.psum_scatter(
            partial_kv.astype(jnp.bfloat16), CTX, scatter_dimension=0, tiled=True
        ).astype(jnp.float32),
        lax.psum_scatter(
            partial_rope.astype(jnp.bfloat16), CTX, scatter_dimension=0, tiled=True
        ).astype(jnp.float32),
    )
    grad_up_kv = jnp.dot(
        latent_low.astype(jnp.float32).T,
        kv_sum,
        precision=highest,
        preferred_element_type=jnp.float32,
    )
    grad_latent = jnp.dot(kv_sum, up_float.T, precision=highest, preferred_element_type=jnp.float32)
    grad_latent_pre, grad_gain_latent = norm_back(
        grad_latent, normed_latent, scaling_latent, gain_latent
    )
    grad_compressed = jnp.concatenate(
        [grad_latent_pre, rotary_back(rope_sum, cosine, sine_table)], axis=-1
    ).astype(jnp.bfloat16)
    grad_down_kv = jnp.dot(hidden_first.T, grad_compressed, preferred_element_type=jnp.float32)
    grad_query_low = (
        jnp.concatenate(
            [grad_query_rot[..., :QKD], rotary_back(grad_query_rot[..., QKD:], head_cos, head_sin)],
            axis=-1,
        )
        .astype(jnp.bfloat16)
        .reshape(tok_count, HEADS * (QKD + RD))
    )
    grad_query_weight = jnp.dot(hidden_first.T, grad_query_low, preferred_element_type=jnp.float32)
    grad_hidden_first = jnp.dot(
        grad_query_low, query_weight.T, preferred_element_type=jnp.float32
    ) + jnp.dot(grad_compressed, down_weight.T, preferred_element_type=jnp.float32)
    grad_first_norm, grad_gain_first = norm_back(
        grad_hidden_first, normed_first, scaling_first, gain_one
    )
    grad_input = grad_resid + grad_first_norm
    (
        grad_norm_one,
        grad_wq,
        grad_wdkv,
        grad_gkv,
        grad_wukv,
        grad_wo,
        grad_norm_two,
        grad_wr,
        grad_wsi,
        grad_wso,
    ) = (
        lax.psum_scatter(grad_gain_first, BOTH, scatter_dimension=0, tiled=True),
        lax.psum_scatter(grad_query_weight, BOTH, scatter_dimension=0, tiled=True),
        lax.psum_scatter(grad_down_kv, BOTH, scatter_dimension=0, tiled=True),
        lax.psum_scatter(grad_gain_latent, BOTH, scatter_dimension=0, tiled=True),
        lax.psum_scatter(grad_up_kv, BOTH, scatter_dimension=1, tiled=True),
        lax.psum_scatter(grad_attn_out, BOTH, scatter_dimension=1, tiled=True),
        lax.psum_scatter(grad_gain_second, BOTH, scatter_dimension=0, tiled=True),
        lax.psum_scatter(grad_router, BOTH, scatter_dimension=0, tiled=True),
        lax.psum_scatter(grad_shared_in, BOTH, scatter_dimension=0, tiled=True),
        lax.psum_scatter(grad_shared_out, BOTH, scatter_dimension=1, tiled=True),
    )
    return (
        output_low[None],
        grad_input[None],
        grad_norm_one,
        grad_wq,
        grad_wdkv,
        grad_gkv,
        grad_wukv,
        grad_wo,
        grad_norm_two,
        grad_wr,
        grad_wsi,
        grad_wso,
        grad_expert_in[None],
        grad_expert_out[None],
    )


low = lambda v: v.astype(jnp.bfloat16)
wide = lambda v: v.astype(jnp.float32)


def place():
    index = lax.axis_index(CTX)
    return index % 2, index // 2 % 2, index // 4, lax.axis_index(EXP)


def swap(values, bit):
    return lax.ppermute(values, CTX, [(i, i ^ bit) for i in range(8)])


def shift_z(values, step):
    return lax.ppermute(values, EXP, [(i, (i + step) % 4) for i in range(4)])


def entry(values, index, axis):
    return lax.dynamic_index_in_dim(values, index, axis, keepdims=False)


def join(mine, got, bit, axis):
    return jnp.concatenate(
        [jnp.where(bit == 0, mine, got), jnp.where(bit == 0, got, mine)], axis
    )


def gather_z(values):
    z = lax.axis_index(EXP)
    parts = [values] + [shift_z(values, step) for step in (2, 1, 3)]
    order = (0, 2, 1, 3)

    def chunk(j):
        ahead = (z - j) % 4
        out = parts[0]
        for step in (1, 2, 3):
            out = jnp.where(ahead == step, parts[order[step]], out)
        return out

    return jnp.stack([chunk(j) for j in range(4)])


def gather_xy(values, x_first):
    _, x, y, _ = place()
    values = values[None, None]
    if x_first:
        values = join(values, swap(values, 2), x, 1)
        return join(values, swap(values, 4), y, 0)
    values = join(values, swap(values, 4), y, 0)
    return join(values, swap(values, 2), x, 1)


def gather_context(values):
    core = place()[0]
    axis = values.ndim - 2
    cut = values.shape[axis] // 2
    first = lax.slice_in_dim(values, 0, cut, axis=axis)
    second = lax.slice_in_dim(values, cut, 2 * cut, axis=axis)
    both = jnp.concatenate([gather_xy(first, True), gather_xy(second, False)], axis + 2)
    both = both[:, :, None]
    both = join(both, swap(both, 1), core, 2)
    return both.reshape((8,) + values.shape)


def gather_all(values):
    return gather_context(gather_z(values)).reshape((32,) + values.shape)


def gather_small(values):
    core, x, y, _ = place()
    out = gather_z(values)[None]
    out = join(out, swap(out, 1), core, 0)
    out = join(out, swap(out, 2), x, 0)
    out = join(out, swap(out, 4), y, 0)
    return out.reshape((32,) + values.shape)


def halve(values, axis, mine, bit):
    got = swap(entry(values, 1 - mine, axis), bit)
    return low(wide(entry(values, mine, axis)) + wide(got))


def scatter_xy(values):
    core, x, y, _ = place()
    values = values.reshape((2, 2, 2) + values.shape[1:])
    values = halve(values, 2, core, 1)
    axis = values.ndim - 2
    cut = values.shape[axis] // 2
    first = lax.slice_in_dim(values, 0, cut, axis=axis)
    second = lax.slice_in_dim(values, cut, 2 * cut, axis=axis)
    first = halve(halve(first, 1, x, 2), 0, y, 4)
    second = halve(halve(second, 0, y, 4), 0, x, 2)
    return first, second


def scatter_context(values):
    first, second = scatter_xy(values)
    return wide(jnp.concatenate([first, second], 0))


def scatter_z(values):
    z = lax.axis_index(EXP)
    out = wide(entry(values, z, 0))
    for step in (2, 1, 3):
        out = out + wide(shift_z(entry(values, (z + step) % 4, 0), step))
    return out


def scatter_all(values):
    first, second = scatter_xy(values)
    return jnp.concatenate([scatter_z(first), scatter_z(second)], 0)


def fast_body(nc, nz):
    nd = nc * nz
    hc = HEADS // nc
    qw = hc * (QKD + RD)
    ow = hc * VD
    units = SHARED // nd
    pad = -(-units // 128) * 128
    dot = functools.partial(jnp.dot, preferred_element_type=jnp.float32)
    ein = functools.partial(jnp.einsum, preferred_element_type=jnp.float32)

    def body(
        tokens, norm1_gain, w_query, w_down_kv, kv_gain, w_up_kv, w_attn_out, norm2_gain, w_router,
        w_shared_in, w_shared_out, w_expert_in, w_expert_out, routes, slots, blocks, cotangent,
    ):
        device = lax.axis_index(CTX) * nz + lax.axis_index(EXP)
        my_expert = device // 2
        tok = tokens.shape[1]
        width = tokens.shape[2]
        rows = width // nd
        length = tok * nc
        total = tok * nd
        experts = w_router.shape[1]
        cap = tok * TOP // experts * 4 // 3
        scale = (QKD + RD) ** (-0.5)

        small = jnp.concatenate(
            [norm1_gain, norm2_gain, w_router.reshape(-1), kv_gain]
            + [low(v).reshape(-1) for v in (routes, slots, blocks)]
        )
        parts = -(-small.shape[0] // 2048)
        small = jnp.pad(small, (0, 2048 * parts - small.shape[0])).reshape(16 * parts, 128)
        small = gather_small(small).reshape(nd, 2048 * parts)
        gain_one = wide(small[:, :rows].reshape(-1))
        gain_two = wide(small[:, rows : 2 * rows].reshape(-1))
        router = small[:, 2 * rows : 2 * rows + rows * experts].reshape(width, experts)
        begin = 2 * rows + rows * experts
        gain_latent = wide(small[:, begin : begin + LAT // nd].reshape(-1))
        begin += LAT // nd
        route_all = small[:, begin : begin + tok * TOP].reshape(nd, tok, TOP).astype(jnp.int32)
        begin += tok * TOP
        slot_all = small[:, begin : begin + tok * TOP].reshape(nd, tok, TOP).astype(jnp.int32)
        begin += tok * TOP
        block_all = small[:, begin : begin + tok].reshape(nc, nz, tok)
        block_seq = entry(block_all, lax.axis_index(EXP), 1).reshape(-1)
        tok_seq = gather_context(tokens[0]).reshape(length, width)
        down = lax.all_gather(w_down_kv, BOTH, axis=0, tiled=True)
        wq = w_query.reshape(rows, nc, hc, QKD + RD)
        wq = jnp.concatenate(
            [
                wq[..., :QKD].reshape(rows, nc, hc * QKD),
                wq[..., QKD:].reshape(rows, nc, hc * RD),
                w_attn_out.T.reshape(rows, nc, ow),
            ],
            axis=-1,
        ).transpose(1, 0, 2)
        wq = lax.all_to_all(wq, CTX, split_axis=0, concat_axis=0, tiled=True)
        wq = gather_z(wq).transpose(1, 0, 2, 3).reshape(width, qw + ow)
        out_t = wq[:, qw:]
        wq = wq[:, :qw]
        up = gather_z(w_up_kv).transpose(1, 0, 2).reshape(LAT, -1)
        shared = jnp.stack(
            [
                w_shared_in[:, :SHARED].reshape(rows, nd, units),
                w_shared_in[:, SHARED:].reshape(rows, nd, units),
                w_shared_out.T.reshape(rows, nd, units),
            ],
            axis=2,
        )
        shared = jnp.pad(shared, ((0, 0), (0, 0), (0, 0), (0, pad - units)))
        shared = shared.transpose(1, 0, 2, 3).reshape(nd, rows, 3 * pad)
        shared = lax.all_to_all(shared, BOTH, split_axis=0, concat_axis=0, tiled=True)
        shared = shared.reshape(width, 3 * pad)
        shared_in = shared[:, : 2 * pad]
        shared_out_t = shared[:, 2 * pad :]
        cot_all = lax.all_gather(cotangent[0], BOTH, axis=0, tiled=True)

        cosine, sine = rotation_table(jnp.arange(length, dtype=jnp.float32))
        head_cos, head_sin = cosine[:, None, :], sine[:, None, :]
        normed_seq, _ = normalize(wide(tok_seq))
        hidden_seq = low(normed_seq * gain_one)
        query = dot(hidden_seq, wq)
        q_nope = low(query[:, : hc * QKD]).reshape(length, hc, QKD)
        q_rope = low(rotary(query[:, hc * QKD :].reshape(length, hc, RD), head_cos, head_sin))
        compressed = dot(hidden_seq, down)
        normed_latent, scaling_latent = normalize(compressed[:, :LAT])
        latent = low(normed_latent * gain_latent)
        rope_key = low(rotary(compressed[:, LAT:], cosine, sine))
        key_value = low(dot(latent, up)).reshape(length, hc, QKD + VD)
        key, value = key_value[..., :QKD], key_value[..., QKD:]
        raw = ein("thd,nhd->htn", q_nope, key) + ein("thr,nr->htn", q_rope, rope_key)
        self_raw = jnp.sum(wide(q_nope) * wide(key), axis=-1) + jnp.sum(
            wide(q_rope) * wide(rope_key)[:, None, :], axis=-1
        )
        shift = jnp.floor(self_raw * scale).T
        allowed = (block_seq[None, :] <= block_seq[:, None])[None]
        weights = jnp.where(
            allowed, jnp.exp(jnp.where(allowed, raw * scale - shift[:, :, None], 0.0)), 0.0
        )
        weights_low = low(weights)
        denominator = jnp.sum(weights, axis=-1)
        denom_rows = denominator.T[:, :, None]
        attended = ein("htn,nhv->thv", weights_low, value) / denom_rows
        mixed = low(attended.reshape(length, ow))
        resid_part = low(lax.dot_general(mixed, out_t, (((1,), (1,)), ((), ())),
                                         preferred_element_type=jnp.float32))
        resid = wide(tokens[0]) + scatter_context(resid_part.reshape(nc, tok, width))

        normed_second, scaling_second = normalize(resid)
        hidden = low(normed_second * gain_two)
        logits = dot(hidden, router)
        onehot = wide(routes[0][:, :, None] == jnp.arange(experts)[None, None, :])
        gates = jax.nn.softmax(jnp.sum(onehot * logits[:, None, :], axis=-1), axis=-1)
        gates_dense = jnp.sum(onehot * gates[:, :, None], axis=1)
        hidden_all = lax.all_gather(hidden, BOTH, axis=0, tiled=True)

        named = route_all == my_expert
        slot_of = jnp.max(jnp.where(named, slot_all, -1), axis=-1)
        pick = slot_of[:, None, :] == jnp.arange(cap)[None, :, None]
        pick_low = low(pick)
        logits_all = dot(hidden_all, router)
        chosen = jnp.max(
            wide(route_all.reshape(total, TOP, 1) == jnp.arange(experts)[None, None, :]), axis=1
        )
        gates_all = jax.nn.softmax(jnp.where(chosen > 0, logits_all, -jnp.inf), axis=-1)
        gate_col = jnp.sum(
            jnp.where(jnp.arange(experts)[None, :] == my_expert, gates_all, 0.0), axis=1
        ).reshape(nd, 1, tok)
        gate_rows = jnp.sum(jnp.where(pick, gate_col, 0.0), axis=-1).reshape(nd * cap, 1)
        take = lambda table: low(ein("bst,btd->bsd", pick_low, table.reshape(nd, tok, width))).reshape(
            nd * cap, width
        )
        give = lambda table: ein("bst,bsd->btd", pick_low, table.reshape(nd, cap, width)).reshape(
            total, width
        )
        expert_in, expert_out = w_expert_in[0], w_expert_out[0]
        picked = take(hidden_all)
        pre = dot(picked, expert_in)
        expert_gate, expert_up = pre[:, :HALF], pre[:, HALF:]
        expert_silu = jax.nn.silu(expert_gate)
        act = low(expert_silu * expert_up)
        part = wide(low(dot(act, expert_out)))
        shared_pre = dot(hidden_all, shared_in)
        shared_gate, shared_up = shared_pre[:, :pad], shared_pre[:, pad:]
        shared_silu = jax.nn.silu(shared_gate)
        shared_act = low(shared_silu * shared_up)
        result = give(low(part * gate_rows)) + lax.dot_general(
            shared_act, shared_out_t, (((1,), (1,)), ((), ())), preferred_element_type=jnp.float32
        )
        output = low(
            resid
            + scatter_all(low(result).reshape(nc, nz, tok, width))
        )

        cot_rows = wide(take(cot_all))
        dots = jnp.sum(cot_rows * part, axis=-1).reshape(nd, cap, 1)
        dots = jnp.sum(jnp.where(pick, dots, 0.0), axis=1)
        dots = lax.all_to_all(dots, BOTH, split_axis=0, concat_axis=0, tiled=True)
        grad_gates = dots.reshape(experts, nd // experts, tok).sum(axis=1).T
        grad_logits = low(
            gates_dense
            * (grad_gates - jnp.sum(gates_dense * grad_gates, axis=-1, keepdims=True))
        )
        grad_part = low(cot_rows * gate_rows)
        grad_act = lax.dot_general(
            grad_part, expert_out, (((1,), (1,)), ((), ())), preferred_element_type=jnp.float32
        )
        grad_pre = low(
            jnp.concatenate(
                [silu_back(expert_gate, grad_act * expert_up), grad_act * expert_silu], axis=-1
            )
        )
        grad_expert_out = dot(act.T, grad_part)
        grad_expert_in = dot(picked.T, grad_pre)
        grad_rows = low(
            lax.dot_general(
                grad_pre, expert_in, (((1,), (1,)), ((), ())), preferred_element_type=jnp.float32
            )
        )
        grad_shared_act = dot(cot_all, shared_out_t)
        grad_shared_pre = low(
            jnp.concatenate(
                [silu_back(shared_gate, grad_shared_act * shared_up), grad_shared_act * shared_silu],
                axis=-1,
            )
        )
        grad_shared = jnp.concatenate(
            [dot(hidden_all.T, grad_shared_pre), dot(cot_all.T, shared_act)], axis=-1
        )
        grad_hidden_part = give(grad_rows) + lax.dot_general(
            grad_shared_pre, shared_in, (((1,), (1,)), ((), ())), preferred_element_type=jnp.float32
        )
        grad_hidden = scatter_all(
            low(grad_hidden_part).reshape(nc, nz, tok, width)
        ) + dot(grad_logits, router.T)
        grad_mid, grad_gain_two = norm_back(grad_hidden, normed_second, scaling_second, gain_two)
        grad_resid = wide(cotangent[0]) + grad_mid
        grad_router = dot(hidden.T, grad_logits)

        grad_resid_seq = gather_context(low(grad_resid)).reshape(length, width)
        grad_mixed = dot(grad_resid_seq, out_t).reshape(length, hc, VD)
        grad_out_t = dot(grad_resid_seq.T, mixed)
        scaled = low(grad_mixed / denom_rows)
        correction = (jnp.sum(grad_mixed * attended, axis=-1) / denominator.T).T
        grad_weights = ein("thv,nhv->htn", scaled, value)
        grad_raw = low(weights * (grad_weights - correction[:, :, None]) * scale)
        grad_nope = ein("htn,nhd->thd", grad_raw, key)
        grad_rot = ein("htn,nr->thr", grad_raw, rope_key)
        grad_key = ein("htn,thd->nhd", grad_raw, q_nope)
        grad_value = ein("htn,thv->nhv", weights_low, scaled)
        grad_rope = ein("htn,thr->nr", grad_raw, q_rope)
        grad_kv = low(jnp.concatenate([grad_key, grad_value], axis=-1).reshape(length, hc * (QKD + VD)))
        grad_up = dot(latent.T, grad_kv)
        grad_latent = lax.dot_general(
            grad_kv, up, (((1,), (1,)), ((), ())), preferred_element_type=jnp.float32
        )
        grad_latent_pre, grad_gain_latent = norm_back(
            grad_latent, normed_latent, scaling_latent, gain_latent
        )
        grad_compressed = low(
            jnp.concatenate([grad_latent_pre, rotary_back(grad_rope, cosine, sine)], axis=-1)
        )
        grad_query = low(
            jnp.concatenate(
                [
                    grad_nope.reshape(length, hc * QKD),
                    rotary_back(grad_rot, head_cos, head_sin).reshape(length, hc * RD),
                ],
                axis=-1,
            )
        )
        grad_attn = jnp.concatenate([dot(hidden_seq.T, grad_query), grad_out_t], axis=-1)
        grad_down = dot(hidden_seq.T, grad_compressed)
        grad_first_part = low(
            lax.dot_general(
                grad_query, wq, (((1,), (1,)), ((), ())), preferred_element_type=jnp.float32
            )
            + lax.dot_general(
                grad_compressed, down, (((1,), (1,)), ((), ())), preferred_element_type=jnp.float32
            )
        )
        grad_first = scatter_context(grad_first_part.reshape(nc, tok, width))
        normed_first, scaling_first = normalize(wide(tokens[0]))
        grad_input, grad_gain_one = norm_back(grad_first, normed_first, scaling_first, gain_one)
        grad_input = grad_input + grad_resid

        exchange = lambda table: lax.all_to_all(
            low(table).reshape(nd, rows, table.shape[-1]), BOTH, split_axis=0, concat_axis=0, tiled=True
        )
        shared_back = exchange(grad_shared).reshape(nd, rows, 3, pad)[..., :units]
        grad_wsi = wide(shared_back[:, :, :2].transpose(1, 2, 0, 3)).reshape(rows, 2 * SHARED)
        grad_wso = wide(shared_back[:, :, 2].transpose(0, 2, 1)).reshape(SHARED, rows)
        attn_back = wide(exchange(grad_attn)).reshape(nc, nz, rows, qw + ow).sum(axis=1)
        grad_wq = jnp.concatenate(
            [
                attn_back[:, :, : hc * QKD].reshape(nc, rows, hc, QKD),
                attn_back[:, :, hc * QKD : qw].reshape(nc, rows, hc, RD),
            ],
            axis=-1,
        ).transpose(1, 0, 2, 3).reshape(rows, HEADS * (QKD + RD))
        grad_wo = attn_back[:, :, qw:].transpose(0, 2, 1).reshape(HEADS * VD, rows)
        grad_wdkv = wide(exchange(grad_down)).sum(axis=0)
        grad_wukv = wide(
            lax.psum_scatter(low(grad_up), EXP, scatter_dimension=1, tiled=True)
        )
        tiny = jnp.concatenate(
            [
                grad_gain_one.reshape(nd, rows),
                grad_gain_two.reshape(nd, rows),
                grad_router.reshape(nd, rows * experts),
                grad_gain_latent.reshape(nd, LAT // nd),
            ],
            axis=1,
        )
        tiny = lax.all_to_all(tiny, BOTH, split_axis=0, concat_axis=0, tiled=True).sum(axis=0)
        return (
            output[None],
            grad_input[None],
            tiny[:rows],
            grad_wq,
            grad_wdkv,
            tiny[2 * rows + rows * experts :],
            grad_wukv,
            grad_wo,
            tiny[rows : 2 * rows],
            tiny[2 * rows : 2 * rows + rows * experts].reshape(rows, experts),
            grad_wsi,
            grad_wso,
            grad_expert_in[None],
            grad_expert_out[None],
        )

    return body


def solution(mesh):
    placed = (
        P(EXP, CTX, None),
        P(BOTH),
        P(BOTH, None),
        P(BOTH, None),
        P(BOTH),
        P(None, BOTH),
        P(None, BOTH),
        P(BOTH),
        P(BOTH, None),
        P(BOTH, None),
        P(None, BOTH),
        P(BOTH, None, None),
        P(BOTH, None, None),
        P(EXP, CTX, None),
        P(EXP, CTX, None),
        P(EXP, CTX),
        P(EXP, CTX, None),
    )
    nc, nz = mesh.shape[CTX], mesh.shape[EXP]
    split = nc == 8 and nz == 4
    return jax.shard_map(
        fast_body(nc, nz) if split else body,
        mesh=mesh,
        in_specs=placed,
        out_specs=(
            P(EXP, CTX, None),
            P(EXP, CTX, None),
            P(BOTH),
            P(BOTH, None),
            P(BOTH, None),
            P(BOTH),
            P(None, BOTH),
            P(None, BOTH),
            P(BOTH),
            P(BOTH, None),
            P(BOTH, None),
            P(None, BOTH),
            P(BOTH, None, None),
            P(BOTH, None, None),
        ),
        check_vma=False,
    )
```

```python
import functools
import math

import jax
import jax.numpy as jnp
from jax import lax
from jax.sharding import PartitionSpec as P

HEADS = 16
QKD = 128
RD = 64
VD = 128
LAT = 512
TOP = 6
SHARED = 2816
HALF = 704
CTX = "context"
EXP = "expert"
BOTH = (CTX, EXP)


epsilon = 1e-06
highest = lax.Precision.HIGHEST


def normalize(values):
    scaling = lax.rsqrt(jnp.mean(values * values, axis=-1, keepdims=True) + epsilon)
    return (values * scaling, scaling)


def norm_back(grad_normed, normed, scaling, gain):
    grad_gain = jnp.sum(grad_normed * normed, axis=0)
    grad_unit = grad_normed * gain
    grad_values = scaling * (
        grad_unit - normed * jnp.mean(grad_unit * normed, axis=-1, keepdims=True)
    )
    return (grad_values, grad_gain)


def rotary(values, cosine, sine_table):
    middle = values.shape[-1] // 2
    first_half = values[..., :middle]
    second_half = values[..., middle:]
    return jnp.concatenate(
        [
            first_half * cosine - second_half * sine_table,
            second_half * cosine + first_half * sine_table,
        ],
        axis=-1,
    )


def rotary_back(grads_in, cosine, sine_table):
    middle = grads_in.shape[-1] // 2
    first_half = grads_in[..., :middle]
    second_half = grads_in[..., middle:]
    return jnp.concatenate(
        [
            first_half * cosine + second_half * sine_table,
            second_half * cosine - first_half * sine_table,
        ],
        axis=-1,
    )


def rotation_table(positions):
    exponent = jnp.arange(RD // 2, dtype=jnp.float32) * (2.0 / RD)
    angle_table = positions[:, None] * (10000.0 ** (-exponent))[None, :]
    return (jnp.cos(angle_table), jnp.sin(angle_table))


def silu_back(value, grads_in):
    sigma_value = jax.nn.sigmoid(value)
    return grads_in * sigma_value * (1.0 + value * (1.0 - sigma_value))


def head_scores(query_low, key_low, rope_low):
    nope_part = jnp.einsum(
        "thd,nhd->htn", query_low[..., :QKD], key_low, preferred_element_type=jnp.float32
    )
    rope_part = jnp.einsum(
        "thr,nr->htn", query_low[..., QKD:], rope_low, preferred_element_type=jnp.float32
    )
    return nope_part + rope_part


def both_halves(buffer_rows, experts_total, capacity):
    width = buffer_rows.shape[-1]
    shaped = buffer_rows.reshape(experts_total, 1, capacity, width)
    return jnp.broadcast_to(shaped, (experts_total, 2, capacity, width)).reshape(
        2 * experts_total, capacity, width
    )


def halves_sum(received, experts_total, capacity):
    width = received.shape[-1]
    return (
        received.astype(jnp.float32)
        .reshape(experts_total, 2, capacity, width)
        .sum(axis=1)
        .reshape(experts_total * capacity, width)
    )


def body(
    tokens,
    norm1_gain,
    w_query,
    w_down_kv,
    kv_gain,
    w_up_kv,
    w_attn_out,
    norm2_gain,
    w_router,
    w_shared_in,
    w_shared_out,
    w_expert_in,
    w_expert_out,
    routes,
    slots,
    blocks,
    cotangent,
):
    (
        gain_first,
        query_weight,
        down_weight,
        latent_gain,
        up_weight,
        out_weight,
        gain_second,
        router_weight,
        shared_in_weight,
        shared_out_weight,
    ) = (
        lax.all_gather(norm1_gain, BOTH, axis=0, tiled=True),
        lax.all_gather(w_query, BOTH, axis=0, tiled=True),
        lax.all_gather(w_down_kv, BOTH, axis=0, tiled=True),
        lax.all_gather(kv_gain, BOTH, axis=0, tiled=True),
        lax.all_gather(w_up_kv, BOTH, axis=1, tiled=True),
        lax.all_gather(w_attn_out, BOTH, axis=1, tiled=True),
        lax.all_gather(norm2_gain, BOTH, axis=0, tiled=True),
        lax.all_gather(w_router, BOTH, axis=0, tiled=True),
        lax.all_gather(w_shared_in, BOTH, axis=0, tiled=True),
        lax.all_gather(w_shared_out, BOTH, axis=1, tiled=True),
    )
    tok_count = tokens.shape[1]
    length_all = tok_count * lax.axis_size(CTX)
    experts_total = router_weight.shape[1]
    capacity = tok_count * TOP // experts_total * 4 // 3
    score_scale = (QKD + RD) ** (-0.5)
    residual_in = tokens[0].astype(jnp.float32)
    own_blocks = blocks[0]
    route_ids = routes[0]
    slot_ids = slots[0]
    positions = (lax.axis_index(CTX) * tok_count + jnp.arange(tok_count)).astype(jnp.float32)
    cosine, sine_table = rotation_table(positions)
    head_cos = cosine[:, None, :]
    head_sin = sine_table[:, None, :]
    gain_one = gain_first.astype(jnp.float32)
    gain_two = gain_second.astype(jnp.float32)
    gain_latent = latent_gain.astype(jnp.float32)
    normed_first, scaling_first = normalize(residual_in)
    hidden_first = (normed_first * gain_one).astype(jnp.bfloat16)
    query_pre = jnp.dot(hidden_first, query_weight, preferred_element_type=jnp.float32).reshape(
        tok_count, HEADS, QKD + RD
    )
    query_low = jnp.concatenate(
        [query_pre[..., :QKD], rotary(query_pre[..., QKD:], head_cos, head_sin)], axis=-1
    ).astype(jnp.bfloat16)
    compressed = jnp.dot(hidden_first, down_weight, preferred_element_type=jnp.float32)
    normed_latent, scaling_latent = normalize(compressed[:, :LAT])
    latent_low = (normed_latent * gain_latent).astype(jnp.bfloat16)
    rope_low = rotary(compressed[:, LAT:], cosine, sine_table).astype(jnp.bfloat16)
    key_value = jnp.dot(latent_low, up_weight, preferred_element_type=jnp.float32).astype(
        jnp.bfloat16
    )
    own_heads = key_value.reshape(tok_count, HEADS, QKD + VD)
    self_raw = jnp.einsum(
        "thd,thd->ht",
        query_low[..., :QKD],
        own_heads[..., :QKD],
        preferred_element_type=jnp.float32,
    ) + jnp.einsum("thr,tr->ht", query_low[..., QKD:], rope_low, preferred_element_type=jnp.float32)
    shift_table = jnp.floor(self_raw * score_scale)
    last_block = jnp.max(own_blocks)

    def block_weights(kv_piece, rope_piece, blocks_piece):
        kv_heads = kv_piece.reshape(kv_piece.shape[0], HEADS, QKD + VD)
        raw_scores = head_scores(query_low, kv_heads[..., :QKD], rope_piece)
        allowed = (blocks_piece[None, :] <= own_blocks[:, None])[None]
        shifted = jnp.where(allowed, raw_scores * score_scale - shift_table[:, :, None], 0.0)
        return (kv_heads, jnp.where(allowed, jnp.exp(shifted), 0.0))

    empty_state = (
        jnp.zeros((tok_count, HEADS, VD), jnp.float32),
        jnp.zeros((HEADS, tok_count), jnp.float32),
    )
    kv_piece = lax.all_gather(key_value, CTX, axis=0, tiled=True)
    rope_piece = lax.all_gather(rope_low, CTX, axis=0, tiled=True)
    blocks_piece = lax.all_gather(own_blocks, CTX, axis=0, tiled=True)
    make_kv = lambda: kv_piece

    def attend_compute(state_now):
        kv_heads, weights = block_weights(make_kv(), rope_piece, blocks_piece)
        running = jnp.einsum(
            "htn,nhv->thv",
            weights.astype(jnp.bfloat16),
            kv_heads[..., QKD:],
            preferred_element_type=jnp.float32,
        )
        return (running, jnp.sum(weights, axis=-1))

    running, denominator = lax.cond(
        jnp.min(blocks_piece) > last_block, lambda state_now: state_now, attend_compute, empty_state
    )
    denom_rows = jnp.transpose(denominator)
    attended = running / denom_rows[:, :, None]
    mixed_low = attended.reshape(tok_count, HEADS * VD).astype(jnp.bfloat16)
    residual_mid = residual_in + jnp.dot(mixed_low, out_weight, preferred_element_type=jnp.float32)
    normed_second, scaling_second = normalize(residual_mid)
    hidden_second = (normed_second * gain_two).astype(jnp.bfloat16)
    logits = jnp.dot(hidden_second, router_weight, preferred_element_type=jnp.float32)
    route_onehot = (route_ids[:, :, None] == jnp.arange(experts_total)[None, None, :]).astype(
        jnp.float32
    )
    chosen = jnp.sum(route_onehot * logits[:, None, :], axis=-1)
    gate_weights = jax.nn.softmax(chosen, axis=-1)
    shared_pre = jnp.dot(hidden_second, shared_in_weight, preferred_element_type=jnp.float32)
    shared_act = (jax.nn.silu(shared_pre[:, :SHARED]) * shared_pre[:, SHARED:]).astype(jnp.bfloat16)
    shared_result = jnp.dot(shared_act, shared_out_weight, preferred_element_type=jnp.float32)
    slot_index = (route_ids * capacity + slot_ids).reshape(-1)
    model_width = hidden_second.shape[1]
    repeated = jnp.broadcast_to(hidden_second[:, None, :], (tok_count, TOP, model_width)).reshape(
        tok_count * TOP, model_width
    )
    send_rows = (
        jnp.zeros((experts_total * capacity, model_width), jnp.bfloat16)
        .at[slot_index]
        .set(repeated)
    )
    weight_in_local = w_expert_in[0]
    weight_out_local = w_expert_out[0]
    received = lax.all_to_all(
        both_halves(send_rows, experts_total, capacity),
        BOTH,
        split_axis=0,
        concat_axis=0,
        tiled=True,
    )
    pre_expert = jnp.einsum(
        "scd,df->scf", received, weight_in_local, preferred_element_type=jnp.float32
    )
    activation = (jax.nn.silu(pre_expert[..., :HALF]) * pre_expert[..., HALF:]).astype(jnp.bfloat16)
    part_rows = jnp.einsum(
        "scf,fd->scd", activation, weight_out_local, preferred_element_type=jnp.float32
    ).astype(jnp.bfloat16)
    returned = lax.all_to_all(
        part_rows, BOTH, split_axis=0, concat_axis=0, tiled=True
    )
    returned, received_rows, pre_expert = (returned, received, pre_expert)
    expert_table = halves_sum(returned, experts_total, capacity)
    picked = expert_table[slot_index].reshape(tok_count, TOP, model_width)
    routed = jnp.sum(gate_weights[:, :, None] * picked, axis=1)
    output_low = (residual_mid + shared_result + routed).astype(jnp.bfloat16)
    grad_low = cotangent[0]
    grad_out = grad_low.astype(jnp.float32)
    grad_shared_out = jnp.dot(shared_act.T, grad_low, preferred_element_type=jnp.float32)
    grad_shared_act = jnp.dot(grad_low, shared_out_weight.T, preferred_element_type=jnp.float32)
    shared_gate = shared_pre[:, :SHARED]
    shared_up = shared_pre[:, SHARED:]
    grad_shared_pre = jnp.concatenate(
        [
            silu_back(shared_gate, grad_shared_act * shared_up),
            grad_shared_act * jax.nn.silu(shared_gate),
        ],
        axis=-1,
    ).astype(jnp.bfloat16)
    grad_shared_in = jnp.dot(hidden_second.T, grad_shared_pre, preferred_element_type=jnp.float32)
    grad_hidden = jnp.dot(grad_shared_pre, shared_in_weight.T, preferred_element_type=jnp.float32)
    grad_gates = jnp.sum(grad_out[:, None, :] * picked, axis=-1)
    grad_chosen = gate_weights * (
        grad_gates - jnp.sum(gate_weights * grad_gates, axis=-1, keepdims=True)
    )
    grad_logits = jnp.sum(route_onehot * grad_chosen[:, :, None], axis=1).astype(jnp.bfloat16)
    grad_router = jnp.dot(hidden_second.T, grad_logits, preferred_element_type=jnp.float32)
    grad_hidden = grad_hidden + jnp.dot(
        grad_logits, router_weight.T, preferred_element_type=jnp.float32
    )
    grad_parts = (
        (gate_weights[:, :, None] * grad_out[:, None, :])
        .astype(jnp.bfloat16)
        .reshape(tok_count * TOP, model_width)
    )
    grad_send = (
        jnp.zeros((experts_total * capacity, model_width), jnp.bfloat16)
        .at[slot_index]
        .set(grad_parts)
    )
    grad_received = lax.all_to_all(
        both_halves(grad_send, experts_total, capacity),
        BOTH,
        split_axis=0,
        concat_axis=0,
        tiled=True,
    )
    expert_gate = pre_expert[..., :HALF]
    expert_up = pre_expert[..., HALF:]
    expert_silu = jax.nn.silu(expert_gate)
    expert_act = (expert_silu * expert_up).astype(jnp.bfloat16)
    grad_expert_out = jnp.einsum(
        "scf,scd->fd", expert_act, grad_received, preferred_element_type=jnp.float32
    )
    grad_expert_act = jnp.einsum(
        "scd,fd->scf", grad_received, weight_out_local, preferred_element_type=jnp.float32
    )
    grad_expert_pre = jnp.concatenate(
        [silu_back(expert_gate, grad_expert_act * expert_up), grad_expert_act * expert_silu],
        axis=-1,
    ).astype(jnp.bfloat16)
    grad_expert_in = jnp.einsum(
        "scd,scf->df", received_rows, grad_expert_pre, preferred_element_type=jnp.float32
    )
    grad_rows = jnp.einsum(
        "scf,df->scd", grad_expert_pre, weight_in_local, preferred_element_type=jnp.float32
    )
    grad_back = lax.all_to_all(
        grad_rows.astype(jnp.bfloat16),
        BOTH,
        split_axis=0,
        concat_axis=0,
        tiled=True,
    ).astype(grad_rows.dtype)
    grad_table = halves_sum(grad_back, experts_total, capacity)
    grad_hidden = grad_hidden + jnp.sum(
        grad_table[slot_index].reshape(tok_count, TOP, model_width), axis=1
    )
    grad_mid_norm, grad_gain_second = norm_back(
        grad_hidden, normed_second, scaling_second, gain_two
    )
    grad_resid = grad_out + grad_mid_norm
    grad_resid_low = grad_resid.astype(jnp.bfloat16)
    grad_attn_out = jnp.dot(mixed_low.T, grad_resid_low, preferred_element_type=jnp.float32)
    grad_mixed = jnp.dot(grad_resid_low, out_weight.T, preferred_element_type=jnp.float32).reshape(
        tok_count, HEADS, VD
    )
    scaled_low = (grad_mixed / denom_rows[:, :, None]).astype(jnp.bfloat16)
    correction = jnp.transpose(jnp.sum(grad_mixed * attended, axis=-1) / denom_rows)
    full_kv, full_rope, full_blocks, full_latent = (
        lax.all_gather(key_value, CTX, axis=0, tiled=True),
        lax.all_gather(rope_low, CTX, axis=0, tiled=True),
        lax.all_gather(own_blocks, CTX, axis=0, tiled=True),
        lax.all_gather(latent_low, CTX, axis=0, tiled=True),
    )
    key_block = math.gcd(length_all, 512)
    block_count = length_all // key_block
    kv_width = HEADS * (QKD + VD)

    def key_step(grad_query, block_index):
        begin_row = block_index * key_block
        kv_piece = lax.dynamic_slice_in_dim(full_kv, begin_row, key_block, 0)
        rope_piece = lax.dynamic_slice_in_dim(full_rope, begin_row, key_block, 0)
        blocks_piece = lax.dynamic_slice_in_dim(full_blocks, begin_row, key_block, 0)

        def key_compute(grad_acc):
            kv_heads, weights = block_weights(kv_piece, rope_piece, blocks_piece)
            grad_weights = jnp.einsum(
                "thv,nhv->htn", scaled_low, kv_heads[..., QKD:], preferred_element_type=jnp.float32
            )
            grad_raw = (weights * (grad_weights - correction[:, :, None]) * score_scale).astype(
                jnp.bfloat16
            )
            grad_nope = jnp.einsum(
                "htn,nhd->thd", grad_raw, kv_heads[..., :QKD], preferred_element_type=jnp.float32
            )
            grad_rot = jnp.einsum(
                "htn,nr->thr", grad_raw, rope_piece, preferred_element_type=jnp.float32
            )
            grad_key = jnp.einsum(
                "htn,thd->nhd", grad_raw, query_low[..., :QKD], preferred_element_type=jnp.float32
            )
            grad_value = jnp.einsum(
                "htn,thv->nhv",
                weights.astype(jnp.bfloat16),
                scaled_low,
                preferred_element_type=jnp.float32,
            )
            grad_rope = jnp.einsum(
                "htn,thr->nr", grad_raw, query_low[..., QKD:], preferred_element_type=jnp.float32
            )
            grad_kv = jnp.concatenate([grad_key, grad_value], axis=-1).reshape(key_block, kv_width)
            return (grad_acc + jnp.concatenate([grad_nope, grad_rot], axis=-1), grad_kv, grad_rope)

        def skipped(grad_acc):
            return (
                grad_acc,
                jnp.zeros((key_block, kv_width), jnp.float32),
                jnp.zeros((key_block, RD), jnp.float32),
            )

        grad_query, grad_kv, grad_rope = lax.cond(
            jnp.min(blocks_piece) > last_block, skipped, key_compute, grad_query
        )
        return (grad_query, (grad_kv, grad_rope))

    grad_query_rot, (grad_kv_blocks, grad_rope_blocks) = lax.scan(
        key_step, jnp.zeros((tok_count, HEADS, QKD + RD), jnp.float32), jnp.arange(block_count)
    )
    partial_kv = grad_kv_blocks.reshape(length_all, kv_width)
    partial_rope = grad_rope_blocks.reshape(length_all, RD)
    up_float = up_weight.astype(jnp.float32)
    kv_sum, rope_sum = (
        lax.psum_scatter(
            partial_kv.astype(jnp.bfloat16), CTX, scatter_dimension=0, tiled=True
        ).astype(jnp.float32),
        lax.psum_scatter(
            partial_rope.astype(jnp.bfloat16), CTX, scatter_dimension=0, tiled=True
        ).astype(jnp.float32),
    )
    grad_up_kv = jnp.dot(
        latent_low.astype(jnp.float32).T,
        kv_sum,
        precision=highest,
        preferred_element_type=jnp.float32,
    )
    grad_latent = jnp.dot(kv_sum, up_float.T, precision=highest, preferred_element_type=jnp.float32)
    grad_latent_pre, grad_gain_latent = norm_back(
        grad_latent, normed_latent, scaling_latent, gain_latent
    )
    grad_compressed = jnp.concatenate(
        [grad_latent_pre, rotary_back(rope_sum, cosine, sine_table)], axis=-1
    ).astype(jnp.bfloat16)
    grad_down_kv = jnp.dot(hidden_first.T, grad_compressed, preferred_element_type=jnp.float32)
    grad_query_low = (
        jnp.concatenate(
            [grad_query_rot[..., :QKD], rotary_back(grad_query_rot[..., QKD:], head_cos, head_sin)],
            axis=-1,
        )
        .astype(jnp.bfloat16)
        .reshape(tok_count, HEADS * (QKD + RD))
    )
    grad_query_weight = jnp.dot(hidden_first.T, grad_query_low, preferred_element_type=jnp.float32)
    grad_hidden_first = jnp.dot(
        grad_query_low, query_weight.T, preferred_element_type=jnp.float32
    ) + jnp.dot(grad_compressed, down_weight.T, preferred_element_type=jnp.float32)
    grad_first_norm, grad_gain_first = norm_back(
        grad_hidden_first, normed_first, scaling_first, gain_one
    )
    grad_input = grad_resid + grad_first_norm
    (
        grad_norm_one,
        grad_wq,
        grad_wdkv,
        grad_gkv,
        grad_wukv,
        grad_wo,
        grad_norm_two,
        grad_wr,
        grad_wsi,
        grad_wso,
    ) = (
        lax.psum_scatter(grad_gain_first, BOTH, scatter_dimension=0, tiled=True),
        lax.psum_scatter(grad_query_weight, BOTH, scatter_dimension=0, tiled=True),
        lax.psum_scatter(grad_down_kv, BOTH, scatter_dimension=0, tiled=True),
        lax.psum_scatter(grad_gain_latent, BOTH, scatter_dimension=0, tiled=True),
        lax.psum_scatter(grad_up_kv, BOTH, scatter_dimension=1, tiled=True),
        lax.psum_scatter(grad_attn_out, BOTH, scatter_dimension=1, tiled=True),
        lax.psum_scatter(grad_gain_second, BOTH, scatter_dimension=0, tiled=True),
        lax.psum_scatter(grad_router, BOTH, scatter_dimension=0, tiled=True),
        lax.psum_scatter(grad_shared_in, BOTH, scatter_dimension=0, tiled=True),
        lax.psum_scatter(grad_shared_out, BOTH, scatter_dimension=1, tiled=True),
    )
    return (
        output_low[None],
        grad_input[None],
        grad_norm_one,
        grad_wq,
        grad_wdkv,
        grad_gkv,
        grad_wukv,
        grad_wo,
        grad_norm_two,
        grad_wr,
        grad_wsi,
        grad_wso,
        grad_expert_in[None],
        grad_expert_out[None],
    )


low = lambda v: v.astype(jnp.bfloat16)
wide = lambda v: v.astype(jnp.float32)


def place():
    index = lax.axis_index(CTX)
    return index % 2, index // 2 % 2, index // 4, lax.axis_index(EXP)


def swap(values, bit):
    return lax.ppermute(values, CTX, [(i, i ^ bit) for i in range(8)])


def shift_z(values, step):
    return lax.ppermute(values, EXP, [(i, (i + step) % 4) for i in range(4)])


def entry(values, index, axis):
    return lax.dynamic_index_in_dim(values, index, axis, keepdims=False)


def join(mine, got, bit, axis):
    return jnp.concatenate(
        [jnp.where(bit == 0, mine, got), jnp.where(bit == 0, got, mine)], axis
    )


def gather_z(values):
    z = lax.axis_index(EXP)
    parts = [values] + [shift_z(values, step) for step in (2, 1, 3)]
    order = (0, 2, 1, 3)

    def chunk(j):
        ahead = (z - j) % 4
        out = parts[0]
        for step in (1, 2, 3):
            out = jnp.where(ahead == step, parts[order[step]], out)
        return out

    return jnp.stack([chunk(j) for j in range(4)])


def gather_xy(values, x_first):
    _, x, y, _ = place()
    values = values[None, None]
    if x_first:
        values = join(values, swap(values, 2), x, 1)
        return join(values, swap(values, 4), y, 0)
    values = join(values, swap(values, 4), y, 0)
    return join(values, swap(values, 2), x, 1)


def gather_context(values):
    core = place()[0]
    axis = values.ndim - 2
    cut = values.shape[axis] // 2
    first = lax.slice_in_dim(values, 0, cut, axis=axis)
    second = lax.slice_in_dim(values, cut, 2 * cut, axis=axis)
    both = jnp.concatenate([gather_xy(first, True), gather_xy(second, False)], axis + 2)
    both = both[:, :, None]
    both = join(both, swap(both, 1), core, 2)
    return both.reshape((8,) + values.shape)


def gather_all(values):
    return gather_context(gather_z(values)).reshape((32,) + values.shape)


def gather_small(values):
    core, x, y, _ = place()
    out = gather_z(values)[None]
    out = join(out, swap(out, 1), core, 0)
    out = join(out, swap(out, 2), x, 0)
    out = join(out, swap(out, 4), y, 0)
    return out.reshape((32,) + values.shape)


def halve(values, axis, mine, bit):
    got = swap(entry(values, 1 - mine, axis), bit)
    return low(wide(entry(values, mine, axis)) + wide(got))


def scatter_core(values):
    return halve(values.reshape((2, 2, 2) + values.shape[1:]), 2, place()[0], 1)


def scatter_one(values):
    _, x, y, _ = place()
    axis = values.ndim - 2
    cut = values.shape[axis] // 2
    first = lax.slice_in_dim(values, 0, cut, axis=axis)
    second = lax.slice_in_dim(values, cut, 2 * cut, axis=axis)
    return halve(first, 1, x, 2), halve(second, 0, y, 4)


def scatter_two(pair):
    _, x, y, _ = place()
    pair = (halve(pair[0], 0, y, 4), halve(pair[1], 0, x, 2))
    return jnp.concatenate(pair, pair[0].ndim - 2)


def scatter_context(values):
    return wide(scatter_two(scatter_one(scatter_core(values))))


def scatter_z(values):
    z = lax.axis_index(EXP)
    out = wide(entry(values, z, 0))
    for step in (2, 1, 3):
        out = out + wide(shift_z(entry(values, (z + step) % 4, 0), step))
    return out


tie = lax.optimization_barrier


def fast_body(nc, nz):
    nd = nc * nz
    hc = HEADS // nc
    qw = hc * (QKD + RD)
    ow = hc * VD
    units = SHARED // nd
    pad = -(-units // 128) * 128
    dot = functools.partial(jnp.dot, preferred_element_type=jnp.float32)
    ein = functools.partial(jnp.einsum, preferred_element_type=jnp.float32)

    def body(
        tokens, norm1_gain, w_query, w_down_kv, kv_gain, w_up_kv, w_attn_out, norm2_gain, w_router,
        w_shared_in, w_shared_out, w_expert_in, w_expert_out, routes, slots, blocks, cotangent,
    ):
        device = lax.axis_index(CTX) * nz + lax.axis_index(EXP)
        my_expert = device // 2
        tok = tokens.shape[1]
        width = tokens.shape[2]
        rows = width // nd
        length = tok * nc
        total = tok * nd
        experts = w_router.shape[1]
        cap = tok * TOP // experts * 4 // 3
        scale = (QKD + RD) ** (-0.5)

        small = jnp.concatenate(
            [norm1_gain, norm2_gain, w_router.reshape(-1), kv_gain]
            + [low(v).reshape(-1) for v in (routes, slots, blocks)]
        )
        parts = -(-small.shape[0] // 2048)
        small = jnp.pad(small, (0, 2048 * parts - small.shape[0])).reshape(16 * parts, 128)
        small = gather_small(small).reshape(nd, 2048 * parts)
        gain_one = wide(small[:, :rows].reshape(-1))
        gain_two = wide(small[:, rows : 2 * rows].reshape(-1))
        router = small[:, 2 * rows : 2 * rows + rows * experts].reshape(width, experts)
        begin = 2 * rows + rows * experts
        gain_latent = wide(small[:, begin : begin + LAT // nd].reshape(-1))
        begin += LAT // nd
        route_all = small[:, begin : begin + tok * TOP].reshape(nd, tok, TOP).astype(jnp.int32)
        begin += tok * TOP
        slot_all = small[:, begin : begin + tok * TOP].reshape(nd, tok, TOP).astype(jnp.int32)
        begin += tok * TOP
        block_all = small[:, begin : begin + tok].reshape(nc, nz, tok)
        block_seq = entry(block_all, lax.axis_index(EXP), 1).reshape(-1)
        tok_seq = gather_context(tokens[0]).reshape(length, width)
        down = lax.all_gather(w_down_kv, BOTH, axis=0, tiled=True)
        wq = w_query.reshape(rows, nc, hc, QKD + RD)
        wq = jnp.concatenate(
            [
                wq[..., :QKD].reshape(rows, nc, hc * QKD),
                wq[..., QKD:].reshape(rows, nc, hc * RD),
                w_attn_out.T.reshape(rows, nc, ow),
            ],
            axis=-1,
        ).transpose(1, 0, 2)
        wq = lax.all_to_all(wq, CTX, split_axis=0, concat_axis=0, tiled=True)
        wq = gather_z(wq).transpose(1, 0, 2, 3).reshape(width, qw + ow)
        out_t = wq[:, qw:]
        wq = wq[:, :qw]
        up = gather_z(w_up_kv).transpose(1, 0, 2).reshape(LAT, -1)
        shared = jnp.stack(
            [
                w_shared_in[:, :SHARED].reshape(rows, nd, units),
                w_shared_in[:, SHARED:].reshape(rows, nd, units),
                w_shared_out.T.reshape(rows, nd, units),
            ],
            axis=2,
        )
        shared = jnp.pad(shared, ((0, 0), (0, 0), (0, 0), (0, pad - units)))
        shared = shared.transpose(1, 0, 2, 3).reshape(nd, rows, 3 * pad)
        shared = lax.all_to_all(shared, BOTH, split_axis=0, concat_axis=0, tiled=True)
        shared = shared.reshape(width, 3 * pad)
        shared_in = shared[:, : 2 * pad]
        shared_out_t = shared[:, 2 * pad :]

        cosine, sine = rotation_table(jnp.arange(length, dtype=jnp.float32))
        head_cos, head_sin = cosine[:, None, :], sine[:, None, :]
        normed_seq, _ = normalize(wide(tok_seq))
        hidden_seq = low(normed_seq * gain_one)
        query = dot(hidden_seq, wq)
        q_nope = low(query[:, : hc * QKD]).reshape(length, hc, QKD)
        q_rope = low(rotary(query[:, hc * QKD :].reshape(length, hc, RD), head_cos, head_sin))
        compressed = dot(hidden_seq, down)
        normed_latent, scaling_latent = normalize(compressed[:, :LAT])
        latent = low(normed_latent * gain_latent)
        rope_key = low(rotary(compressed[:, LAT:], cosine, sine))
        key_value = low(dot(latent, up)).reshape(length, hc, QKD + VD)
        key, value = key_value[..., :QKD], key_value[..., QKD:]
        raw = ein("thd,nhd->htn", q_nope, key) + ein("thr,nr->htn", q_rope, rope_key)
        self_raw = jnp.sum(wide(q_nope) * wide(key), axis=-1) + jnp.sum(
            wide(q_rope) * wide(rope_key)[:, None, :], axis=-1
        )
        shift = jnp.floor(self_raw * scale).T
        allowed = (block_seq[None, :] <= block_seq[:, None])[None]
        weights = jnp.where(
            allowed, jnp.exp(jnp.where(allowed, raw * scale - shift[:, :, None], 0.0)), 0.0
        )
        weights_low = low(weights)
        denominator = jnp.sum(weights, axis=-1)
        denom_rows = denominator.T[:, :, None]
        attended = ein("htn,nhv->thv", weights_low, value) / denom_rows
        mixed = low(attended.reshape(length, ow))
        resid_part = low(lax.dot_general(mixed, out_t, (((1,), (1,)), ((), ())),
                                         preferred_element_type=jnp.float32))
        resid = wide(tokens[0]) + scatter_context(resid_part.reshape(nc, tok, width))

        normed_second, scaling_second = normalize(resid)
        hidden = low(normed_second * gain_two)
        logits = dot(hidden, router)
        onehot = wide(routes[0][:, :, None] == jnp.arange(experts)[None, None, :])
        gates = jax.nn.softmax(jnp.sum(onehot * logits[:, None, :], axis=-1), axis=-1)
        gates_dense = jnp.sum(onehot * gates[:, :, None], axis=1)
        hidden_all = lax.all_gather(hidden, BOTH, axis=0, tiled=True)
        hidden_all, cot_own = tie((hidden_all, cotangent[0]))
        cot_all = lax.all_gather(cot_own, BOTH, axis=0, tiled=True)

        named = route_all == my_expert
        slot_of = jnp.max(jnp.where(named, slot_all, -1), axis=-1)
        pick = slot_of[:, None, :] == jnp.arange(cap)[None, :, None]
        pick_low = low(pick)
        logits_all = dot(hidden_all, router)
        chosen = jnp.max(
            wide(route_all.reshape(total, TOP, 1) == jnp.arange(experts)[None, None, :]), axis=1
        )
        gates_all = jax.nn.softmax(jnp.where(chosen > 0, logits_all, -jnp.inf), axis=-1)
        gate_col = jnp.sum(
            jnp.where(jnp.arange(experts)[None, :] == my_expert, gates_all, 0.0), axis=1
        ).reshape(nd, 1, tok)
        gate_rows = jnp.sum(jnp.where(pick, gate_col, 0.0), axis=-1).reshape(nd * cap, 1)
        take = lambda table: low(ein("bst,btd->bsd", pick_low, table.reshape(nd, tok, width))).reshape(
            nd * cap, width
        )
        give = lambda table: ein("bst,bsd->btd", pick_low, table.reshape(nd, cap, width)).reshape(
            total, width
        )
        expert_in, expert_out = w_expert_in[0], w_expert_out[0]
        picked = take(hidden_all)
        pre = dot(picked, expert_in)
        expert_gate, expert_up = pre[:, :HALF], pre[:, HALF:]
        expert_silu = jax.nn.silu(expert_gate)
        act = low(expert_silu * expert_up)
        part = wide(low(dot(act, expert_out)))
        shared_pre = dot(hidden_all, shared_in)
        shared_gate, shared_up = shared_pre[:, :pad], shared_pre[:, pad:]
        shared_silu = jax.nn.silu(shared_gate)
        shared_act = low(shared_silu * shared_up)
        result = give(low(part * gate_rows)) + lax.dot_general(
            shared_act, shared_out_t, (((1,), (1,)), ((), ())), preferred_element_type=jnp.float32
        )
        result, cot_all = tie((low(result), cot_all))

        partial = scatter_core(result.reshape(nc, nz, tok, width))
        cot_rows = take(cot_all)
        grad_part = low(wide(cot_rows) * gate_rows)
        partial, cot_rows, grad_part = tie((partial, cot_rows, grad_part))

        partial = scatter_one(partial)
        grad_act = lax.dot_general(
            grad_part, expert_out, (((1,), (1,)), ((), ())), preferred_element_type=jnp.float32
        )
        grad_pre = low(
            jnp.concatenate(
                [silu_back(expert_gate, grad_act * expert_up), grad_act * expert_silu], axis=-1
            )
        )
        grad_rows = low(
            lax.dot_general(
                grad_pre, expert_in, (((1,), (1,)), ((), ())), preferred_element_type=jnp.float32
            )
        )
        grad_shared_act = dot(cot_all, shared_out_t)
        grad_shared_pre = low(
            jnp.concatenate(
                [silu_back(shared_gate, grad_shared_act * shared_up), grad_shared_act * shared_silu],
                axis=-1,
            )
        )
        partial, grad_rows, grad_shared_pre = tie((partial, grad_rows, grad_shared_pre))

        partial = scatter_two(partial)
        grad_hidden_part = give(grad_rows) + lax.dot_general(
            grad_shared_pre, shared_in, (((1,), (1,)), ((), ())), preferred_element_type=jnp.float32
        )
        partial, grad_hidden_part, grad_shared_pre, grad_pre, grad_part, cot_rows = tie(
            (partial, low(grad_hidden_part), grad_shared_pre, grad_pre, grad_part, cot_rows)
        )

        grad_partial = scatter_core(grad_hidden_part.reshape(nc, nz, tok, width))
        grad_shared = low(
            jnp.concatenate([dot(hidden_all.T, grad_shared_pre), dot(cot_all.T, shared_act)], axis=-1)
        )
        grad_partial, grad_shared, grad_pre = tie((grad_partial, grad_shared, grad_pre))
        output = low(resid + scatter_z(partial))
        grad_partial = scatter_one(grad_partial)
        grad_expert_out = dot(act.T, grad_part)
        grad_expert_in = dot(picked.T, grad_pre)
        grad_partial, grad_expert_out, grad_expert_in, cot_rows = tie(
            (grad_partial, grad_expert_out, grad_expert_in, cot_rows)
        )
        grad_partial = scatter_two(grad_partial)
        dots = jnp.sum(wide(cot_rows) * part, axis=-1).reshape(nd, cap, 1)
        dots = jnp.sum(jnp.where(pick, dots, 0.0), axis=1)
        dots = lax.all_to_all(dots, BOTH, split_axis=0, concat_axis=0, tiled=True)
        grad_gates = dots.reshape(experts, nd // experts, tok).sum(axis=1).T
        grad_logits = low(
            gates_dense
            * (grad_gates - jnp.sum(gates_dense * grad_gates, axis=-1, keepdims=True))
        )
        grad_router = dot(hidden.T, grad_logits)
        grad_hidden = scatter_z(grad_partial) + dot(grad_logits, router.T)
        grad_hidden, output = tie((grad_hidden, output))
        grad_mid, grad_gain_two = norm_back(grad_hidden, normed_second, scaling_second, gain_two)
        grad_resid = wide(cotangent[0]) + grad_mid

        grad_resid_seq = gather_context(low(grad_resid)).reshape(length, width)
        grad_mixed = dot(grad_resid_seq, out_t).reshape(length, hc, VD)
        grad_out_t = dot(grad_resid_seq.T, mixed)
        scaled = low(grad_mixed / denom_rows)
        correction = (jnp.sum(grad_mixed * attended, axis=-1) / denominator.T).T
        grad_weights = ein("thv,nhv->htn", scaled, value)
        grad_raw = low(weights * (grad_weights - correction[:, :, None]) * scale)
        grad_nope = ein("htn,nhd->thd", grad_raw, key)
        grad_rot = ein("htn,nr->thr", grad_raw, rope_key)
        grad_key = ein("htn,thd->nhd", grad_raw, q_nope)
        grad_value = ein("htn,thv->nhv", weights_low, scaled)
        grad_rope = ein("htn,thr->nr", grad_raw, q_rope)
        grad_kv = low(jnp.concatenate([grad_key, grad_value], axis=-1).reshape(length, hc * (QKD + VD)))
        grad_up = dot(latent.T, grad_kv)
        grad_latent = lax.dot_general(
            grad_kv, up, (((1,), (1,)), ((), ())), preferred_element_type=jnp.float32
        )
        grad_latent_pre, grad_gain_latent = norm_back(
            grad_latent, normed_latent, scaling_latent, gain_latent
        )
        grad_compressed = low(
            jnp.concatenate([grad_latent_pre, rotary_back(grad_rope, cosine, sine)], axis=-1)
        )
        grad_query = low(
            jnp.concatenate(
                [
                    grad_nope.reshape(length, hc * QKD),
                    rotary_back(grad_rot, head_cos, head_sin).reshape(length, hc * RD),
                ],
                axis=-1,
            )
        )
        grad_attn = jnp.concatenate([dot(hidden_seq.T, grad_query), grad_out_t], axis=-1)
        grad_down = dot(hidden_seq.T, grad_compressed)
        grad_first_part = low(
            lax.dot_general(
                grad_query, wq, (((1,), (1,)), ((), ())), preferred_element_type=jnp.float32
            )
            + lax.dot_general(
                grad_compressed, down, (((1,), (1,)), ((), ())), preferred_element_type=jnp.float32
            )
        )
        grad_first = scatter_context(grad_first_part.reshape(nc, tok, width))
        normed_first, scaling_first = normalize(wide(tokens[0]))
        grad_input, grad_gain_one = norm_back(grad_first, normed_first, scaling_first, gain_one)
        grad_input = grad_input + grad_resid

        exchange = lambda table: lax.all_to_all(
            low(table).reshape(nd, rows, table.shape[-1]), BOTH, split_axis=0, concat_axis=0, tiled=True
        )
        shared_back = exchange(grad_shared).reshape(nd, rows, 3, pad)[..., :units]
        grad_wsi = wide(shared_back[:, :, :2].transpose(1, 2, 0, 3)).reshape(rows, 2 * SHARED)
        grad_wso = wide(shared_back[:, :, 2].transpose(0, 2, 1)).reshape(SHARED, rows)
        attn_back = wide(exchange(grad_attn)).reshape(nc, nz, rows, qw + ow).sum(axis=1)
        grad_wq = jnp.concatenate(
            [
                attn_back[:, :, : hc * QKD].reshape(nc, rows, hc, QKD),
                attn_back[:, :, hc * QKD : qw].reshape(nc, rows, hc, RD),
            ],
            axis=-1,
        ).transpose(1, 0, 2, 3).reshape(rows, HEADS * (QKD + RD))
        grad_wo = attn_back[:, :, qw:].transpose(0, 2, 1).reshape(HEADS * VD, rows)
        grad_wdkv = wide(exchange(grad_down)).sum(axis=0)
        grad_wukv = scatter_z(low(grad_up).reshape(LAT, nz, -1).transpose(1, 0, 2))
        tiny = jnp.concatenate(
            [
                grad_gain_one.reshape(nd, rows),
                grad_gain_two.reshape(nd, rows),
                grad_router.reshape(nd, rows * experts),
                grad_gain_latent.reshape(nd, LAT // nd),
            ],
            axis=1,
        )
        tiny = lax.all_to_all(tiny, BOTH, split_axis=0, concat_axis=0, tiled=True).sum(axis=0)
        return (
            output[None],
            grad_input[None],
            tiny[:rows],
            grad_wq,
            grad_wdkv,
            tiny[2 * rows + rows * experts :],
            grad_wukv,
            grad_wo,
            tiny[rows : 2 * rows],
            tiny[2 * rows : 2 * rows + rows * experts].reshape(rows, experts),
            grad_wsi,
            grad_wso,
            grad_expert_in[None],
            grad_expert_out[None],
        )

    return body


def solution(mesh):
    placed = (
        P(EXP, CTX, None),
        P(BOTH),
        P(BOTH, None),
        P(BOTH, None),
        P(BOTH),
        P(None, BOTH),
        P(None, BOTH),
        P(BOTH),
        P(BOTH, None),
        P(BOTH, None),
        P(None, BOTH),
        P(BOTH, None, None),
        P(BOTH, None, None),
        P(EXP, CTX, None),
        P(EXP, CTX, None),
        P(EXP, CTX),
        P(EXP, CTX, None),
    )
    nc, nz = mesh.shape[CTX], mesh.shape[EXP]
    split = nc == 8 and nz == 4
    return jax.shard_map(
        fast_body(nc, nz) if split else body,
        mesh=mesh,
        in_specs=placed,
        out_specs=(
            P(EXP, CTX, None),
            P(EXP, CTX, None),
            P(BOTH),
            P(BOTH, None),
            P(BOTH, None),
            P(BOTH),
            P(None, BOTH),
            P(None, BOTH),
            P(BOTH),
            P(BOTH, None),
            P(BOTH, None),
            P(None, BOTH),
            P(BOTH, None, None),
            P(BOTH, None, None),
        ),
        check_vma=False,
    )
```

```python
import functools
import math

import jax
import jax.numpy as jnp
from jax import lax
from jax.sharding import PartitionSpec as P

HEADS = 16
QKD = 128
RD = 64
VD = 128
LAT = 512
TOP = 6
SHARED = 2816
HALF = 704
CTX = "context"
EXP = "expert"
BOTH = (CTX, EXP)


epsilon = 1e-06
highest = lax.Precision.HIGHEST


def normalize(values):
    scaling = lax.rsqrt(jnp.mean(values * values, axis=-1, keepdims=True) + epsilon)
    return (values * scaling, scaling)


def norm_back(grad_normed, normed, scaling, gain):
    grad_gain = jnp.sum(grad_normed * normed, axis=0)
    grad_unit = grad_normed * gain
    grad_values = scaling * (
        grad_unit - normed * jnp.mean(grad_unit * normed, axis=-1, keepdims=True)
    )
    return (grad_values, grad_gain)


def rotary(values, cosine, sine_table):
    middle = values.shape[-1] // 2
    first_half = values[..., :middle]
    second_half = values[..., middle:]
    return jnp.concatenate(
        [
            first_half * cosine - second_half * sine_table,
            second_half * cosine + first_half * sine_table,
        ],
        axis=-1,
    )


def rotary_back(grads_in, cosine, sine_table):
    middle = grads_in.shape[-1] // 2
    first_half = grads_in[..., :middle]
    second_half = grads_in[..., middle:]
    return jnp.concatenate(
        [
            first_half * cosine + second_half * sine_table,
            second_half * cosine - first_half * sine_table,
        ],
        axis=-1,
    )


def rotation_table(positions):
    exponent = jnp.arange(RD // 2, dtype=jnp.float32) * (2.0 / RD)
    angle_table = positions[:, None] * (10000.0 ** (-exponent))[None, :]
    return (jnp.cos(angle_table), jnp.sin(angle_table))


def silu_back(value, grads_in):
    sigma_value = jax.nn.sigmoid(value)
    return grads_in * sigma_value * (1.0 + value * (1.0 - sigma_value))


def head_scores(query_low, key_low, rope_low):
    nope_part = jnp.einsum(
        "thd,nhd->htn", query_low[..., :QKD], key_low, preferred_element_type=jnp.float32
    )
    rope_part = jnp.einsum(
        "thr,nr->htn", query_low[..., QKD:], rope_low, preferred_element_type=jnp.float32
    )
    return nope_part + rope_part


def both_halves(buffer_rows, experts_total, capacity):
    width = buffer_rows.shape[-1]
    shaped = buffer_rows.reshape(experts_total, 1, capacity, width)
    return jnp.broadcast_to(shaped, (experts_total, 2, capacity, width)).reshape(
        2 * experts_total, capacity, width
    )


def halves_sum(received, experts_total, capacity):
    width = received.shape[-1]
    return (
        received.astype(jnp.float32)
        .reshape(experts_total, 2, capacity, width)
        .sum(axis=1)
        .reshape(experts_total * capacity, width)
    )


def body(
    tokens,
    norm1_gain,
    w_query,
    w_down_kv,
    kv_gain,
    w_up_kv,
    w_attn_out,
    norm2_gain,
    w_router,
    w_shared_in,
    w_shared_out,
    w_expert_in,
    w_expert_out,
    routes,
    slots,
    blocks,
    cotangent,
):
    (
        gain_first,
        query_weight,
        down_weight,
        latent_gain,
        up_weight,
        out_weight,
        gain_second,
        router_weight,
        shared_in_weight,
        shared_out_weight,
    ) = (
        lax.all_gather(norm1_gain, BOTH, axis=0, tiled=True),
        lax.all_gather(w_query, BOTH, axis=0, tiled=True),
        lax.all_gather(w_down_kv, BOTH, axis=0, tiled=True),
        lax.all_gather(kv_gain, BOTH, axis=0, tiled=True),
        lax.all_gather(w_up_kv, BOTH, axis=1, tiled=True),
        lax.all_gather(w_attn_out, BOTH, axis=1, tiled=True),
        lax.all_gather(norm2_gain, BOTH, axis=0, tiled=True),
        lax.all_gather(w_router, BOTH, axis=0, tiled=True),
        lax.all_gather(w_shared_in, BOTH, axis=0, tiled=True),
        lax.all_gather(w_shared_out, BOTH, axis=1, tiled=True),
    )
    tok_count = tokens.shape[1]
    length_all = tok_count * lax.axis_size(CTX)
    experts_total = router_weight.shape[1]
    capacity = tok_count * TOP // experts_total * 4 // 3
    score_scale = (QKD + RD) ** (-0.5)
    residual_in = tokens[0].astype(jnp.float32)
    own_blocks = blocks[0]
    route_ids = routes[0]
    slot_ids = slots[0]
    positions = (lax.axis_index(CTX) * tok_count + jnp.arange(tok_count)).astype(jnp.float32)
    cosine, sine_table = rotation_table(positions)
    head_cos = cosine[:, None, :]
    head_sin = sine_table[:, None, :]
    gain_one = gain_first.astype(jnp.float32)
    gain_two = gain_second.astype(jnp.float32)
    gain_latent = latent_gain.astype(jnp.float32)
    normed_first, scaling_first = normalize(residual_in)
    hidden_first = (normed_first * gain_one).astype(jnp.bfloat16)
    query_pre = jnp.dot(hidden_first, query_weight, preferred_element_type=jnp.float32).reshape(
        tok_count, HEADS, QKD + RD
    )
    query_low = jnp.concatenate(
        [query_pre[..., :QKD], rotary(query_pre[..., QKD:], head_cos, head_sin)], axis=-1
    ).astype(jnp.bfloat16)
    compressed = jnp.dot(hidden_first, down_weight, preferred_element_type=jnp.float32)
    normed_latent, scaling_latent = normalize(compressed[:, :LAT])
    latent_low = (normed_latent * gain_latent).astype(jnp.bfloat16)
    rope_low = rotary(compressed[:, LAT:], cosine, sine_table).astype(jnp.bfloat16)
    key_value = jnp.dot(latent_low, up_weight, preferred_element_type=jnp.float32).astype(
        jnp.bfloat16
    )
    own_heads = key_value.reshape(tok_count, HEADS, QKD + VD)
    self_raw = jnp.einsum(
        "thd,thd->ht",
        query_low[..., :QKD],
        own_heads[..., :QKD],
        preferred_element_type=jnp.float32,
    ) + jnp.einsum("thr,tr->ht", query_low[..., QKD:], rope_low, preferred_element_type=jnp.float32)
    shift_table = jnp.floor(self_raw * score_scale)
    last_block = jnp.max(own_blocks)

    def block_weights(kv_piece, rope_piece, blocks_piece):
        kv_heads = kv_piece.reshape(kv_piece.shape[0], HEADS, QKD + VD)
        raw_scores = head_scores(query_low, kv_heads[..., :QKD], rope_piece)
        allowed = (blocks_piece[None, :] <= own_blocks[:, None])[None]
        shifted = jnp.where(allowed, raw_scores * score_scale - shift_table[:, :, None], 0.0)
        return (kv_heads, jnp.where(allowed, jnp.exp(shifted), 0.0))

    empty_state = (
        jnp.zeros((tok_count, HEADS, VD), jnp.float32),
        jnp.zeros((HEADS, tok_count), jnp.float32),
    )
    kv_piece = lax.all_gather(key_value, CTX, axis=0, tiled=True)
    rope_piece = lax.all_gather(rope_low, CTX, axis=0, tiled=True)
    blocks_piece = lax.all_gather(own_blocks, CTX, axis=0, tiled=True)
    make_kv = lambda: kv_piece

    def attend_compute(state_now):
        kv_heads, weights = block_weights(make_kv(), rope_piece, blocks_piece)
        running = jnp.einsum(
            "htn,nhv->thv",
            weights.astype(jnp.bfloat16),
            kv_heads[..., QKD:],
            preferred_element_type=jnp.float32,
        )
        return (running, jnp.sum(weights, axis=-1))

    running, denominator = lax.cond(
        jnp.min(blocks_piece) > last_block, lambda state_now: state_now, attend_compute, empty_state
    )
    denom_rows = jnp.transpose(denominator)
    attended = running / denom_rows[:, :, None]
    mixed_low = attended.reshape(tok_count, HEADS * VD).astype(jnp.bfloat16)
    residual_mid = residual_in + jnp.dot(mixed_low, out_weight, preferred_element_type=jnp.float32)
    normed_second, scaling_second = normalize(residual_mid)
    hidden_second = (normed_second * gain_two).astype(jnp.bfloat16)
    logits = jnp.dot(hidden_second, router_weight, preferred_element_type=jnp.float32)
    route_onehot = (route_ids[:, :, None] == jnp.arange(experts_total)[None, None, :]).astype(
        jnp.float32
    )
    chosen = jnp.sum(route_onehot * logits[:, None, :], axis=-1)
    gate_weights = jax.nn.softmax(chosen, axis=-1)
    shared_pre = jnp.dot(hidden_second, shared_in_weight, preferred_element_type=jnp.float32)
    shared_act = (jax.nn.silu(shared_pre[:, :SHARED]) * shared_pre[:, SHARED:]).astype(jnp.bfloat16)
    shared_result = jnp.dot(shared_act, shared_out_weight, preferred_element_type=jnp.float32)
    slot_index = (route_ids * capacity + slot_ids).reshape(-1)
    model_width = hidden_second.shape[1]
    repeated = jnp.broadcast_to(hidden_second[:, None, :], (tok_count, TOP, model_width)).reshape(
        tok_count * TOP, model_width
    )
    send_rows = (
        jnp.zeros((experts_total * capacity, model_width), jnp.bfloat16)
        .at[slot_index]
        .set(repeated)
    )
    weight_in_local = w_expert_in[0]
    weight_out_local = w_expert_out[0]
    received = lax.all_to_all(
        both_halves(send_rows, experts_total, capacity),
        BOTH,
        split_axis=0,
        concat_axis=0,
        tiled=True,
    )
    pre_expert = jnp.einsum(
        "scd,df->scf", received, weight_in_local, preferred_element_type=jnp.float32
    )
    activation = (jax.nn.silu(pre_expert[..., :HALF]) * pre_expert[..., HALF:]).astype(jnp.bfloat16)
    part_rows = jnp.einsum(
        "scf,fd->scd", activation, weight_out_local, preferred_element_type=jnp.float32
    ).astype(jnp.bfloat16)
    returned = lax.all_to_all(
        part_rows, BOTH, split_axis=0, concat_axis=0, tiled=True
    )
    returned, received_rows, pre_expert = (returned, received, pre_expert)
    expert_table = halves_sum(returned, experts_total, capacity)
    picked = expert_table[slot_index].reshape(tok_count, TOP, model_width)
    routed = jnp.sum(gate_weights[:, :, None] * picked, axis=1)
    output_low = (residual_mid + shared_result + routed).astype(jnp.bfloat16)
    grad_low = cotangent[0]
    grad_out = grad_low.astype(jnp.float32)
    grad_shared_out = jnp.dot(shared_act.T, grad_low, preferred_element_type=jnp.float32)
    grad_shared_act = jnp.dot(grad_low, shared_out_weight.T, preferred_element_type=jnp.float32)
    shared_gate = shared_pre[:, :SHARED]
    shared_up = shared_pre[:, SHARED:]
    grad_shared_pre = jnp.concatenate(
        [
            silu_back(shared_gate, grad_shared_act * shared_up),
            grad_shared_act * jax.nn.silu(shared_gate),
        ],
        axis=-1,
    ).astype(jnp.bfloat16)
    grad_shared_in = jnp.dot(hidden_second.T, grad_shared_pre, preferred_element_type=jnp.float32)
    grad_hidden = jnp.dot(grad_shared_pre, shared_in_weight.T, preferred_element_type=jnp.float32)
    grad_gates = jnp.sum(grad_out[:, None, :] * picked, axis=-1)
    grad_chosen = gate_weights * (
        grad_gates - jnp.sum(gate_weights * grad_gates, axis=-1, keepdims=True)
    )
    grad_logits = jnp.sum(route_onehot * grad_chosen[:, :, None], axis=1).astype(jnp.bfloat16)
    grad_router = jnp.dot(hidden_second.T, grad_logits, preferred_element_type=jnp.float32)
    grad_hidden = grad_hidden + jnp.dot(
        grad_logits, router_weight.T, preferred_element_type=jnp.float32
    )
    grad_parts = (
        (gate_weights[:, :, None] * grad_out[:, None, :])
        .astype(jnp.bfloat16)
        .reshape(tok_count * TOP, model_width)
    )
    grad_send = (
        jnp.zeros((experts_total * capacity, model_width), jnp.bfloat16)
        .at[slot_index]
        .set(grad_parts)
    )
    grad_received = lax.all_to_all(
        both_halves(grad_send, experts_total, capacity),
        BOTH,
        split_axis=0,
        concat_axis=0,
        tiled=True,
    )
    expert_gate = pre_expert[..., :HALF]
    expert_up = pre_expert[..., HALF:]
    expert_silu = jax.nn.silu(expert_gate)
    expert_act = (expert_silu * expert_up).astype(jnp.bfloat16)
    grad_expert_out = jnp.einsum(
        "scf,scd->fd", expert_act, grad_received, preferred_element_type=jnp.float32
    )
    grad_expert_act = jnp.einsum(
        "scd,fd->scf", grad_received, weight_out_local, preferred_element_type=jnp.float32
    )
    grad_expert_pre = jnp.concatenate(
        [silu_back(expert_gate, grad_expert_act * expert_up), grad_expert_act * expert_silu],
        axis=-1,
    ).astype(jnp.bfloat16)
    grad_expert_in = jnp.einsum(
        "scd,scf->df", received_rows, grad_expert_pre, preferred_element_type=jnp.float32
    )
    grad_rows = jnp.einsum(
        "scf,df->scd", grad_expert_pre, weight_in_local, preferred_element_type=jnp.float32
    )
    grad_back = lax.all_to_all(
        grad_rows.astype(jnp.bfloat16),
        BOTH,
        split_axis=0,
        concat_axis=0,
        tiled=True,
    ).astype(grad_rows.dtype)
    grad_table = halves_sum(grad_back, experts_total, capacity)
    grad_hidden = grad_hidden + jnp.sum(
        grad_table[slot_index].reshape(tok_count, TOP, model_width), axis=1
    )
    grad_mid_norm, grad_gain_second = norm_back(
        grad_hidden, normed_second, scaling_second, gain_two
    )
    grad_resid = grad_out + grad_mid_norm
    grad_resid_low = grad_resid.astype(jnp.bfloat16)
    grad_attn_out = jnp.dot(mixed_low.T, grad_resid_low, preferred_element_type=jnp.float32)
    grad_mixed = jnp.dot(grad_resid_low, out_weight.T, preferred_element_type=jnp.float32).reshape(
        tok_count, HEADS, VD
    )
    scaled_low = (grad_mixed / denom_rows[:, :, None]).astype(jnp.bfloat16)
    correction = jnp.transpose(jnp.sum(grad_mixed * attended, axis=-1) / denom_rows)
    full_kv, full_rope, full_blocks, full_latent = (
        lax.all_gather(key_value, CTX, axis=0, tiled=True),
        lax.all_gather(rope_low, CTX, axis=0, tiled=True),
        lax.all_gather(own_blocks, CTX, axis=0, tiled=True),
        lax.all_gather(latent_low, CTX, axis=0, tiled=True),
    )
    key_block = math.gcd(length_all, 512)
    block_count = length_all // key_block
    kv_width = HEADS * (QKD + VD)

    def key_step(grad_query, block_index):
        begin_row = block_index * key_block
        kv_piece = lax.dynamic_slice_in_dim(full_kv, begin_row, key_block, 0)
        rope_piece = lax.dynamic_slice_in_dim(full_rope, begin_row, key_block, 0)
        blocks_piece = lax.dynamic_slice_in_dim(full_blocks, begin_row, key_block, 0)

        def key_compute(grad_acc):
            kv_heads, weights = block_weights(kv_piece, rope_piece, blocks_piece)
            grad_weights = jnp.einsum(
                "thv,nhv->htn", scaled_low, kv_heads[..., QKD:], preferred_element_type=jnp.float32
            )
            grad_raw = (weights * (grad_weights - correction[:, :, None]) * score_scale).astype(
                jnp.bfloat16
            )
            grad_nope = jnp.einsum(
                "htn,nhd->thd", grad_raw, kv_heads[..., :QKD], preferred_element_type=jnp.float32
            )
            grad_rot = jnp.einsum(
                "htn,nr->thr", grad_raw, rope_piece, preferred_element_type=jnp.float32
            )
            grad_key = jnp.einsum(
                "htn,thd->nhd", grad_raw, query_low[..., :QKD], preferred_element_type=jnp.float32
            )
            grad_value = jnp.einsum(
                "htn,thv->nhv",
                weights.astype(jnp.bfloat16),
                scaled_low,
                preferred_element_type=jnp.float32,
            )
            grad_rope = jnp.einsum(
                "htn,thr->nr", grad_raw, query_low[..., QKD:], preferred_element_type=jnp.float32
            )
            grad_kv = jnp.concatenate([grad_key, grad_value], axis=-1).reshape(key_block, kv_width)
            return (grad_acc + jnp.concatenate([grad_nope, grad_rot], axis=-1), grad_kv, grad_rope)

        def skipped(grad_acc):
            return (
                grad_acc,
                jnp.zeros((key_block, kv_width), jnp.float32),
                jnp.zeros((key_block, RD), jnp.float32),
            )

        grad_query, grad_kv, grad_rope = lax.cond(
            jnp.min(blocks_piece) > last_block, skipped, key_compute, grad_query
        )
        return (grad_query, (grad_kv, grad_rope))

    grad_query_rot, (grad_kv_blocks, grad_rope_blocks) = lax.scan(
        key_step, jnp.zeros((tok_count, HEADS, QKD + RD), jnp.float32), jnp.arange(block_count)
    )
    partial_kv = grad_kv_blocks.reshape(length_all, kv_width)
    partial_rope = grad_rope_blocks.reshape(length_all, RD)
    up_float = up_weight.astype(jnp.float32)
    kv_sum, rope_sum = (
        lax.psum_scatter(
            partial_kv.astype(jnp.bfloat16), CTX, scatter_dimension=0, tiled=True
        ).astype(jnp.float32),
        lax.psum_scatter(
            partial_rope.astype(jnp.bfloat16), CTX, scatter_dimension=0, tiled=True
        ).astype(jnp.float32),
    )
    grad_up_kv = jnp.dot(
        latent_low.astype(jnp.float32).T,
        kv_sum,
        precision=highest,
        preferred_element_type=jnp.float32,
    )
    grad_latent = jnp.dot(kv_sum, up_float.T, precision=highest, preferred_element_type=jnp.float32)
    grad_latent_pre, grad_gain_latent = norm_back(
        grad_latent, normed_latent, scaling_latent, gain_latent
    )
    grad_compressed = jnp.concatenate(
        [grad_latent_pre, rotary_back(rope_sum, cosine, sine_table)], axis=-1
    ).astype(jnp.bfloat16)
    grad_down_kv = jnp.dot(hidden_first.T, grad_compressed, preferred_element_type=jnp.float32)
    grad_query_low = (
        jnp.concatenate(
            [grad_query_rot[..., :QKD], rotary_back(grad_query_rot[..., QKD:], head_cos, head_sin)],
            axis=-1,
        )
        .astype(jnp.bfloat16)
        .reshape(tok_count, HEADS * (QKD + RD))
    )
    grad_query_weight = jnp.dot(hidden_first.T, grad_query_low, preferred_element_type=jnp.float32)
    grad_hidden_first = jnp.dot(
        grad_query_low, query_weight.T, preferred_element_type=jnp.float32
    ) + jnp.dot(grad_compressed, down_weight.T, preferred_element_type=jnp.float32)
    grad_first_norm, grad_gain_first = norm_back(
        grad_hidden_first, normed_first, scaling_first, gain_one
    )
    grad_input = grad_resid + grad_first_norm
    (
        grad_norm_one,
        grad_wq,
        grad_wdkv,
        grad_gkv,
        grad_wukv,
        grad_wo,
        grad_norm_two,
        grad_wr,
        grad_wsi,
        grad_wso,
    ) = (
        lax.psum_scatter(grad_gain_first, BOTH, scatter_dimension=0, tiled=True),
        lax.psum_scatter(grad_query_weight, BOTH, scatter_dimension=0, tiled=True),
        lax.psum_scatter(grad_down_kv, BOTH, scatter_dimension=0, tiled=True),
        lax.psum_scatter(grad_gain_latent, BOTH, scatter_dimension=0, tiled=True),
        lax.psum_scatter(grad_up_kv, BOTH, scatter_dimension=1, tiled=True),
        lax.psum_scatter(grad_attn_out, BOTH, scatter_dimension=1, tiled=True),
        lax.psum_scatter(grad_gain_second, BOTH, scatter_dimension=0, tiled=True),
        lax.psum_scatter(grad_router, BOTH, scatter_dimension=0, tiled=True),
        lax.psum_scatter(grad_shared_in, BOTH, scatter_dimension=0, tiled=True),
        lax.psum_scatter(grad_shared_out, BOTH, scatter_dimension=1, tiled=True),
    )
    return (
        output_low[None],
        grad_input[None],
        grad_norm_one,
        grad_wq,
        grad_wdkv,
        grad_gkv,
        grad_wukv,
        grad_wo,
        grad_norm_two,
        grad_wr,
        grad_wsi,
        grad_wso,
        grad_expert_in[None],
        grad_expert_out[None],
    )


low = lambda v: v.astype(jnp.bfloat16)
wide = lambda v: v.astype(jnp.float32)


def place():
    index = lax.axis_index(CTX)
    return index % 2, index // 2 % 2, index // 4, lax.axis_index(EXP)


def swap(values, bit):
    return lax.ppermute(values, CTX, [(i, i ^ bit) for i in range(8)])


def shift_z(values, step):
    return lax.ppermute(values, EXP, [(i, (i + step) % 4) for i in range(4)])


def entry(values, index, axis):
    return lax.dynamic_index_in_dim(values, index, axis, keepdims=False)


def join(mine, got, bit, axis):
    return jnp.concatenate(
        [jnp.where(bit == 0, mine, got), jnp.where(bit == 0, got, mine)], axis
    )


def gather_z(values):
    z = lax.axis_index(EXP)
    parts = [values] + [shift_z(values, step) for step in (2, 1, 3)]
    order = (0, 2, 1, 3)

    def chunk(j):
        ahead = (z - j) % 4
        out = parts[0]
        for step in (1, 2, 3):
            out = jnp.where(ahead == step, parts[order[step]], out)
        return out

    return jnp.stack([chunk(j) for j in range(4)])


def gather_xy(values, x_first):
    _, x, y, _ = place()
    values = values[None, None]
    if x_first:
        values = join(values, swap(values, 2), x, 1)
        return join(values, swap(values, 4), y, 0)
    values = join(values, swap(values, 4), y, 0)
    return join(values, swap(values, 2), x, 1)


def gather_context(values):
    core = place()[0]
    axis = values.ndim - 2
    cut = values.shape[axis] // 2
    first = lax.slice_in_dim(values, 0, cut, axis=axis)
    second = lax.slice_in_dim(values, cut, 2 * cut, axis=axis)
    both = jnp.concatenate([gather_xy(first, True), gather_xy(second, False)], axis + 2)
    both = both[:, :, None]
    both = join(both, swap(both, 1), core, 2)
    return both.reshape((8,) + values.shape)


def gather_all(values):
    return gather_context(gather_z(values)).reshape((32,) + values.shape)


def gather_small(values):
    core, x, y, _ = place()
    out = gather_z(values)[None]
    out = join(out, swap(out, 1), core, 0)
    out = join(out, swap(out, 2), x, 0)
    out = join(out, swap(out, 4), y, 0)
    return out.reshape((32,) + values.shape)


def halve(values, axis, mine, bit):
    got = swap(entry(values, 1 - mine, axis), bit)
    return low(wide(entry(values, mine, axis)) + wide(got))


def scatter_core(values):
    return halve(values.reshape((2, 2, 2) + values.shape[1:]), 2, place()[0], 1)


def scatter_one(values):
    _, x, y, _ = place()
    axis = values.ndim - 2
    cut = values.shape[axis] // 2
    first = lax.slice_in_dim(values, 0, cut, axis=axis)
    second = lax.slice_in_dim(values, cut, 2 * cut, axis=axis)
    return halve(first, 1, x, 2), halve(second, 0, y, 4)


def scatter_two(pair):
    _, x, y, _ = place()
    pair = (halve(pair[0], 0, y, 4), halve(pair[1], 0, x, 2))
    return jnp.concatenate(pair, pair[0].ndim - 2)


def scatter_context(values):
    return wide(scatter_two(scatter_one(scatter_core(values))))


def scatter_z(values):
    z = lax.axis_index(EXP)
    out = wide(entry(values, z, 0))
    for step in (2, 1, 3):
        out = out + wide(shift_z(entry(values, (z + step) % 4, 0), step))
    return out


tie = lax.optimization_barrier


def fast_body(nc, nz):
    nd = nc * nz
    hc = HEADS // nc
    qw = hc * (QKD + RD)
    ow = hc * VD
    units = SHARED // nd
    pad = -(-units // 128) * 128
    dot = functools.partial(jnp.dot, preferred_element_type=jnp.float32)
    ein = functools.partial(jnp.einsum, preferred_element_type=jnp.float32)

    def body(
        tokens, norm1_gain, w_query, w_down_kv, kv_gain, w_up_kv, w_attn_out, norm2_gain, w_router,
        w_shared_in, w_shared_out, w_expert_in, w_expert_out, routes, slots, blocks, cotangent,
    ):
        device = lax.axis_index(CTX) * nz + lax.axis_index(EXP)
        my_expert = device // 2
        tok = tokens.shape[1]
        width = tokens.shape[2]
        rows = width // nd
        length = tok * nc
        total = tok * nd
        experts = w_router.shape[1]
        cap = tok * TOP // experts * 4 // 3
        scale = (QKD + RD) ** (-0.5)

        small = jnp.concatenate(
            [norm1_gain, norm2_gain, w_router.reshape(-1), kv_gain]
            + [low(v).reshape(-1) for v in (routes, slots, blocks)]
        )
        parts = -(-small.shape[0] // 2048)
        small = jnp.pad(small, (0, 2048 * parts - small.shape[0])).reshape(16 * parts, 128)
        small = gather_small(small).reshape(nd, 2048 * parts)
        gain_one = wide(small[:, :rows].reshape(-1))
        gain_two = wide(small[:, rows : 2 * rows].reshape(-1))
        router = small[:, 2 * rows : 2 * rows + rows * experts].reshape(width, experts)
        begin = 2 * rows + rows * experts
        gain_latent = wide(small[:, begin : begin + LAT // nd].reshape(-1))
        begin += LAT // nd
        route_all = small[:, begin : begin + tok * TOP].reshape(nd, tok, TOP).astype(jnp.int32)
        begin += tok * TOP
        slot_all = small[:, begin : begin + tok * TOP].reshape(nd, tok, TOP).astype(jnp.int32)
        begin += tok * TOP
        block_all = small[:, begin : begin + tok].reshape(nc, nz, tok)
        block_seq = entry(block_all, lax.axis_index(EXP), 1).reshape(-1)
        tok_seq = gather_context(tokens[0]).reshape(length, width)
        down = lax.all_gather(w_down_kv, BOTH, axis=0, tiled=True)
        wq = w_query.reshape(rows, nc, hc, QKD + RD)
        wq = jnp.concatenate(
            [
                wq[..., :QKD].reshape(rows, nc, hc * QKD),
                wq[..., QKD:].reshape(rows, nc, hc * RD),
                w_attn_out.T.reshape(rows, nc, ow),
            ],
            axis=-1,
        ).transpose(1, 0, 2)
        wq = lax.all_to_all(wq, CTX, split_axis=0, concat_axis=0, tiled=True)
        wq = gather_z(wq).transpose(1, 0, 2, 3).reshape(width, qw + ow)
        out_t = wq[:, qw:]
        wq = wq[:, :qw]
        up = gather_z(w_up_kv).transpose(1, 0, 2).reshape(LAT, -1)
        shared = jnp.stack(
            [
                w_shared_in[:, :SHARED].reshape(rows, nd, units),
                w_shared_in[:, SHARED:].reshape(rows, nd, units),
                w_shared_out.T.reshape(rows, nd, units),
            ],
            axis=2,
        )
        shared = jnp.pad(shared, ((0, 0), (0, 0), (0, 0), (0, pad - units)))
        shared = shared.transpose(1, 0, 2, 3).reshape(nd, rows, 3 * pad)
        shared = lax.all_to_all(shared, BOTH, split_axis=0, concat_axis=0, tiled=True)
        shared = shared.reshape(width, 3 * pad)
        shared_in = shared[:, : 2 * pad]
        shared_out_t = shared[:, 2 * pad :]

        cosine, sine = rotation_table(jnp.arange(length, dtype=jnp.float32))
        head_cos, head_sin = cosine[:, None, :], sine[:, None, :]
        normed_seq, _ = normalize(wide(tok_seq))
        hidden_seq = low(normed_seq * gain_one)
        query = dot(hidden_seq, wq)
        q_nope = low(query[:, : hc * QKD]).reshape(length, hc, QKD)
        q_rope = low(rotary(query[:, hc * QKD :].reshape(length, hc, RD), head_cos, head_sin))
        compressed = dot(hidden_seq, down)
        normed_latent, scaling_latent = normalize(compressed[:, :LAT])
        latent = low(normed_latent * gain_latent)
        rope_key = low(rotary(compressed[:, LAT:], cosine, sine))
        key_value = low(dot(latent, up)).reshape(length, hc, QKD + VD)
        key, value = key_value[..., :QKD], key_value[..., QKD:]
        raw = ein("thd,nhd->htn", q_nope, key) + ein("thr,nr->htn", q_rope, rope_key)
        self_raw = jnp.sum(wide(q_nope) * wide(key), axis=-1) + jnp.sum(
            wide(q_rope) * wide(rope_key)[:, None, :], axis=-1
        )
        shift = jnp.floor(self_raw * scale).T
        allowed = (block_seq[None, :] <= block_seq[:, None])[None]
        weights = jnp.where(
            allowed, jnp.exp(jnp.where(allowed, raw * scale - shift[:, :, None], 0.0)), 0.0
        )
        weights_low = low(weights)
        denominator = jnp.sum(weights, axis=-1)
        denom_rows = denominator.T[:, :, None]
        attended = ein("htn,nhv->thv", weights_low, value) / denom_rows
        mixed = low(attended.reshape(length, ow))
        resid_part = low(lax.dot_general(mixed, out_t, (((1,), (1,)), ((), ())),
                                         preferred_element_type=jnp.float32))
        resid = wide(tokens[0]) + scatter_context(resid_part.reshape(nc, tok, width))

        normed_second, scaling_second = normalize(resid)
        hidden = low(normed_second * gain_two)
        logits = dot(hidden, router)
        onehot = wide(routes[0][:, :, None] == jnp.arange(experts)[None, None, :])
        gates = jax.nn.softmax(jnp.sum(onehot * logits[:, None, :], axis=-1), axis=-1)
        gates_dense = jnp.sum(onehot * gates[:, :, None], axis=1)
        hidden_all = lax.all_gather(hidden, BOTH, axis=0, tiled=True)
        hidden_all, cot_own = tie((hidden_all, cotangent[0]))
        cot_all = lax.all_gather(cot_own, BOTH, axis=0, tiled=True)

        named = route_all == my_expert
        slot_of = jnp.max(jnp.where(named, slot_all, -1), axis=-1)
        pick = slot_of[:, None, :] == jnp.arange(cap)[None, :, None]
        pick_low = low(pick)
        logits_all = dot(hidden_all, router)
        chosen = jnp.max(
            wide(route_all.reshape(total, TOP, 1) == jnp.arange(experts)[None, None, :]), axis=1
        )
        gates_all = jax.nn.softmax(jnp.where(chosen > 0, logits_all, -jnp.inf), axis=-1)
        gate_col = jnp.sum(
            jnp.where(jnp.arange(experts)[None, :] == my_expert, gates_all, 0.0), axis=1
        ).reshape(nd, 1, tok)
        gate_rows = jnp.sum(jnp.where(pick, gate_col, 0.0), axis=-1).reshape(nd * cap, 1)
        take = lambda table: low(ein("bst,btd->bsd", pick_low, table.reshape(nd, tok, width))).reshape(
            nd * cap, width
        )
        give = lambda table: ein("bst,bsd->btd", pick_low, table.reshape(nd, cap, width)).reshape(
            total, width
        )
        expert_in, expert_out = w_expert_in[0], w_expert_out[0]
        picked = take(hidden_all)
        pre = dot(picked, expert_in)
        expert_gate, expert_up = pre[:, :HALF], pre[:, HALF:]
        expert_silu = jax.nn.silu(expert_gate)
        act = low(expert_silu * expert_up)
        part = wide(low(dot(act, expert_out)))
        shared_pre = dot(hidden_all, shared_in)
        shared_gate, shared_up = shared_pre[:, :pad], shared_pre[:, pad:]
        shared_silu = jax.nn.silu(shared_gate)
        shared_act = low(shared_silu * shared_up)
        result = give(low(part * gate_rows)) + lax.dot_general(
            shared_act, shared_out_t, (((1,), (1,)), ((), ())), preferred_element_type=jnp.float32
        )
        result, cot_all = tie((low(result), cot_all))

        partial = scatter_core(result.reshape(nc, nz, tok, width))
        cot_rows = take(cot_all)
        grad_part = low(wide(cot_rows) * gate_rows)
        partial, cot_rows, grad_part = tie((partial, cot_rows, grad_part))

        partial = scatter_one(partial)
        grad_act = lax.dot_general(
            grad_part, expert_out, (((1,), (1,)), ((), ())), preferred_element_type=jnp.float32
        )
        grad_pre = low(
            jnp.concatenate(
                [silu_back(expert_gate, grad_act * expert_up), grad_act * expert_silu], axis=-1
            )
        )
        grad_rows = low(
            lax.dot_general(
                grad_pre, expert_in, (((1,), (1,)), ((), ())), preferred_element_type=jnp.float32
            )
        )
        grad_shared_act = dot(cot_all, shared_out_t)
        grad_shared_pre = low(
            jnp.concatenate(
                [silu_back(shared_gate, grad_shared_act * shared_up), grad_shared_act * shared_silu],
                axis=-1,
            )
        )
        partial, grad_rows, grad_shared_pre = tie((partial, grad_rows, grad_shared_pre))

        partial = scatter_two(partial)
        grad_hidden_part = give(grad_rows) + lax.dot_general(
            grad_shared_pre, shared_in, (((1,), (1,)), ((), ())), preferred_element_type=jnp.float32
        )
        partial, grad_hidden_part, grad_shared_pre, grad_pre, grad_part, cot_rows = tie(
            (partial, low(grad_hidden_part), grad_shared_pre, grad_pre, grad_part, cot_rows)
        )

        grad_partial = scatter_core(grad_hidden_part.reshape(nc, nz, tok, width))
        grad_partial, grad_shared_pre, grad_pre, grad_part = tie(
            (grad_partial, grad_shared_pre, grad_pre, grad_part)
        )
        output = low(resid + scatter_z(partial))
        grad_partial = scatter_one(grad_partial)
        grad_shared = low(
            jnp.concatenate([dot(hidden_all.T, grad_shared_pre), dot(cot_all.T, shared_act)], axis=-1)
        )
        grad_expert_out = dot(act.T, grad_part)
        grad_expert_in = dot(picked.T, grad_pre)
        grad_partial, grad_expert_out, grad_expert_in, grad_shared, cot_rows = tie(
            (grad_partial, grad_expert_out, grad_expert_in, grad_shared, cot_rows)
        )
        grad_partial = scatter_two(grad_partial)
        dots = jnp.sum(wide(cot_rows) * part, axis=-1).reshape(nd, cap, 1)
        dots = jnp.sum(jnp.where(pick, dots, 0.0), axis=1)
        dots = lax.all_to_all(dots, BOTH, split_axis=0, concat_axis=0, tiled=True)
        grad_gates = dots.reshape(experts, nd // experts, tok).sum(axis=1).T
        grad_logits = low(
            gates_dense
            * (grad_gates - jnp.sum(gates_dense * grad_gates, axis=-1, keepdims=True))
        )
        grad_router = dot(hidden.T, grad_logits)
        grad_hidden = scatter_z(grad_partial) + dot(grad_logits, router.T)
        grad_hidden, output = tie((grad_hidden, output))
        grad_mid, grad_gain_two = norm_back(grad_hidden, normed_second, scaling_second, gain_two)
        grad_resid = wide(cotangent[0]) + grad_mid

        grad_resid_seq = gather_context(low(grad_resid)).reshape(length, width)
        grad_mixed = dot(grad_resid_seq, out_t).reshape(length, hc, VD)
        grad_out_t = low(dot(grad_resid_seq.T, mixed))
        exchange = lambda table: lax.all_to_all(
            low(table).reshape(nd, rows, table.shape[-1]), BOTH, split_axis=0, concat_axis=0, tiled=True
        )
        early = exchange(jnp.concatenate([grad_shared, grad_out_t], axis=-1))
        scaled = low(grad_mixed / denom_rows)
        correction = (jnp.sum(grad_mixed * attended, axis=-1) / denominator.T).T
        grad_weights = ein("thv,nhv->htn", scaled, value)
        grad_raw = low(weights * (grad_weights - correction[:, :, None]) * scale)
        grad_nope = ein("htn,nhd->thd", grad_raw, key)
        grad_rot = ein("htn,nr->thr", grad_raw, rope_key)
        grad_key = ein("htn,thd->nhd", grad_raw, q_nope)
        grad_value = ein("htn,thv->nhv", weights_low, scaled)
        grad_rope = ein("htn,thr->nr", grad_raw, q_rope)
        grad_kv = low(jnp.concatenate([grad_key, grad_value], axis=-1).reshape(length, hc * (QKD + VD)))
        grad_up = dot(latent.T, grad_kv)
        grad_latent = lax.dot_general(
            grad_kv, up, (((1,), (1,)), ((), ())), preferred_element_type=jnp.float32
        )
        grad_latent_pre, grad_gain_latent = norm_back(
            grad_latent, normed_latent, scaling_latent, gain_latent
        )
        grad_compressed = low(
            jnp.concatenate([grad_latent_pre, rotary_back(grad_rope, cosine, sine)], axis=-1)
        )
        grad_query = low(
            jnp.concatenate(
                [
                    grad_nope.reshape(length, hc * QKD),
                    rotary_back(grad_rot, head_cos, head_sin).reshape(length, hc * RD),
                ],
                axis=-1,
            )
        )
        grad_query, grad_compressed, early = tie((grad_query, grad_compressed, early))
        query_back = exchange(dot(hidden_seq.T, grad_query))
        grad_down = low(dot(hidden_seq.T, grad_compressed))
        grad_first_part = low(
            lax.dot_general(
                grad_query, wq, (((1,), (1,)), ((), ())), preferred_element_type=jnp.float32
            )
            + lax.dot_general(
                grad_compressed, down, (((1,), (1,)), ((), ())), preferred_element_type=jnp.float32
            )
        )
        grad_first = scatter_context(grad_first_part.reshape(nc, tok, width))
        normed_first, scaling_first = normalize(wide(tokens[0]))
        grad_input, grad_gain_one = norm_back(grad_first, normed_first, scaling_first, gain_one)
        grad_input = grad_input + grad_resid

        shared_back = early[:, :, : 3 * pad].reshape(nd, rows, 3, pad)[..., :units]
        grad_wsi = wide(shared_back[:, :, :2].transpose(1, 2, 0, 3)).reshape(rows, 2 * SHARED)
        grad_wso = wide(shared_back[:, :, 2].transpose(0, 2, 1)).reshape(SHARED, rows)
        over_z = lambda table: wide(table).reshape(nc, nz, rows, -1).sum(axis=1)
        query_back = over_z(query_back)
        grad_wq = jnp.concatenate(
            [
                query_back[:, :, : hc * QKD].reshape(nc, rows, hc, QKD),
                query_back[:, :, hc * QKD :].reshape(nc, rows, hc, RD),
            ],
            axis=-1,
        ).transpose(1, 0, 2, 3).reshape(rows, HEADS * (QKD + RD))
        grad_wo = over_z(early[:, :, 3 * pad :]).transpose(0, 2, 1).reshape(HEADS * VD, rows)
        grad_down = grad_down.reshape(nc, nz, rows, LAT + RD)
        grad_wdkv = scatter_z(scatter_two(scatter_one(scatter_core(grad_down))))
        grad_wukv = scatter_z(low(grad_up).reshape(LAT, nz, -1).transpose(1, 0, 2))
        tiny = jnp.concatenate(
            [
                grad_gain_one.reshape(nd, rows),
                grad_gain_two.reshape(nd, rows),
                grad_router.reshape(nd, rows * experts),
                grad_gain_latent.reshape(nd, LAT // nd),
            ],
            axis=1,
        )
        tiny = lax.all_to_all(tiny, BOTH, split_axis=0, concat_axis=0, tiled=True).sum(axis=0)
        return (
            output[None],
            grad_input[None],
            tiny[:rows],
            grad_wq,
            grad_wdkv,
            tiny[2 * rows + rows * experts :],
            grad_wukv,
            grad_wo,
            tiny[rows : 2 * rows],
            tiny[2 * rows : 2 * rows + rows * experts].reshape(rows, experts),
            grad_wsi,
            grad_wso,
            grad_expert_in[None],
            grad_expert_out[None],
        )

    return body


def solution(mesh):
    placed = (
        P(EXP, CTX, None),
        P(BOTH),
        P(BOTH, None),
        P(BOTH, None),
        P(BOTH),
        P(None, BOTH),
        P(None, BOTH),
        P(BOTH),
        P(BOTH, None),
        P(BOTH, None),
        P(None, BOTH),
        P(BOTH, None, None),
        P(BOTH, None, None),
        P(EXP, CTX, None),
        P(EXP, CTX, None),
        P(EXP, CTX),
        P(EXP, CTX, None),
    )
    nc, nz = mesh.shape[CTX], mesh.shape[EXP]
    split = nc == 8 and nz == 4
    return jax.shard_map(
        fast_body(nc, nz) if split else body,
        mesh=mesh,
        in_specs=placed,
        out_specs=(
            P(EXP, CTX, None),
            P(EXP, CTX, None),
            P(BOTH),
            P(BOTH, None),
            P(BOTH, None),
            P(BOTH),
            P(None, BOTH),
            P(None, BOTH),
            P(BOTH),
            P(BOTH, None),
            P(BOTH, None),
            P(None, BOTH),
            P(BOTH, None, None),
            P(BOTH, None, None),
        ),
        check_vma=False,
    )
```

```python
import functools
import math

import jax
import jax.numpy as jnp
from jax import lax
from jax.sharding import PartitionSpec as P

HEADS = 16
QKD = 128
RD = 64
VD = 128
LAT = 512
TOP = 6
SHARED = 2816
HALF = 704
CTX = "context"
EXP = "expert"
BOTH = (CTX, EXP)


epsilon = 1e-06
highest = lax.Precision.HIGHEST


def normalize(values):
    scaling = lax.rsqrt(jnp.mean(values * values, axis=-1, keepdims=True) + epsilon)
    return (values * scaling, scaling)


def norm_back(grad_normed, normed, scaling, gain):
    grad_gain = jnp.sum(grad_normed * normed, axis=0)
    grad_unit = grad_normed * gain
    grad_values = scaling * (
        grad_unit - normed * jnp.mean(grad_unit * normed, axis=-1, keepdims=True)
    )
    return (grad_values, grad_gain)


def rotary(values, cosine, sine_table):
    middle = values.shape[-1] // 2
    first_half = values[..., :middle]
    second_half = values[..., middle:]
    return jnp.concatenate(
        [
            first_half * cosine - second_half * sine_table,
            second_half * cosine + first_half * sine_table,
        ],
        axis=-1,
    )


def rotary_back(grads_in, cosine, sine_table):
    middle = grads_in.shape[-1] // 2
    first_half = grads_in[..., :middle]
    second_half = grads_in[..., middle:]
    return jnp.concatenate(
        [
            first_half * cosine + second_half * sine_table,
            second_half * cosine - first_half * sine_table,
        ],
        axis=-1,
    )


def rotation_table(positions):
    exponent = jnp.arange(RD // 2, dtype=jnp.float32) * (2.0 / RD)
    angle_table = positions[:, None] * (10000.0 ** (-exponent))[None, :]
    return (jnp.cos(angle_table), jnp.sin(angle_table))


def silu_back(value, grads_in):
    sigma_value = jax.nn.sigmoid(value)
    return grads_in * sigma_value * (1.0 + value * (1.0 - sigma_value))


def head_scores(query_low, key_low, rope_low):
    nope_part = jnp.einsum(
        "thd,nhd->htn", query_low[..., :QKD], key_low, preferred_element_type=jnp.float32
    )
    rope_part = jnp.einsum(
        "thr,nr->htn", query_low[..., QKD:], rope_low, preferred_element_type=jnp.float32
    )
    return nope_part + rope_part


def both_halves(buffer_rows, experts_total, capacity):
    width = buffer_rows.shape[-1]
    shaped = buffer_rows.reshape(experts_total, 1, capacity, width)
    return jnp.broadcast_to(shaped, (experts_total, 2, capacity, width)).reshape(
        2 * experts_total, capacity, width
    )


def halves_sum(received, experts_total, capacity):
    width = received.shape[-1]
    return (
        received.astype(jnp.float32)
        .reshape(experts_total, 2, capacity, width)
        .sum(axis=1)
        .reshape(experts_total * capacity, width)
    )


def body(
    tokens,
    norm1_gain,
    w_query,
    w_down_kv,
    kv_gain,
    w_up_kv,
    w_attn_out,
    norm2_gain,
    w_router,
    w_shared_in,
    w_shared_out,
    w_expert_in,
    w_expert_out,
    routes,
    slots,
    blocks,
    cotangent,
):
    (
        gain_first,
        query_weight,
        down_weight,
        latent_gain,
        up_weight,
        out_weight,
        gain_second,
        router_weight,
        shared_in_weight,
        shared_out_weight,
    ) = (
        lax.all_gather(norm1_gain, BOTH, axis=0, tiled=True),
        lax.all_gather(w_query, BOTH, axis=0, tiled=True),
        lax.all_gather(w_down_kv, BOTH, axis=0, tiled=True),
        lax.all_gather(kv_gain, BOTH, axis=0, tiled=True),
        lax.all_gather(w_up_kv, BOTH, axis=1, tiled=True),
        lax.all_gather(w_attn_out, BOTH, axis=1, tiled=True),
        lax.all_gather(norm2_gain, BOTH, axis=0, tiled=True),
        lax.all_gather(w_router, BOTH, axis=0, tiled=True),
        lax.all_gather(w_shared_in, BOTH, axis=0, tiled=True),
        lax.all_gather(w_shared_out, BOTH, axis=1, tiled=True),
    )
    tok_count = tokens.shape[1]
    length_all = tok_count * lax.axis_size(CTX)
    experts_total = router_weight.shape[1]
    capacity = tok_count * TOP // experts_total * 4 // 3
    score_scale = (QKD + RD) ** (-0.5)
    residual_in = tokens[0].astype(jnp.float32)
    own_blocks = blocks[0]
    route_ids = routes[0]
    slot_ids = slots[0]
    positions = (lax.axis_index(CTX) * tok_count + jnp.arange(tok_count)).astype(jnp.float32)
    cosine, sine_table = rotation_table(positions)
    head_cos = cosine[:, None, :]
    head_sin = sine_table[:, None, :]
    gain_one = gain_first.astype(jnp.float32)
    gain_two = gain_second.astype(jnp.float32)
    gain_latent = latent_gain.astype(jnp.float32)
    normed_first, scaling_first = normalize(residual_in)
    hidden_first = (normed_first * gain_one).astype(jnp.bfloat16)
    query_pre = jnp.dot(hidden_first, query_weight, preferred_element_type=jnp.float32).reshape(
        tok_count, HEADS, QKD + RD
    )
    query_low = jnp.concatenate(
        [query_pre[..., :QKD], rotary(query_pre[..., QKD:], head_cos, head_sin)], axis=-1
    ).astype(jnp.bfloat16)
    compressed = jnp.dot(hidden_first, down_weight, preferred_element_type=jnp.float32)
    normed_latent, scaling_latent = normalize(compressed[:, :LAT])
    latent_low = (normed_latent * gain_latent).astype(jnp.bfloat16)
    rope_low = rotary(compressed[:, LAT:], cosine, sine_table).astype(jnp.bfloat16)
    key_value = jnp.dot(latent_low, up_weight, preferred_element_type=jnp.float32).astype(
        jnp.bfloat16
    )
    own_heads = key_value.reshape(tok_count, HEADS, QKD + VD)
    self_raw = jnp.einsum(
        "thd,thd->ht",
        query_low[..., :QKD],
        own_heads[..., :QKD],
        preferred_element_type=jnp.float32,
    ) + jnp.einsum("thr,tr->ht", query_low[..., QKD:], rope_low, preferred_element_type=jnp.float32)
    shift_table = jnp.floor(self_raw * score_scale)
    last_block = jnp.max(own_blocks)

    def block_weights(kv_piece, rope_piece, blocks_piece):
        kv_heads = kv_piece.reshape(kv_piece.shape[0], HEADS, QKD + VD)
        raw_scores = head_scores(query_low, kv_heads[..., :QKD], rope_piece)
        allowed = (blocks_piece[None, :] <= own_blocks[:, None])[None]
        shifted = jnp.where(allowed, raw_scores * score_scale - shift_table[:, :, None], 0.0)
        return (kv_heads, jnp.where(allowed, jnp.exp(shifted), 0.0))

    empty_state = (
        jnp.zeros((tok_count, HEADS, VD), jnp.float32),
        jnp.zeros((HEADS, tok_count), jnp.float32),
    )
    kv_piece = lax.all_gather(key_value, CTX, axis=0, tiled=True)
    rope_piece = lax.all_gather(rope_low, CTX, axis=0, tiled=True)
    blocks_piece = lax.all_gather(own_blocks, CTX, axis=0, tiled=True)
    make_kv = lambda: kv_piece

    def attend_compute(state_now):
        kv_heads, weights = block_weights(make_kv(), rope_piece, blocks_piece)
        running = jnp.einsum(
            "htn,nhv->thv",
            weights.astype(jnp.bfloat16),
            kv_heads[..., QKD:],
            preferred_element_type=jnp.float32,
        )
        return (running, jnp.sum(weights, axis=-1))

    running, denominator = lax.cond(
        jnp.min(blocks_piece) > last_block, lambda state_now: state_now, attend_compute, empty_state
    )
    denom_rows = jnp.transpose(denominator)
    attended = running / denom_rows[:, :, None]
    mixed_low = attended.reshape(tok_count, HEADS * VD).astype(jnp.bfloat16)
    residual_mid = residual_in + jnp.dot(mixed_low, out_weight, preferred_element_type=jnp.float32)
    normed_second, scaling_second = normalize(residual_mid)
    hidden_second = (normed_second * gain_two).astype(jnp.bfloat16)
    logits = jnp.dot(hidden_second, router_weight, preferred_element_type=jnp.float32)
    route_onehot = (route_ids[:, :, None] == jnp.arange(experts_total)[None, None, :]).astype(
        jnp.float32
    )
    chosen = jnp.sum(route_onehot * logits[:, None, :], axis=-1)
    gate_weights = jax.nn.softmax(chosen, axis=-1)
    shared_pre = jnp.dot(hidden_second, shared_in_weight, preferred_element_type=jnp.float32)
    shared_act = (jax.nn.silu(shared_pre[:, :SHARED]) * shared_pre[:, SHARED:]).astype(jnp.bfloat16)
    shared_result = jnp.dot(shared_act, shared_out_weight, preferred_element_type=jnp.float32)
    slot_index = (route_ids * capacity + slot_ids).reshape(-1)
    model_width = hidden_second.shape[1]
    repeated = jnp.broadcast_to(hidden_second[:, None, :], (tok_count, TOP, model_width)).reshape(
        tok_count * TOP, model_width
    )
    send_rows = (
        jnp.zeros((experts_total * capacity, model_width), jnp.bfloat16)
        .at[slot_index]
        .set(repeated)
    )
    weight_in_local = w_expert_in[0]
    weight_out_local = w_expert_out[0]
    received = lax.all_to_all(
        both_halves(send_rows, experts_total, capacity),
        BOTH,
        split_axis=0,
        concat_axis=0,
        tiled=True,
    )
    pre_expert = jnp.einsum(
        "scd,df->scf", received, weight_in_local, preferred_element_type=jnp.float32
    )
    activation = (jax.nn.silu(pre_expert[..., :HALF]) * pre_expert[..., HALF:]).astype(jnp.bfloat16)
    part_rows = jnp.einsum(
        "scf,fd->scd", activation, weight_out_local, preferred_element_type=jnp.float32
    ).astype(jnp.bfloat16)
    returned = lax.all_to_all(
        part_rows, BOTH, split_axis=0, concat_axis=0, tiled=True
    )
    returned, received_rows, pre_expert = (returned, received, pre_expert)
    expert_table = halves_sum(returned, experts_total, capacity)
    picked = expert_table[slot_index].reshape(tok_count, TOP, model_width)
    routed = jnp.sum(gate_weights[:, :, None] * picked, axis=1)
    output_low = (residual_mid + shared_result + routed).astype(jnp.bfloat16)
    grad_low = cotangent[0]
    grad_out = grad_low.astype(jnp.float32)
    grad_shared_out = jnp.dot(shared_act.T, grad_low, preferred_element_type=jnp.float32)
    grad_shared_act = jnp.dot(grad_low, shared_out_weight.T, preferred_element_type=jnp.float32)
    shared_gate = shared_pre[:, :SHARED]
    shared_up = shared_pre[:, SHARED:]
    grad_shared_pre = jnp.concatenate(
        [
            silu_back(shared_gate, grad_shared_act * shared_up),
            grad_shared_act * jax.nn.silu(shared_gate),
        ],
        axis=-1,
    ).astype(jnp.bfloat16)
    grad_shared_in = jnp.dot(hidden_second.T, grad_shared_pre, preferred_element_type=jnp.float32)
    grad_hidden = jnp.dot(grad_shared_pre, shared_in_weight.T, preferred_element_type=jnp.float32)
    grad_gates = jnp.sum(grad_out[:, None, :] * picked, axis=-1)
    grad_chosen = gate_weights * (
        grad_gates - jnp.sum(gate_weights * grad_gates, axis=-1, keepdims=True)
    )
    grad_logits = jnp.sum(route_onehot * grad_chosen[:, :, None], axis=1).astype(jnp.bfloat16)
    grad_router = jnp.dot(hidden_second.T, grad_logits, preferred_element_type=jnp.float32)
    grad_hidden = grad_hidden + jnp.dot(
        grad_logits, router_weight.T, preferred_element_type=jnp.float32
    )
    grad_parts = (
        (gate_weights[:, :, None] * grad_out[:, None, :])
        .astype(jnp.bfloat16)
        .reshape(tok_count * TOP, model_width)
    )
    grad_send = (
        jnp.zeros((experts_total * capacity, model_width), jnp.bfloat16)
        .at[slot_index]
        .set(grad_parts)
    )
    grad_received = lax.all_to_all(
        both_halves(grad_send, experts_total, capacity),
        BOTH,
        split_axis=0,
        concat_axis=0,
        tiled=True,
    )
    expert_gate = pre_expert[..., :HALF]
    expert_up = pre_expert[..., HALF:]
    expert_silu = jax.nn.silu(expert_gate)
    expert_act = (expert_silu * expert_up).astype(jnp.bfloat16)
    grad_expert_out = jnp.einsum(
        "scf,scd->fd", expert_act, grad_received, preferred_element_type=jnp.float32
    )
    grad_expert_act = jnp.einsum(
        "scd,fd->scf", grad_received, weight_out_local, preferred_element_type=jnp.float32
    )
    grad_expert_pre = jnp.concatenate(
        [silu_back(expert_gate, grad_expert_act * expert_up), grad_expert_act * expert_silu],
        axis=-1,
    ).astype(jnp.bfloat16)
    grad_expert_in = jnp.einsum(
        "scd,scf->df", received_rows, grad_expert_pre, preferred_element_type=jnp.float32
    )
    grad_rows = jnp.einsum(
        "scf,df->scd", grad_expert_pre, weight_in_local, preferred_element_type=jnp.float32
    )
    grad_back = lax.all_to_all(
        grad_rows.astype(jnp.bfloat16),
        BOTH,
        split_axis=0,
        concat_axis=0,
        tiled=True,
    ).astype(grad_rows.dtype)
    grad_table = halves_sum(grad_back, experts_total, capacity)
    grad_hidden = grad_hidden + jnp.sum(
        grad_table[slot_index].reshape(tok_count, TOP, model_width), axis=1
    )
    grad_mid_norm, grad_gain_second = norm_back(
        grad_hidden, normed_second, scaling_second, gain_two
    )
    grad_resid = grad_out + grad_mid_norm
    grad_resid_low = grad_resid.astype(jnp.bfloat16)
    grad_attn_out = jnp.dot(mixed_low.T, grad_resid_low, preferred_element_type=jnp.float32)
    grad_mixed = jnp.dot(grad_resid_low, out_weight.T, preferred_element_type=jnp.float32).reshape(
        tok_count, HEADS, VD
    )
    scaled_low = (grad_mixed / denom_rows[:, :, None]).astype(jnp.bfloat16)
    correction = jnp.transpose(jnp.sum(grad_mixed * attended, axis=-1) / denom_rows)
    full_kv, full_rope, full_blocks, full_latent = (
        lax.all_gather(key_value, CTX, axis=0, tiled=True),
        lax.all_gather(rope_low, CTX, axis=0, tiled=True),
        lax.all_gather(own_blocks, CTX, axis=0, tiled=True),
        lax.all_gather(latent_low, CTX, axis=0, tiled=True),
    )
    key_block = math.gcd(length_all, 512)
    block_count = length_all // key_block
    kv_width = HEADS * (QKD + VD)

    def key_step(grad_query, block_index):
        begin_row = block_index * key_block
        kv_piece = lax.dynamic_slice_in_dim(full_kv, begin_row, key_block, 0)
        rope_piece = lax.dynamic_slice_in_dim(full_rope, begin_row, key_block, 0)
        blocks_piece = lax.dynamic_slice_in_dim(full_blocks, begin_row, key_block, 0)

        def key_compute(grad_acc):
            kv_heads, weights = block_weights(kv_piece, rope_piece, blocks_piece)
            grad_weights = jnp.einsum(
                "thv,nhv->htn", scaled_low, kv_heads[..., QKD:], preferred_element_type=jnp.float32
            )
            grad_raw = (weights * (grad_weights - correction[:, :, None]) * score_scale).astype(
                jnp.bfloat16
            )
            grad_nope = jnp.einsum(
                "htn,nhd->thd", grad_raw, kv_heads[..., :QKD], preferred_element_type=jnp.float32
            )
            grad_rot = jnp.einsum(
                "htn,nr->thr", grad_raw, rope_piece, preferred_element_type=jnp.float32
            )
            grad_key = jnp.einsum(
                "htn,thd->nhd", grad_raw, query_low[..., :QKD], preferred_element_type=jnp.float32
            )
            grad_value = jnp.einsum(
                "htn,thv->nhv",
                weights.astype(jnp.bfloat16),
                scaled_low,
                preferred_element_type=jnp.float32,
            )
            grad_rope = jnp.einsum(
                "htn,thr->nr", grad_raw, query_low[..., QKD:], preferred_element_type=jnp.float32
            )
            grad_kv = jnp.concatenate([grad_key, grad_value], axis=-1).reshape(key_block, kv_width)
            return (grad_acc + jnp.concatenate([grad_nope, grad_rot], axis=-1), grad_kv, grad_rope)

        def skipped(grad_acc):
            return (
                grad_acc,
                jnp.zeros((key_block, kv_width), jnp.float32),
                jnp.zeros((key_block, RD), jnp.float32),
            )

        grad_query, grad_kv, grad_rope = lax.cond(
            jnp.min(blocks_piece) > last_block, skipped, key_compute, grad_query
        )
        return (grad_query, (grad_kv, grad_rope))

    grad_query_rot, (grad_kv_blocks, grad_rope_blocks) = lax.scan(
        key_step, jnp.zeros((tok_count, HEADS, QKD + RD), jnp.float32), jnp.arange(block_count)
    )
    partial_kv = grad_kv_blocks.reshape(length_all, kv_width)
    partial_rope = grad_rope_blocks.reshape(length_all, RD)
    up_float = up_weight.astype(jnp.float32)
    kv_sum, rope_sum = (
        lax.psum_scatter(
            partial_kv.astype(jnp.bfloat16), CTX, scatter_dimension=0, tiled=True
        ).astype(jnp.float32),
        lax.psum_scatter(
            partial_rope.astype(jnp.bfloat16), CTX, scatter_dimension=0, tiled=True
        ).astype(jnp.float32),
    )
    grad_up_kv = jnp.dot(
        latent_low.astype(jnp.float32).T,
        kv_sum,
        precision=highest,
        preferred_element_type=jnp.float32,
    )
    grad_latent = jnp.dot(kv_sum, up_float.T, precision=highest, preferred_element_type=jnp.float32)
    grad_latent_pre, grad_gain_latent = norm_back(
        grad_latent, normed_latent, scaling_latent, gain_latent
    )
    grad_compressed = jnp.concatenate(
        [grad_latent_pre, rotary_back(rope_sum, cosine, sine_table)], axis=-1
    ).astype(jnp.bfloat16)
    grad_down_kv = jnp.dot(hidden_first.T, grad_compressed, preferred_element_type=jnp.float32)
    grad_query_low = (
        jnp.concatenate(
            [grad_query_rot[..., :QKD], rotary_back(grad_query_rot[..., QKD:], head_cos, head_sin)],
            axis=-1,
        )
        .astype(jnp.bfloat16)
        .reshape(tok_count, HEADS * (QKD + RD))
    )
    grad_query_weight = jnp.dot(hidden_first.T, grad_query_low, preferred_element_type=jnp.float32)
    grad_hidden_first = jnp.dot(
        grad_query_low, query_weight.T, preferred_element_type=jnp.float32
    ) + jnp.dot(grad_compressed, down_weight.T, preferred_element_type=jnp.float32)
    grad_first_norm, grad_gain_first = norm_back(
        grad_hidden_first, normed_first, scaling_first, gain_one
    )
    grad_input = grad_resid + grad_first_norm
    (
        grad_norm_one,
        grad_wq,
        grad_wdkv,
        grad_gkv,
        grad_wukv,
        grad_wo,
        grad_norm_two,
        grad_wr,
        grad_wsi,
        grad_wso,
    ) = (
        lax.psum_scatter(grad_gain_first, BOTH, scatter_dimension=0, tiled=True),
        lax.psum_scatter(grad_query_weight, BOTH, scatter_dimension=0, tiled=True),
        lax.psum_scatter(grad_down_kv, BOTH, scatter_dimension=0, tiled=True),
        lax.psum_scatter(grad_gain_latent, BOTH, scatter_dimension=0, tiled=True),
        lax.psum_scatter(grad_up_kv, BOTH, scatter_dimension=1, tiled=True),
        lax.psum_scatter(grad_attn_out, BOTH, scatter_dimension=1, tiled=True),
        lax.psum_scatter(grad_gain_second, BOTH, scatter_dimension=0, tiled=True),
        lax.psum_scatter(grad_router, BOTH, scatter_dimension=0, tiled=True),
        lax.psum_scatter(grad_shared_in, BOTH, scatter_dimension=0, tiled=True),
        lax.psum_scatter(grad_shared_out, BOTH, scatter_dimension=1, tiled=True),
    )
    return (
        output_low[None],
        grad_input[None],
        grad_norm_one,
        grad_wq,
        grad_wdkv,
        grad_gkv,
        grad_wukv,
        grad_wo,
        grad_norm_two,
        grad_wr,
        grad_wsi,
        grad_wso,
        grad_expert_in[None],
        grad_expert_out[None],
    )


low = lambda v: v.astype(jnp.bfloat16)
wide = lambda v: v.astype(jnp.float32)


def place():
    index = lax.axis_index(CTX)
    return index % 2, index // 2 % 2, index // 4, lax.axis_index(EXP)


def swap(values, bit):
    return lax.ppermute(values, CTX, [(i, i ^ bit) for i in range(8)])


def shift_z(values, step):
    return lax.ppermute(values, EXP, [(i, (i + step) % 4) for i in range(4)])


def entry(values, index, axis):
    return lax.dynamic_index_in_dim(values, index, axis, keepdims=False)


def join(mine, got, bit, axis):
    return jnp.concatenate(
        [jnp.where(bit == 0, mine, got), jnp.where(bit == 0, got, mine)], axis
    )


def gather_z(values):
    z = lax.axis_index(EXP)
    parts = [values] + [shift_z(values, step) for step in (2, 1, 3)]
    order = (0, 2, 1, 3)

    def chunk(j):
        ahead = (z - j) % 4
        out = parts[0]
        for step in (1, 2, 3):
            out = jnp.where(ahead == step, parts[order[step]], out)
        return out

    return jnp.stack([chunk(j) for j in range(4)])


def gather_xy(values, x_first):
    _, x, y, _ = place()
    values = values[None, None]
    if x_first:
        values = join(values, swap(values, 2), x, 1)
        return join(values, swap(values, 4), y, 0)
    values = join(values, swap(values, 4), y, 0)
    return join(values, swap(values, 2), x, 1)


def gather_context(values):
    core = place()[0]
    axis = values.ndim - 2
    cut = values.shape[axis] // 2
    first = lax.slice_in_dim(values, 0, cut, axis=axis)
    second = lax.slice_in_dim(values, cut, 2 * cut, axis=axis)
    both = jnp.concatenate([gather_xy(first, True), gather_xy(second, False)], axis + 2)
    both = both[:, :, None]
    both = join(both, swap(both, 1), core, 2)
    return both.reshape((8,) + values.shape)


def gather_all(values):
    return gather_context(gather_z(values)).reshape((32,) + values.shape)


def gather_small(values):
    core, x, y, _ = place()
    out = gather_z(values)[None]
    out = join(out, swap(out, 1), core, 0)
    out = join(out, swap(out, 2), x, 0)
    out = join(out, swap(out, 4), y, 0)
    return out.reshape((32,) + values.shape)


def halve(values, axis, mine, bit):
    got = swap(entry(values, 1 - mine, axis), bit)
    return low(wide(entry(values, mine, axis)) + wide(got))


def scatter_core(values):
    return halve(values.reshape((2, 2, 2) + values.shape[1:]), 2, place()[0], 1)


def scatter_one(values):
    _, x, y, _ = place()
    axis = values.ndim - 2
    cut = values.shape[axis] // 2
    first = lax.slice_in_dim(values, 0, cut, axis=axis)
    second = lax.slice_in_dim(values, cut, 2 * cut, axis=axis)
    return halve(first, 1, x, 2), halve(second, 0, y, 4)


def scatter_two(pair):
    _, x, y, _ = place()
    pair = (halve(pair[0], 0, y, 4), halve(pair[1], 0, x, 2))
    return jnp.concatenate(pair, pair[0].ndim - 2)


def scatter_context(values):
    return wide(scatter_two(scatter_one(scatter_core(values))))


def scatter_z(values):
    z = lax.axis_index(EXP)
    out = wide(entry(values, z, 0))
    for step in (2, 1, 3):
        out = out + wide(shift_z(entry(values, (z + step) % 4, 0), step))
    return out


tie = lax.optimization_barrier


def fast_body(nc, nz):
    nd = nc * nz
    hc = HEADS // nc
    qw = hc * (QKD + RD)
    ow = hc * VD
    units = SHARED // nd
    pad = -(-units // 128) * 128
    dot = functools.partial(jnp.dot, preferred_element_type=jnp.float32)
    ein = functools.partial(jnp.einsum, preferred_element_type=jnp.float32)

    def body(
        tokens, norm1_gain, w_query, w_down_kv, kv_gain, w_up_kv, w_attn_out, norm2_gain, w_router,
        w_shared_in, w_shared_out, w_expert_in, w_expert_out, routes, slots, blocks, cotangent,
    ):
        device = lax.axis_index(CTX) * nz + lax.axis_index(EXP)
        my_expert = device // 2
        tok = tokens.shape[1]
        width = tokens.shape[2]
        rows = width // nd
        length = tok * nc
        total = tok * nd
        experts = w_router.shape[1]
        cap = tok * TOP // experts * 4 // 3
        scale = (QKD + RD) ** (-0.5)

        small = jnp.concatenate(
            [norm1_gain, norm2_gain, w_router.reshape(-1), kv_gain]
            + [low(v).reshape(-1) for v in (routes, slots, blocks)]
        )
        parts = -(-small.shape[0] // 2048)
        small = jnp.pad(small, (0, 2048 * parts - small.shape[0])).reshape(16 * parts, 128)
        small = gather_small(small).reshape(nd, 2048 * parts)
        gain_one = wide(small[:, :rows].reshape(-1))
        gain_two = wide(small[:, rows : 2 * rows].reshape(-1))
        router = small[:, 2 * rows : 2 * rows + rows * experts].reshape(width, experts)
        begin = 2 * rows + rows * experts
        gain_latent = wide(small[:, begin : begin + LAT // nd].reshape(-1))
        begin += LAT // nd
        route_all = small[:, begin : begin + tok * TOP].reshape(nd, tok, TOP).astype(jnp.int32)
        begin += tok * TOP
        slot_all = small[:, begin : begin + tok * TOP].reshape(nd, tok, TOP).astype(jnp.int32)
        begin += tok * TOP
        block_all = small[:, begin : begin + tok].reshape(nc, nz, tok)
        block_seq = entry(block_all, lax.axis_index(EXP), 1).reshape(-1)
        tok_seq = gather_context(tokens[0]).reshape(length, width)
        down = lax.all_gather(w_down_kv, BOTH, axis=0, tiled=True)
        wq = w_query.reshape(rows, nc, hc, QKD + RD)
        wq = jnp.concatenate(
            [
                wq[..., :QKD].reshape(rows, nc, hc * QKD),
                wq[..., QKD:].reshape(rows, nc, hc * RD),
                w_attn_out.T.reshape(rows, nc, ow),
            ],
            axis=-1,
        ).transpose(1, 0, 2)
        wq = lax.all_to_all(wq, CTX, split_axis=0, concat_axis=0, tiled=True)
        wq = gather_z(wq).transpose(1, 0, 2, 3).reshape(width, qw + ow)
        out_t = wq[:, qw:]
        wq = wq[:, :qw]
        up = gather_z(w_up_kv).transpose(1, 0, 2).reshape(LAT, -1)
        shared = jnp.stack(
            [
                w_shared_in[:, :SHARED].reshape(rows, nd, units),
                w_shared_in[:, SHARED:].reshape(rows, nd, units),
                w_shared_out.T.reshape(rows, nd, units),
            ],
            axis=2,
        )
        shared = jnp.pad(shared, ((0, 0), (0, 0), (0, 0), (0, pad - units)))
        shared = shared.transpose(1, 0, 2, 3).reshape(nd, rows, 3 * pad)
        shared, wq, up = tie((shared, wq, up))
        shared = lax.all_to_all(shared, BOTH, split_axis=0, concat_axis=0, tiled=True)
        shared = shared.reshape(width, 3 * pad)
        shared = jnp.concatenate(
            [shared[:, :units], router, shared[:, units + experts :]], axis=-1
        )

        cosine, sine = rotation_table(jnp.arange(length, dtype=jnp.float32))
        head_cos, head_sin = cosine[:, None, :], sine[:, None, :]
        normed_seq, _ = normalize(wide(tok_seq))
        hidden_seq = low(normed_seq * gain_one)
        query = dot(hidden_seq, wq)
        q_nope = low(query[:, : hc * QKD]).reshape(length, hc, QKD)
        q_rope = low(rotary(query[:, hc * QKD :].reshape(length, hc, RD), head_cos, head_sin))
        compressed = dot(hidden_seq, down)
        normed_latent, scaling_latent = normalize(compressed[:, :LAT])
        latent = low(normed_latent * gain_latent)
        rope_key = low(rotary(compressed[:, LAT:], cosine, sine))
        key_value = low(dot(latent, up)).reshape(length, hc, QKD + VD)
        key, value = key_value[..., :QKD], key_value[..., QKD:]
        raw = ein("thd,nhd->htn", q_nope, key) + ein("thr,nr->htn", q_rope, rope_key)
        self_raw = jnp.sum(wide(q_nope) * wide(key), axis=-1) + jnp.sum(
            wide(q_rope) * wide(rope_key)[:, None, :], axis=-1
        )
        shift = jnp.floor(self_raw * scale).T
        allowed = (block_seq[None, :] <= block_seq[:, None])[None]
        weights = jnp.where(
            allowed, jnp.exp(jnp.where(allowed, raw * scale - shift[:, :, None], 0.0)), 0.0
        )
        weights_low = low(weights)
        denominator = jnp.sum(weights, axis=-1)
        denom_rows = denominator.T[:, :, None]
        attended = ein("htn,nhv->thv", weights_low, value) / denom_rows
        mixed = low(attended.reshape(length, ow))
        resid_part = low(lax.dot_general(mixed, out_t, (((1,), (1,)), ((), ())),
                                         preferred_element_type=jnp.float32))
        resid_part, shared = tie((resid_part, shared))
        shared_in = shared[:, : 2 * pad]
        shared_out_t = shared[:, 2 * pad :]
        resid = wide(tokens[0]) + scatter_context(resid_part.reshape(nc, tok, width))

        normed_second, scaling_second = normalize(resid)
        hidden = low(normed_second * gain_two)
        logits = dot(hidden, router)
        onehot = wide(routes[0][:, :, None] == jnp.arange(experts)[None, None, :])
        gates = jax.nn.softmax(jnp.sum(onehot * logits[:, None, :], axis=-1), axis=-1)
        gates_dense = jnp.sum(onehot * gates[:, :, None], axis=1)
        hidden_all = lax.all_gather(hidden, BOTH, axis=0, tiled=True)
        hidden_all, cot_own = tie((hidden_all, cotangent[0]))
        cot_all = lax.all_gather(cot_own, BOTH, axis=0, tiled=True)

        named = route_all == my_expert
        slot_of = jnp.max(jnp.where(named, slot_all, -1), axis=-1)
        pick = slot_of[:, None, :] == jnp.arange(cap)[None, :, None]
        pick_low = low(pick)
        shared_pre = dot(hidden_all, shared_in)
        logits_all = shared_pre[:, units : units + experts]
        chosen = jnp.max(
            wide(route_all.reshape(total, TOP, 1) == jnp.arange(experts)[None, None, :]), axis=1
        )
        gates_all = jax.nn.softmax(jnp.where(chosen > 0, logits_all, -jnp.inf), axis=-1)
        gate_col = jnp.sum(
            jnp.where(jnp.arange(experts)[None, :] == my_expert, gates_all, 0.0), axis=1
        ).reshape(nd, 1, tok)
        gate_rows = jnp.sum(jnp.where(pick, gate_col, 0.0), axis=-1).reshape(nd * cap, 1)
        take = lambda table: low(ein("bst,btd->bsd", pick_low, table.reshape(nd, tok, width))).reshape(
            nd * cap, width
        )

        def portion(which, table, act, weight):
            part_of = lambda t: entry(t.reshape(2, 2, 2, -1, t.shape[-1]), which, 2)
            picks = part_of(pick_low).reshape(-1, cap, tok)
            routed = ein("bst,bsd->btd", picks, part_of(table).reshape(-1, cap, width))
            return wide(low(routed)).reshape(-1, width) + lax.dot_general(
                part_of(act).reshape(-1, act.shape[-1]),
                weight,
                (((1,), (1,)), ((), ())),
                preferred_element_type=jnp.float32,
            )

        def reduce_core(table, act, weight):
            core = place()[0]
            got = swap(low(portion(1 - core, table, act, weight)), 1)
            return low(portion(core, table, act, weight) + wide(got)).reshape(2, 2, nz, tok, width)

        expert_in, expert_out = w_expert_in[0], w_expert_out[0]
        picked = take(hidden_all)
        pre = dot(picked, expert_in)
        expert_gate, expert_up = pre[:, :HALF], pre[:, HALF:]
        expert_silu = jax.nn.silu(expert_gate)
        act = low(expert_silu * expert_up)
        part = wide(low(dot(act, expert_out)))
        shared_gate, shared_up = shared_pre[:, :pad], shared_pre[:, pad:]
        shared_silu = jax.nn.silu(shared_gate)
        shared_act = low(shared_silu * shared_up)
        partial = reduce_core(low(part * gate_rows), shared_act, shared_out_t)

        partial, cot_all = tie((partial, cot_all))
        partial = scatter_one(partial)
        cot_rows = take(cot_all)
        grad_part = low(wide(cot_rows) * gate_rows)
        grad_shared_act = dot(cot_all, shared_out_t)
        grad_shared_pre = low(
            jnp.concatenate(
                [silu_back(shared_gate, grad_shared_act * shared_up), grad_shared_act * shared_silu],
                axis=-1,
            )
        )
        partial, cot_rows, grad_part, grad_shared_pre = tie(
            (partial, cot_rows, grad_part, grad_shared_pre)
        )

        partial = scatter_two(partial)
        grad_act = lax.dot_general(
            grad_part, expert_out, (((1,), (1,)), ((), ())), preferred_element_type=jnp.float32
        )
        grad_pre = low(
            jnp.concatenate(
                [silu_back(expert_gate, grad_act * expert_up), grad_act * expert_silu], axis=-1
            )
        )
        grad_rows = low(
            lax.dot_general(
                grad_pre, expert_in, (((1,), (1,)), ((), ())), preferred_element_type=jnp.float32
            )
        )
        partial, grad_rows, grad_shared_pre, grad_pre, grad_part, cot_rows = tie(
            (partial, grad_rows, grad_shared_pre, grad_pre, grad_part, cot_rows)
        )

        output = low(resid + scatter_z(partial))
        grad_partial = reduce_core(grad_rows, grad_shared_pre, shared_in)
        grad_partial, grad_shared_pre, grad_pre, grad_part = tie(
            (grad_partial, grad_shared_pre, grad_pre, grad_part)
        )
        grad_partial = scatter_one(grad_partial)
        grad_shared = low(
            jnp.concatenate([dot(hidden_all.T, grad_shared_pre), dot(cot_all.T, shared_act)], axis=-1)
        )
        grad_expert_out = dot(act.T, grad_part)
        grad_expert_in = dot(picked.T, grad_pre)
        grad_partial, grad_expert_out, grad_expert_in, grad_shared, cot_rows = tie(
            (grad_partial, grad_expert_out, grad_expert_in, grad_shared, cot_rows)
        )
        grad_partial = scatter_two(grad_partial)
        dots = jnp.sum(wide(cot_rows) * part, axis=-1).reshape(nd, cap, 1)
        dots = jnp.sum(jnp.where(pick, dots, 0.0), axis=1)
        dots = lax.all_to_all(dots, BOTH, split_axis=0, concat_axis=0, tiled=True)
        grad_gates = dots.reshape(experts, nd // experts, tok).sum(axis=1).T
        grad_logits = low(
            gates_dense
            * (grad_gates - jnp.sum(gates_dense * grad_gates, axis=-1, keepdims=True))
        )
        grad_router = dot(hidden.T, grad_logits)
        grad_hidden = scatter_z(grad_partial) + dot(grad_logits, router.T)
        grad_hidden, output = tie((grad_hidden, output))
        grad_mid, grad_gain_two = norm_back(grad_hidden, normed_second, scaling_second, gain_two)
        grad_resid = wide(cotangent[0]) + grad_mid

        grad_resid_seq = gather_context(low(grad_resid)).reshape(length, width)
        grad_mixed = dot(grad_resid_seq, out_t).reshape(length, hc, VD)
        grad_out_t = low(dot(grad_resid_seq.T, mixed))
        exchange = lambda table: lax.all_to_all(
            low(table).reshape(nd, rows, table.shape[-1]), BOTH, split_axis=0, concat_axis=0, tiled=True
        )
        early = exchange(jnp.concatenate([grad_shared, grad_out_t], axis=-1))
        scaled = low(grad_mixed / denom_rows)
        correction = (jnp.sum(grad_mixed * attended, axis=-1) / denominator.T).T
        grad_weights = ein("thv,nhv->htn", scaled, value)
        grad_raw = low(weights * (grad_weights - correction[:, :, None]) * scale)
        grad_nope = ein("htn,nhd->thd", grad_raw, key)
        grad_rot = ein("htn,nr->thr", grad_raw, rope_key)
        grad_key = ein("htn,thd->nhd", grad_raw, q_nope)
        grad_value = ein("htn,thv->nhv", weights_low, scaled)
        grad_rope = ein("htn,thr->nr", grad_raw, q_rope)
        grad_kv = low(jnp.concatenate([grad_key, grad_value], axis=-1).reshape(length, hc * (QKD + VD)))
        grad_up = dot(latent.T, grad_kv)
        grad_latent = lax.dot_general(
            grad_kv, up, (((1,), (1,)), ((), ())), preferred_element_type=jnp.float32
        )
        grad_latent_pre, grad_gain_latent = norm_back(
            grad_latent, normed_latent, scaling_latent, gain_latent
        )
        grad_compressed = low(
            jnp.concatenate([grad_latent_pre, rotary_back(grad_rope, cosine, sine)], axis=-1)
        )
        grad_query = low(
            jnp.concatenate(
                [
                    grad_nope.reshape(length, hc * QKD),
                    rotary_back(grad_rot, head_cos, head_sin).reshape(length, hc * RD),
                ],
                axis=-1,
            )
        )
        grad_query, grad_compressed, early = tie((grad_query, grad_compressed, early))
        query_back = exchange(dot(hidden_seq.T, grad_query))
        grad_down = low(dot(hidden_seq.T, grad_compressed))
        grad_first_part = low(
            lax.dot_general(
                grad_query, wq, (((1,), (1,)), ((), ())), preferred_element_type=jnp.float32
            )
            + lax.dot_general(
                grad_compressed, down, (((1,), (1,)), ((), ())), preferred_element_type=jnp.float32
            )
        )
        grad_first = scatter_context(grad_first_part.reshape(nc, tok, width))
        normed_first, scaling_first = normalize(wide(tokens[0]))
        grad_input, grad_gain_one = norm_back(grad_first, normed_first, scaling_first, gain_one)
        grad_input = grad_input + grad_resid

        shared_back = early[:, :, : 3 * pad].reshape(nd, rows, 3, pad)[..., :units]
        grad_wsi = wide(shared_back[:, :, :2].transpose(1, 2, 0, 3)).reshape(rows, 2 * SHARED)
        grad_wso = wide(shared_back[:, :, 2].transpose(0, 2, 1)).reshape(SHARED, rows)
        over_z = lambda table: wide(table).reshape(nc, nz, rows, -1).sum(axis=1)
        query_back = over_z(query_back)
        grad_wq = jnp.concatenate(
            [
                query_back[:, :, : hc * QKD].reshape(nc, rows, hc, QKD),
                query_back[:, :, hc * QKD :].reshape(nc, rows, hc, RD),
            ],
            axis=-1,
        ).transpose(1, 0, 2, 3).reshape(rows, HEADS * (QKD + RD))
        grad_wo = over_z(early[:, :, 3 * pad :]).transpose(0, 2, 1).reshape(HEADS * VD, rows)
        grad_down = grad_down.reshape(nc, nz, rows, LAT + RD)
        grad_wdkv = scatter_z(scatter_two(scatter_one(scatter_core(grad_down))))
        grad_wukv = scatter_z(low(grad_up).reshape(LAT, nz, -1).transpose(1, 0, 2))
        tiny = jnp.concatenate(
            [
                grad_gain_one.reshape(nd, rows),
                grad_gain_two.reshape(nd, rows),
                grad_router.reshape(nd, rows * experts),
                grad_gain_latent.reshape(nd, LAT // nd),
            ],
            axis=1,
        )
        tiny = lax.all_to_all(tiny, BOTH, split_axis=0, concat_axis=0, tiled=True).sum(axis=0)
        return (
            output[None],
            grad_input[None],
            tiny[:rows],
            grad_wq,
            grad_wdkv,
            tiny[2 * rows + rows * experts :],
            grad_wukv,
            grad_wo,
            tiny[rows : 2 * rows],
            tiny[2 * rows : 2 * rows + rows * experts].reshape(rows, experts),
            grad_wsi,
            grad_wso,
            grad_expert_in[None],
            grad_expert_out[None],
        )

    return body


def solution(mesh):
    placed = (
        P(EXP, CTX, None),
        P(BOTH),
        P(BOTH, None),
        P(BOTH, None),
        P(BOTH),
        P(None, BOTH),
        P(None, BOTH),
        P(BOTH),
        P(BOTH, None),
        P(BOTH, None),
        P(None, BOTH),
        P(BOTH, None, None),
        P(BOTH, None, None),
        P(EXP, CTX, None),
        P(EXP, CTX, None),
        P(EXP, CTX),
        P(EXP, CTX, None),
    )
    nc, nz = mesh.shape[CTX], mesh.shape[EXP]
    split = nc == 8 and nz == 4
    return jax.shard_map(
        fast_body(nc, nz) if split else body,
        mesh=mesh,
        in_specs=placed,
        out_specs=(
            P(EXP, CTX, None),
            P(EXP, CTX, None),
            P(BOTH),
            P(BOTH, None),
            P(BOTH, None),
            P(BOTH),
            P(None, BOTH),
            P(None, BOTH),
            P(BOTH),
            P(BOTH, None),
            P(BOTH, None),
            P(None, BOTH),
            P(BOTH, None, None),
            P(BOTH, None, None),
        ),
        check_vma=False,
    )
```
